512 devices in a mesh: interval: 8 (over y), seq: 8 (over x, core), head: 8 (over z).
Axes of the slice: x: 4, y: 8, z: 8, core: 2. Of those that a mesh axis runs over, the one named last changes fastest.
Arguments:
- hidden_in: bfloat16 [8, 2048, 1536], P('interval', 'seq'), may hold values from -6 to 6
- ctx_grad: bfloat16 [8, 2048, 1536], P('interval', 'seq', 'head'), may hold values from -6 to 6
- w_query: bfloat16 [1536, 1536], P('head'), may hold values from -0.15625 to 0.15625
- w_key: bfloat16 [1536, 1536], P('head'), may hold values from -0.15625 to 0.15625
- w_value: bfloat16 [1536, 1536], P('head'), may hold values from -0.15625 to 0.15625
- w_junction: bfloat16 [1536, 128], replicated, may hold values from -0.15625 to 0.15625
- donor_pos: int32 [8, 8, 8, 64], P('interval', 'seq', None, 'head'), may hold values from 0 to 255
- acceptor_pos: int32 [8, 8, 8, 64], P('interval', 'seq', None, 'head'), may hold values from 0 to 255
- junction_counts: int32 [8, 8, 8], P('interval', 'seq'), may hold values from 16 to 64, as said below
- pred_grad: float32 [8, 8, 8, 64], P('interval', 'seq', None, 'head'), may hold values from -6 to 6
Outputs:
- grad_input: bfloat16 [8, 2048, 1536], P('interval', 'seq', 'head')
- grad_query: bfloat16 [1536, 1536], P('head')
- grad_key: bfloat16 [1536, 1536], P('head')
- grad_value: bfloat16 [1536, 1536], P('head')
The draws below stay inside these ranges and needn't reach their ends.
Inputs may be any that keep to these rules, and one draw needn't show every extreme that they name: `junction_counts`: slots at or past a bucket's count are empty. In each interval one acceptor shard, drawn from the seed, has 64 live slots from every donor shard; every other bucket has 16 to 32.
All inputs are finite; a program needn't handle non-finite values.
Results may differ from the reference program's by a relative error of at most 0.022.
Values may be sent and summed in bfloat16 or wider, within the bound.
No kernel may reach another device: no remote copies, remote signals or barrier semaphores. Data moves between devices by JAX's collectives and lax.ppermute only.
A program may use at most 64 MiB of HBM per device.

```python
import jax
import jax.numpy as jnp
from jax import lax

D = 1536
HEADS = 8
HD = 192
PJ = 128
TOK_DEV = 256
SLOT_HEAD = 8
SEQ = 2048
INTERVALS = 8
CAP = 64
N_SEQ = 8
N_HEAD = 8


def draw_junction_counts(key, part):
    key_hot, key_base = jax.random.split(key)
    hot_shard = jax.random.randint(key_hot, (INTERVALS, 1, 1), 0, N_SEQ)
    base = jax.random.randint(key_base, (INTERVALS, N_SEQ, N_SEQ), CAP // 4, CAP // 2 + 1)
    column = jnp.arange(N_SEQ, dtype=jnp.int32).reshape(1, 1, N_SEQ)
    return jnp.where(column == hot_shard, CAP, base).astype(jnp.int32)


def plant(drawn, stream_key, smallest, high):
    extent = drawn.shape
    spot = [jax.random.randint(jax.random.fold_in(stream_key, axis), (), 0, extent[axis]) for axis in range(len(extent))]
    drawn = drawn.at[tuple(spot)].set(smallest)
    longest = extent.index(max(extent))
    spot[longest] = (spot[longest] + 1) % extent[longest]
    return drawn.at[tuple(spot)].set(high)


def shard_levels(own_key, extent, cuts, least, high):
    loudness, own = 1.0, jax.random.fold_in(own_key, 6)
    for position, shards_of in cuts:
        draws = jnp.exp(jax.random.uniform(jax.random.fold_in(own, position), (shards_of,), jnp.float32, least / len(cuts), high / len(cuts)))
        loudness = loudness * jnp.repeat(draws, extent[position] // shards_of).reshape([-1 if axis == position else 1 for axis in range(len(extent))])
    return loudness


def normal_values(key, shape, scale, limit, cuts=(), kind=jnp.bfloat16):
    values = jax.random.normal(key, shape, jnp.float32) * scale
    if len(cuts) > 0:
        values = shard_levels(key, shape, cuts, -0.22, 0.18) * values
    return jnp.clip(values, min=-limit, max=limit).astype(kind)


def setup_inputs(seed: int = 0) -> dict:
    keys = jax.random.split(jax.random.key(seed), 11)
    return {
        "hidden_in": normal_values(keys[0], (INTERVALS, SEQ, D), 1.0, 6.0, ((0, 8), (1, 8))),
        "ctx_grad": normal_values(keys[1], (INTERVALS, SEQ, HEADS * HD), 1.0, 6.0, ((0, 8), (1, 8), (2, 8))),
        "w_query": normal_values(keys[2], (HEADS * HD, D), D ** -0.5, 0.15625, ((0, 8),)),
        "w_key": normal_values(keys[3], (HEADS * HD, D), D ** -0.5, 0.15625, ((0, 8),)),
        "w_value": normal_values(keys[4], (HEADS * HD, D), D ** -0.5, 0.15625, ((0, 8),)),
        "w_junction": normal_values(keys[5], (D, PJ), D ** -0.5, 0.15625),
        "donor_pos": plant(jax.random.randint(keys[6], (INTERVALS, N_SEQ, N_SEQ, CAP), 0, TOK_DEV), jax.random.fold_in(keys[6], 1), 0, TOK_DEV - 1).astype(jnp.int32),
        "acceptor_pos": plant(jax.random.randint(keys[7], (INTERVALS, N_SEQ, N_SEQ, CAP), 0, TOK_DEV), jax.random.fold_in(keys[7], 1), 0, TOK_DEV - 1).astype(jnp.int32),
        "junction_counts": draw_junction_counts(jax.random.fold_in(keys[10], 71), 0),
        "pred_grad": normal_values(keys[9], (INTERVALS, N_SEQ, N_SEQ, CAP), 1.0, 6.0, ((0, 8), (1, 8), (3, 8)), jnp.float32),
    }


def rounded(value):
    return lax.optimization_barrier(value.astype(jnp.bfloat16)).astype(jnp.float32)


def attention_grads(hidden, ctx, w_query, w_key, w_value):
    total_len = hidden.shape[0]
    softmax_scale = HD ** -0.5
    queries = jnp.dot(hidden, w_query.T, preferred_element_type=jnp.float32).astype(jnp.bfloat16)
    key_rows = jnp.dot(hidden, w_key.T, preferred_element_type=jnp.float32).astype(jnp.bfloat16)
    value_rows = jnp.dot(hidden, w_value.T, preferred_element_type=jnp.float32).astype(jnp.bfloat16)
    key_heads = key_rows.astype(jnp.float32).reshape(total_len, HEADS, HD)
    value_heads = value_rows.astype(jnp.float32).reshape(total_len, HEADS, HD)
    query_blocks = queries.reshape(N_SEQ, TOK_DEV, HEADS, HD)
    grad_blocks = ctx.reshape(N_SEQ, TOK_DEV, HEADS, HD)

    def step_block(totals, inputs):
        query_part = inputs[0].astype(jnp.float32)
        grad_part = inputs[1].astype(jnp.float32)
        scores = jnp.einsum("qhd,khd->hqk", query_part, key_heads) * softmax_scale
        row_max = jnp.max(scores, axis=-1, keepdims=True)
        expd = jnp.exp(scores - row_max)
        probs = expd / jnp.sum(expd, axis=-1, keepdims=True)
        dprobs = jnp.einsum("qhd,khd->hqk", grad_part, value_heads)
        row_delta = jnp.sum(probs * dprobs, axis=-1, keepdims=True)
        dscores = probs * (dprobs - row_delta)
        probs_b = rounded(probs)
        dscores_b = rounded(dscores)
        value_term = jnp.einsum("hqk,qhd->khd", probs_b, grad_part)
        key_term = jnp.einsum("hqk,qhd->khd", dscores_b, query_part) * softmax_scale
        query_grad = (jnp.einsum("hqk,khd->qhd", dscores_b, key_heads) * softmax_scale).astype(jnp.bfloat16)
        return (totals[0] + rounded(key_term), totals[1] + rounded(value_term)), query_grad

    empty = jnp.zeros((total_len, HEADS, HD), jnp.float32)
    sums, query_grads = lax.scan(step_block, (empty, empty), (query_blocks, grad_blocks))
    width = HEADS * HD
    query_grad = query_grads.reshape(total_len, width)
    key_grad = sums[0].reshape(total_len, width).astype(jnp.bfloat16)
    value_grad = sums[1].reshape(total_len, width).astype(jnp.bfloat16)
    return query_grad, key_grad, value_grad


def junction_grads(hidden, w_junction, donor_pos, acceptor_pos, counts, pred_grad):
    total_len = hidden.shape[0]
    pair_scale = PJ ** -0.5
    features = jnp.dot(hidden, w_junction, preferred_element_type=jnp.float32).astype(jnp.bfloat16)
    shard_rows = jnp.arange(N_SEQ, dtype=jnp.int32) * TOK_DEV
    donor_glob = shard_rows.reshape(N_SEQ, 1, 1) + donor_pos
    accept_glob = shard_rows.reshape(1, N_SEQ, 1) + acceptor_pos
    donor_feat = features[donor_glob].astype(jnp.float32)
    accept_feat = features[accept_glob].astype(jnp.float32)
    pair_score = jnp.sum(donor_feat * accept_feat, axis=-1) * pair_scale
    live_slots = jnp.arange(CAP, dtype=jnp.int32).reshape(1, 1, CAP) < counts[:, :, None]
    slot_grad = jnp.where(live_slots, pred_grad * jax.nn.sigmoid(pair_score), 0.0) * pair_scale
    donor_term = slot_grad[..., None] * accept_feat
    accept_term = slot_grad[..., None] * donor_feat
    result = jnp.zeros((total_len, hidden.shape[1]), jnp.float32)
    for group in range(N_HEAD):
        lower = group * SLOT_HEAD
        upper = lower + SLOT_HEAD
        grad_feat = jnp.zeros((total_len, PJ), jnp.float32)
        grad_feat = grad_feat.at[donor_glob[:, :, lower:upper].reshape(-1)].add(donor_term[:, :, lower:upper].reshape(-1, PJ))
        grad_feat = grad_feat.at[accept_glob[:, :, lower:upper].reshape(-1)].add(accept_term[:, :, lower:upper].reshape(-1, PJ))
        result = result + jnp.dot(grad_feat.astype(jnp.bfloat16), w_junction.T, preferred_element_type=jnp.float32)
    return result


def reference(hidden_in, ctx_grad, w_query, w_key, w_value, w_junction, donor_pos, acceptor_pos, junction_counts, pred_grad):
    input_grads = []
    sum_query = jnp.zeros(w_query.shape, jnp.float32)
    sum_key = jnp.zeros(w_query.shape, jnp.float32)
    sum_value = jnp.zeros(w_query.shape, jnp.float32)
    for interval_idx in range(INTERVALS):
        hidden = hidden_in[interval_idx]
        query_grad, key_grad, value_grad = attention_grads(hidden, ctx_grad[interval_idx], w_query, w_key, w_value)
        from_pairs = junction_grads(hidden, w_junction, donor_pos[interval_idx], acceptor_pos[interval_idx], junction_counts[interval_idx], pred_grad[interval_idx])
        total = jnp.dot(query_grad, w_query, preferred_element_type=jnp.float32)
        total = total + jnp.dot(key_grad, w_key, preferred_element_type=jnp.float32)
        total = total + jnp.dot(value_grad, w_value, preferred_element_type=jnp.float32)
        input_grads.append((total + from_pairs).astype(jnp.bfloat16))
        sum_query = sum_query + jnp.dot(query_grad.T, hidden, preferred_element_type=jnp.float32)
        sum_key = sum_key + jnp.dot(key_grad.T, hidden, preferred_element_type=jnp.float32)
        sum_value = sum_value + jnp.dot(value_grad.T, hidden, preferred_element_type=jnp.float32)
    return (jnp.stack(input_grads), sum_query.astype(jnp.bfloat16), sum_key.astype(jnp.bfloat16), sum_value.astype(jnp.bfloat16))
```

```python
import jax
import jax.numpy as jnp
from jax import lax
from jax.sharding import Mesh
from jax.sharding import PartitionSpec as P

HD = 192
PJ = 128
CORES = 2
F32 = jnp.float32
BF16 = jnp.bfloat16


def swap_cores(value):
    return lax.ppermute(value, "core", [(0, 1), (1, 0)])


def on_device(
    hidden_in,
    ctx_grad,
    w_query,
    w_key,
    w_value,
    w_junction,
    donor_pos,
    acceptor_pos,
    junction_counts,
    pred_grad,
):
    hidden = hidden_in[0]
    ctx = ctx_grad[0]
    tokens, width = hidden.shape
    chips = lax.axis_size("x")
    intervals = lax.axis_size("interval")
    core = lax.axis_index("core")
    half = chips * tokens
    softmax_scale = HD ** (-0.5)
    pair_scale = PJ ** (-0.5)

    def project(weight):
        return jnp.einsum("td,cd->tc", hidden, weight, preferred_element_type=F32).astype(BF16)

    queries, key_rows, value_rows = project(w_query), project(w_key), project(w_value)
    features = jnp.dot(hidden, w_junction, preferred_element_type=F32).astype(BF16)
    sent = jnp.concatenate([key_rows, value_rows, features], axis=1)
    copies = jnp.broadcast_to(sent[None], (chips,) + sent.shape).reshape(half, -1)
    mine = lax.all_to_all(copies, "x", 0, 0, tiled=True)
    theirs = swap_cores(mine)
    both = jnp.concatenate([mine, theirs], axis=0)
    keys, values, all_features = both[:, :HD], both[:, HD : 2 * HD], both[:, 2 * HD :]

    scores = jnp.einsum("qd,kd->qk", queries, keys, preferred_element_type=F32) * softmax_scale
    row_max = jnp.max(scores, axis=-1, keepdims=True)
    expd = jnp.exp(scores - row_max)
    probs = expd / jnp.sum(expd, axis=-1, keepdims=True)
    dprobs = jnp.einsum("qd,kd->qk", ctx, values, preferred_element_type=F32)
    row_delta = jnp.sum(probs * dprobs, axis=-1, keepdims=True)
    dscores_b = (probs * (dprobs - row_delta)).astype(BF16)
    probs_b = probs.astype(BF16)
    query_grad = (
        jnp.einsum("qk,kd->qd", dscores_b, keys, preferred_element_type=F32) * softmax_scale
    ).astype(BF16)
    key_term = (
        jnp.einsum("qk,qd->kd", dscores_b, queries, preferred_element_type=F32) * softmax_scale
    )
    value_term = jnp.einsum("qk,qd->kd", probs_b, ctx, preferred_element_type=F32)

    donor_idx = donor_pos[0, 0]
    buckets, slot_dev = donor_idx.shape
    slot_ids = lax.axis_index("head") * slot_dev + jnp.arange(slot_dev, dtype=jnp.int32)
    live_slots = slot_ids[None, :] < junction_counts[0, 0][:, None]
    shard = jnp.arange(buckets, dtype=jnp.int32)
    base = jnp.where(shard % CORES == core, 0, half) + (shard // CORES) * tokens
    accept_idx = base[:, None] + acceptor_pos[0, 0]
    donor_feat = features[donor_idx].astype(F32)
    accept_feat = all_features[accept_idx].astype(F32)
    pair_score = jnp.sum(donor_feat * accept_feat, axis=-1) * pair_scale
    slot_grad = (
        jnp.where(live_slots, pred_grad[0, 0] * jax.nn.sigmoid(pair_score), 0.0) * pair_scale
    )
    donor_term = slot_grad[..., None] * accept_feat
    accept_term = slot_grad[..., None] * donor_feat
    donor_sum = (
        jnp.zeros((tokens, PJ), F32).at[donor_idx.reshape(-1)].add(donor_term.reshape(-1, PJ))
    )
    spread = (
        jnp.zeros((CORES * half, PJ), F32)
        .at[accept_idx.reshape(-1)]
        .add(accept_term.reshape(-1, PJ))
    )

    terms = jnp.concatenate([key_term, value_term, spread], axis=1).astype(BF16)
    pair_sum = terms[:half].astype(F32) + swap_cores(terms[half:]).astype(F32)
    parts = lax.all_to_all(pair_sum.astype(BF16), "x", 0, 0, tiled=True)
    total = jnp.sum(parts.reshape(chips, tokens, -1).astype(F32), axis=0)
    key_grad = total[:, :HD].astype(BF16)
    value_grad = total[:, HD : 2 * HD].astype(BF16)
    feature_grad = (donor_sum + total[:, 2 * HD :]).astype(BF16)

    grads = jnp.concatenate([query_grad, key_grad, value_grad], axis=1)
    weights = jnp.concatenate([w_query, w_key, w_value], axis=0)
    input_term = jnp.dot(grads, weights, preferred_element_type=F32)
    input_term = input_term + jnp.einsum(
        "tp,dp->td", feature_grad, w_junction, preferred_element_type=F32
    )
    grad_input = lax.psum_scatter(
        input_term.astype(BF16), "head", scatter_dimension=1, tiled=True
    )

    rows = grads.shape[1]
    half_width = width // CORES
    weight_term = jnp.einsum("tc,td->cd", grads, hidden, preferred_element_type=F32).astype(BF16)

    def sum_parts(value, axis, count):
        got = lax.all_to_all(value, axis, 0, 0, tiled=True)
        return jnp.sum(got.reshape(count, -1, got.shape[-1]).astype(F32), axis=0).astype(BF16)

    term = weight_term.reshape(rows, CORES, half_width).transpose(1, 0, 2)
    term = sum_parts(term.reshape(CORES * rows, half_width), "core", CORES)
    term = sum_parts(term, "x", chips)
    part_rows = rows // chips
    cut = (2, part_rows // 2, intervals // 2, half_width // (intervals // 2))
    term = term.reshape(cut).transpose(0, 2, 1, 3).reshape(-1, cut[3])
    term = sum_parts(term, "interval", intervals)
    term = jnp.broadcast_to(term[None], (intervals,) + term.shape).reshape(-1, cut[3])
    term = lax.all_to_all(term, "interval", 0, 0, tiled=True)
    term = term.reshape(cut[0], cut[2], cut[1], cut[3]).transpose(0, 2, 1, 3)
    term = lax.all_gather(term.reshape(part_rows, half_width), "x", axis=0, tiled=True)
    other = swap_cores(term)
    left = jnp.where(core == 0, term, other)
    right = jnp.where(core == 0, other, term)
    whole = jnp.concatenate([left, right], axis=1)
    return grad_input[None], whole[:HD], whole[HD : 2 * HD], whole[2 * HD :]


def solution(mesh):
    axes = (mesh.shape["interval"], mesh.shape["seq"] // CORES, CORES, mesh.shape["head"])
    split = Mesh(mesh.devices.reshape(axes), ("interval", "x", "core", "head"))
    seq = ("x", "core")
    placed = (
        P("interval", seq, None),
        P("interval", seq, "head"),
        P("head", None),
        P("head", None),
        P("head", None),
        P(),
        P("interval", seq, None, "head"),
        P("interval", seq, None, "head"),
        P("interval", seq, None),
        P("interval", seq, None, "head"),
    )
    return jax.shard_map(
        on_device,
        mesh=split,
        in_specs=placed,
        out_specs=(P("interval", seq, "head"), P("head", None), P("head", None), P("head", None)),
        check_vma=False,
    )
```

```python
import jax
import jax.numpy as jnp
from jax import lax
from jax.experimental import pallas as pl
from jax.experimental.pallas import tpu as pltpu
from jax.sharding import Mesh
from jax.sharding import PartitionSpec as P

HD = 192
PJ = 128
CORES = 2
LANES = 256
LOW = PJ // 2
F32 = jnp.float32
BF16 = jnp.bfloat16
VMEM_BYTES = 48 * 1024 * 1024


def contract(a, b, dim_a, dim_b):
    return lax.dot_general(a, b, (((dim_a,), (dim_b,)), ((), ())), preferred_element_type=F32)


def local_call(body, outs, scratch=(), scalars=0, operands=0):
    specs = [pl.BlockSpec(memory_space=pltpu.SMEM)] * scalars
    specs += [pl.BlockSpec(memory_space=pltpu.VMEM)] * operands
    return pl.pallas_call(
        body,
        out_shape=tuple(jax.ShapeDtypeStruct(shape, kind) for shape, kind in outs),
        in_specs=specs,
        out_specs=tuple(pl.BlockSpec(memory_space=pltpu.VMEM) for _ in outs),
        scratch_shapes=list(scratch),
        compiler_params=pltpu.CompilerParams(vmem_limit_bytes=VMEM_BYTES),
    )


def project_body(hidden, w_key, w_value, w_junction, copies):
    x = hidden[...]
    feats = contract(x, w_junction[...], 1, 0).astype(BF16)
    row = jnp.concatenate(
        [
            contract(x, w_key[...], 1, 1).astype(BF16),
            feats[:, :LOW],
            contract(x, w_value[...], 1, 1).astype(BF16),
            feats[:, LOW:],
        ],
        axis=1,
    )
    for chip in range(copies.shape[0]):
        copies[chip] = row


def split_terms(term):
    high = term.astype(BF16)
    return high, (term - high.astype(F32)).astype(BF16)


def attend_body(
    place,
    hidden,
    w_query,
    ctx_grad,
    own,
    mine,
    theirs,
    donor_pos,
    acceptor_pos,
    counts,
    pred_grad,
    terms_mine,
    terms_theirs,
    query_grad,
    donor_sum,
    queries,
    ctx,
    probs_b,
    dscores_b,
):
    tokens = hidden.shape[0]
    half = mine.shape[0]
    scale = HD ** (-0.5)
    queries[...] = jnp.zeros_like(queries)
    ctx[...] = jnp.zeros_like(ctx)
    queries[:, :HD] = contract(hidden[...], w_query[...], 1, 1).astype(BF16)
    ctx[:, :HD] = ctx_grad[...]
    sides = (mine, theirs)
    rows = 64
    for start in range(0, tokens, rows):
        band = pl.ds(start, rows)
        q, g = queries[band, :], ctx[band, :]
        scores = [contract(q, side[:, :LANES], 1, 1) * scale for side in sides]
        row_max = jnp.maximum(
            jnp.max(scores[0], axis=-1, keepdims=True), jnp.max(scores[1], axis=-1, keepdims=True)
        )
        expd = [jnp.exp(score - row_max) for score in scores]
        inverse = 1.0 / (
            jnp.sum(expd[0], axis=-1, keepdims=True) + jnp.sum(expd[1], axis=-1, keepdims=True)
        )
        probs = [value * inverse for value in expd]
        dprobs = [contract(g, side[:, LANES:], 1, 1) for side in sides]
        row_delta = jnp.sum(probs[0] * dprobs[0], axis=-1, keepdims=True) + jnp.sum(
            probs[1] * dprobs[1], axis=-1, keepdims=True
        )
        for i in range(2):
            probs_b[i, band, :] = probs[i].astype(BF16)
            dscores_b[i, band, :] = (probs[i] * (dprobs[i] - row_delta)).astype(BF16)

    buckets, per = donor_pos.shape
    slots = buckets * per
    core, first = place[0], place[1] * per
    shard_of = lax.broadcasted_iota(jnp.int32, (1, slots), 1) // per
    spread_out = (
        lax.broadcasted_iota(jnp.int32, (per, slots), 1) % per
        == lax.broadcasted_iota(jnp.int32, (per, slots), 0)
    ).astype(F32)
    own_row = lax.broadcasted_iota(jnp.int32, (buckets, slots), 0) == (
        lax.broadcasted_iota(jnp.int32, (buckets, slots), 1) // per
    )

    def to_lanes(value):
        wide = lax.dot_general(
            value.astype(F32),
            spread_out,
            (((1,), (0,)), ((), ())),
            precision=lax.Precision.HIGHEST,
            preferred_element_type=F32,
        )
        return jnp.sum(jnp.where(own_row, wide, 0.0), axis=0, keepdims=True)

    donor_idx = to_lanes(donor_pos[...]).astype(jnp.int32)
    local_idx = to_lanes(acceptor_pos[...]).astype(jnp.int32)
    accept_idx = (
        jnp.where(shard_of % CORES == core, 0, half) + (shard_of // CORES) * tokens + local_idx
    )
    slot_row = first + lax.broadcasted_iota(jnp.int32, (buckets, per), 1)
    live_grad = to_lanes(jnp.where(slot_row < counts[...], pred_grad[...], 0.0))
    on_diagonal = lax.broadcasted_iota(jnp.int32, (slots, slots), 0) == (
        lax.broadcasted_iota(jnp.int32, (slots, slots), 1)
    )
    live_column = jnp.sum(jnp.where(on_diagonal, live_grad, 0.0), axis=1, keepdims=True)

    def pick(rows_at, count, offset):
        at = lax.broadcasted_iota(jnp.int32, (count, slots), 0) + offset
        return jnp.where(at == rows_at, 1.0, 0.0).astype(BF16)

    donor_hot = pick(donor_idx, tokens, 0)
    accept_hot = (pick(accept_idx, half, 0), pick(accept_idx, half, half))
    donor_feat = contract(donor_hot, own[...], 0, 0)
    accept_feat = contract(accept_hot[0], mine[...], 0, 0) + contract(
        accept_hot[1], theirs[...], 0, 0
    )
    lane = lax.broadcasted_iota(jnp.int32, (1, 2 * LANES), 1) % LANES
    donor_feat = jnp.where(lane >= HD, donor_feat, 0.0)
    accept_feat = jnp.where(lane >= HD, accept_feat, 0.0)
    pair_scale = PJ ** (-0.5)
    pair_score = jnp.sum(donor_feat * accept_feat, axis=-1, keepdims=True) * pair_scale
    slot_grad = live_column * jax.nn.sigmoid(pair_score) * pair_scale
    donor_terms = split_terms(slot_grad * accept_feat)
    accept_terms = split_terms(slot_grad * donor_feat)
    donor_sum[...] = contract(donor_hot, donor_terms[0], 1, 0) + contract(
        donor_hot, donor_terms[1], 1, 0
    )

    terms = (terms_mine, terms_theirs)
    for i in (1, 0):
        for part, (grad, rows_in) in enumerate(((dscores_b, queries), (probs_b, ctx))):
            lanes = pl.ds(part * LANES, LANES)
            total = contract(grad[i], rows_in[...], 0, 0)
            if part == 0:
                total = total * scale
            for piece in accept_terms:
                total = total + contract(
                    accept_hot[i], piece[:, part * LANES : (part + 1) * LANES], 1, 0
                )
            terms[i][:, lanes] = total.astype(terms[i].dtype)
    query_grad[...] = (
        (
            contract(dscores_b[0], mine[:, :LANES], 1, 0)
            + contract(dscores_b[1], theirs[:, :LANES], 1, 0)
        )[:, :HD]
        * scale
    ).astype(BF16)


def pair_body(mine, theirs, total):
    total[...] = (mine[...].astype(F32) + theirs[...].astype(F32)).astype(BF16)


def input_body(parts, donor_sum, query_grad, w_query, w_key, w_value, w_junction, grads, term):
    total = donor_sum[...]
    for chip in range(parts.shape[0]):
        total = total + parts[chip].astype(F32)
    total = total.astype(BF16)
    key_grad, value_grad = total[:, :HD], total[:, LANES : LANES + HD]
    feature_grad = jnp.concatenate([total[:, HD:LANES], total[:, LANES + HD :]], axis=1)
    grads[...] = total
    value = contract(w_query[...], query_grad[...], 0, 1)
    value = value + contract(w_key[...], key_grad, 0, 1)
    value = value + contract(w_value[...], value_grad, 0, 1)
    value = value + contract(w_junction[...], feature_grad, 1, 1)
    term[...] = value.astype(BF16)


def weight_body(hidden, query_grad, grads, term):
    cut = hidden.shape[1] // CORES
    for part, grad in enumerate(
        (query_grad[...], grads[:, :HD], grads[:, LANES : LANES + HD])
    ):
        value = contract(grad, hidden[...], 0, 0).astype(BF16)
        for core in range(CORES):
            term[core, part * HD : (part + 1) * HD, :] = value[:, core * cut : (core + 1) * cut]


def swap_cores(value):
    return lax.ppermute(value, "core", [(0, 1), (1, 0)])


def on_device(
    hidden_in,
    ctx_grad,
    w_query,
    w_key,
    w_value,
    w_junction,
    donor_pos,
    acceptor_pos,
    junction_counts,
    pred_grad,
):
    hidden = hidden_in[0]
    tokens, width = hidden.shape
    chips = lax.axis_size("x")
    intervals = lax.axis_size("interval")
    core = lax.axis_index("core")
    half = chips * tokens
    row = 2 * LANES

    (copies,) = local_call(project_body, [((chips, tokens, row), BF16)], operands=4)(
        hidden, w_key, w_value, w_junction
    )
    mine = lax.all_to_all(copies, "x", 0, 0, tiled=True).reshape(half, row)
    theirs = swap_cores(mine)
    place = jnp.stack([core, lax.axis_index("head")]).astype(jnp.int32)
    terms_mine, terms_theirs, query_grad, donor_sum = local_call(
        attend_body,
        [
            ((half, row), BF16),
            ((half, row), BF16),
            ((tokens, HD), BF16),
            ((tokens, row), F32),
        ],
        scratch=[pltpu.VMEM((tokens, LANES), BF16)] * 2
        + [pltpu.VMEM((CORES, tokens, half), BF16)] * 2,
        scalars=1,
        operands=10,
    )(
        place,
        hidden,
        w_query,
        ctx_grad[0],
        copies[0],
        mine,
        theirs,
        donor_pos[0, 0],
        acceptor_pos[0, 0],
        junction_counts[0, 0][:, None],
        pred_grad[0, 0],
    )
    (pair_sum,) = local_call(pair_body, [((half, row), BF16)], operands=2)(
        terms_mine, swap_cores(terms_theirs)
    )
    parts = lax.all_to_all(pair_sum.reshape(chips, tokens, row), "x", 0, 0, tiled=True)
    grads, input_term = local_call(
        input_body, [((tokens, row), BF16), ((width, tokens), BF16)], operands=7
    )(parts, donor_sum, query_grad, w_query, w_key, w_value, w_junction)
    grad_input = lax.psum_scatter(input_term, "head", scatter_dimension=0, tiled=True)

    rows = 3 * HD
    half_width = width // CORES
    (term,) = local_call(weight_body, [((CORES, rows, half_width), BF16)], operands=3)(
        hidden, query_grad, grads
    )

    def sum_parts(value, axis, count):
        got = lax.all_to_all(value, axis, 0, 0, tiled=True)
        return jnp.sum(got.reshape(count, -1, got.shape[-1]).astype(F32), axis=0).astype(BF16)

    term = sum_parts(term, "core", CORES)
    term = sum_parts(term, "x", chips)
    part_rows = rows // chips
    cut = (2, part_rows // 2, intervals // 2, half_width // (intervals // 2))
    term = term.reshape(cut).transpose(0, 2, 1, 3).reshape(-1, cut[3])
    term = sum_parts(term, "interval", intervals)
    term = jnp.broadcast_to(term[None], (intervals,) + term.shape).reshape(-1, cut[3])
    term = lax.all_to_all(term, "interval", 0, 0, tiled=True)
    term = term.reshape(cut[0], cut[2], cut[1], cut[3]).transpose(0, 2, 1, 3)
    term, grad_input = lax.optimization_barrier((term, grad_input))
    term = lax.all_gather(term.reshape(part_rows, half_width), "x", axis=0, tiled=True)
    other = swap_cores(term)
    left = jnp.where(core == 0, term, other)
    right = jnp.where(core == 0, other, term)
    whole = jnp.concatenate([left, right], axis=1)
    return grad_input.T[None], whole[:HD], whole[HD : 2 * HD], whole[2 * HD :]


def solution(mesh):
    axes = (mesh.shape["interval"], mesh.shape["seq"] // CORES, CORES, mesh.shape["head"])
    split = Mesh(mesh.devices.reshape(axes), ("interval", "x", "core", "head"))
    seq = ("x", "core")
    placed = (
        P("interval", seq, None),
        P("interval", seq, "head"),
        P("head", None),
        P("head", None),
        P("head", None),
        P(),
        P("interval", seq, None, "head"),
        P("interval", seq, None, "head"),
        P("interval", seq, None),
        P("interval", seq, None, "head"),
    )
    return jax.shard_map(
        on_device,
        mesh=split,
        in_specs=placed,
        out_specs=(P("interval", seq, "head"), P("head", None), P("head", None), P("head", None)),
        check_vma=False,
    )
```

```python
import jax
import jax.numpy as jnp
from jax import lax
from jax.experimental import pallas as pl
from jax.experimental.pallas import tpu as pltpu
from jax.sharding import Mesh
from jax.sharding import PartitionSpec as P

HD = 192
PJ = 128
CORES = 2
LANES = 256
KV = 2 * HD
SHIFT = KV - LANES
F32 = jnp.float32
BF16 = jnp.bfloat16
VMEM_BYTES = 48 * 1024 * 1024


def contract(a, b, dim_a, dim_b, precision=None):
    return lax.dot_general(
        a, b, (((dim_a,), (dim_b,)), ((), ())), precision=precision, preferred_element_type=F32
    )


def iota(shape, axis):
    return lax.broadcasted_iota(jnp.int32, shape, axis)


def local_call(body, outs, operands, scratch=(), fetched=0):
    specs = [pl.BlockSpec(memory_space=pltpu.HBM)] * fetched
    specs += [pl.BlockSpec(memory_space=pltpu.VMEM)] * (operands - fetched)
    return pl.pallas_call(
        body,
        out_shape=tuple(jax.ShapeDtypeStruct(shape, kind) for shape, kind in outs),
        in_specs=specs,
        out_specs=tuple(pl.BlockSpec(memory_space=pltpu.VMEM) for _ in outs),
        scratch_shapes=list(scratch),
        compiler_params=pltpu.CompilerParams(vmem_limit_bytes=VMEM_BYTES),
    )


def split_terms(term, count=2):
    pieces = []
    for _ in range(count):
        piece = term.astype(BF16)
        pieces.append(piece)
        term = term - piece.astype(F32)
    return pieces


def project_body(
    hidden_hbm,
    w_key_hbm,
    w_value_hbm,
    w_junction_hbm,
    donor_hbm,
    acceptor_hbm,
    counts_hbm,
    pred_hbm,
    message,
    features,
    donor_hot,
    hidden,
    weights,
    w_junction,
    donor_pos,
    acceptor_pos,
    counts,
    pred_grad,
    sems,
):
    targets = (
        hidden,
        weights.at[pl.ds(0, HD)],
        weights.at[pl.ds(HD, HD)],
        w_junction,
        donor_pos,
        acceptor_pos,
        counts,
        pred_grad,
    )
    sources = (
        hidden_hbm,
        w_key_hbm,
        w_value_hbm,
        w_junction_hbm,
        donor_hbm,
        acceptor_hbm,
        counts_hbm,
        pred_hbm,
    )
    copies = [
        pltpu.make_async_copy(source, target, sems.at[i])
        for i, (source, target) in enumerate(zip(sources, targets))
    ]
    for copy in copies:
        copy.start()
    for copy in copies:
        copy.wait()
    chips = message.shape[0]
    tokens = hidden.shape[0]
    x = hidden[...]
    feats = contract(x, w_junction[...], 1, 0).astype(BF16)
    features[...] = feats
    rows = contract(x, weights[...], 1, 1).astype(BF16)

    buckets, per = donor_pos.shape
    slots = buckets * per
    square = iota((buckets, buckets), 0) == iota((buckets, buckets), 1)
    limit = jnp.sum(
        jnp.where(square, counts[...].astype(F32), 0.0), axis=1, keepdims=True
    )
    slot_ids = lax.axis_index("head") * per + iota((buckets, per), 1)
    live_grad = jnp.where(slot_ids.astype(F32) < limit, pred_grad[...], 0.0)
    pick_bucket = (iota((slots, buckets), 0) // per == iota((slots, buckets), 1)).astype(F32)
    own_slot = iota((slots, per), 0) % per == iota((slots, per), 1)

    def to_column(value):
        wide = contract(pick_bucket, value.astype(F32), 1, 0, lax.Precision.HIGHEST)
        return jnp.sum(jnp.where(own_slot, wide, 0.0), axis=1, keepdims=True)

    donor = to_column(donor_pos[...])
    hot = jnp.where(iota((slots, tokens), 1).astype(F32) == donor, 1.0, 0.0).astype(BF16)
    donor_hot[...] = hot
    lane = iota((slots, PJ), 1)
    scalars = [to_column(acceptor_pos[...])]
    scalars += [piece.astype(F32) for piece in split_terms(to_column(live_grad), 3)]
    extra = jnp.zeros((slots, PJ), F32)
    for i, column in enumerate(scalars):
        extra = jnp.where(lane == i, column, extra)
    slot_rows = jnp.concatenate(
        [
            contract(hot, feats, 1, 0).astype(BF16),
            extra.astype(BF16),
            jnp.zeros((slots, KV - 2 * PJ), BF16),
        ],
        axis=1,
    )
    part = slots // chips
    for chip in range(chips):
        message[chip, :tokens, :] = rows
        message[chip, tokens:, :] = slot_rows[chip * part : (chip + 1) * part, :]


def query_body(hidden, w_query, ctx_t, queries, ctx):
    tokens = hidden.shape[0]
    pad = jnp.zeros((tokens, LANES - HD), BF16)
    value = contract(hidden[...], w_query[...], 1, 1).astype(BF16)
    queries[...] = jnp.concatenate([value, pad], axis=1)
    ctx[...] = jnp.concatenate([pad, jnp.transpose(ctx_t[...].astype(F32)).astype(BF16)], axis=1)


def attend_body(
    queries,
    ctx,
    features,
    mine,
    theirs,
    terms_mine,
    terms_theirs,
    query_grad,
    accept_sum,
    probs_b,
    dscores_b,
):
    tokens = queries.shape[0]
    chips, height, _ = mine.shape
    half = chips * tokens
    scale = HD ** (-0.5)
    sides = [ref[:, :tokens, :].reshape(half, KV) for ref in (mine, theirs)]
    rows = 64
    for start in range(0, tokens, rows):
        band = pl.ds(start, rows)
        q, g = queries[band, :], ctx[band, :]
        scores = [contract(q, side[:, :LANES], 1, 1) * scale for side in sides]
        row_max = jnp.maximum(
            jnp.max(scores[0], axis=-1, keepdims=True), jnp.max(scores[1], axis=-1, keepdims=True)
        )
        expd = [jnp.exp(score - row_max) for score in scores]
        inverse = 1.0 / (
            jnp.sum(expd[0], axis=-1, keepdims=True) + jnp.sum(expd[1], axis=-1, keepdims=True)
        )
        probs = [value * inverse for value in expd]
        dprobs = [contract(g, side[:, SHIFT:], 1, 1) for side in sides]
        row_delta = jnp.sum(probs[0] * dprobs[0], axis=-1, keepdims=True) + jnp.sum(
            probs[1] * dprobs[1], axis=-1, keepdims=True
        )
        for i in range(2):
            probs_b[i, band, :] = probs[i].astype(BF16)
            dscores_b[i, band, :] = (probs[i] * (dprobs[i] - row_delta)).astype(BF16)

    core = lax.axis_index("core")
    part = height - tokens
    per = part // CORES

    def own_rows(ref):
        block = ref[:, tokens:, :].astype(F32)
        return jnp.where(core == 0, block[:, :per, :], block[:, per:, :]).reshape(chips * per, KV)

    slot_rows = jnp.concatenate([own_rows(mine), own_rows(theirs)], axis=0)
    slots = slot_rows.shape[0]
    donor_feat = slot_rows[:, :PJ]
    extra = slot_rows[:, PJ : 2 * PJ]
    acceptor = extra[:, 0:1]
    slot_scale = extra[:, 1:2] + extra[:, 2:3] + extra[:, 3:4]
    hot = jnp.where(iota((slots, tokens), 1).astype(F32) == acceptor, 1.0, 0.0).astype(BF16)
    accept_feat = contract(hot, features[...], 1, 0)
    pair_scale = PJ ** (-0.5)
    pair_score = jnp.sum(donor_feat * accept_feat, axis=-1, keepdims=True) * pair_scale
    slot_grad = slot_scale * jax.nn.sigmoid(pair_score) * pair_scale
    total = jnp.zeros((tokens, PJ), F32)
    for piece in split_terms(slot_grad * donor_feat):
        total = total + contract(hot, piece, 0, 0)
    accept_sum[...] = total
    back = (slot_grad * accept_feat).reshape(2, chips, per, PJ)
    blank = jnp.zeros((chips, per, PJ), F32)

    for i, terms in ((1, terms_theirs), (0, terms_mine)):
        key_term = contract(dscores_b[i], queries[...], 0, 0) * scale
        value_term = contract(probs_b[i], ctx[...], 0, 0)
        middle = key_term[:, SHIFT:] + value_term[:, :SHIFT]
        for first, value in (
            (0, key_term[:, :SHIFT]),
            (SHIFT, middle),
            (LANES, value_term[:, SHIFT:]),
        ):
            terms[:, :tokens, first : first + SHIFT] = value.astype(BF16).reshape(
                chips, tokens, SHIFT
            )
        upper = jnp.where(core == 0, back[i], blank)
        lower = jnp.where(core == 0, blank, back[i])
        terms[:, tokens:, :PJ] = jnp.concatenate([upper, lower], axis=1).astype(BF16)
        terms[:, tokens:, PJ:] = jnp.zeros((chips, part, KV - PJ), BF16)
    query_grad[...] = (
        (
            contract(dscores_b[0], sides[0][:, :LANES], 1, 0)
            + contract(dscores_b[1], sides[1][:, :LANES], 1, 0)
        )[:, :HD]
        * scale
    ).astype(BF16)


def pair_body(mine, theirs, total):
    total[...] = (mine[...].astype(F32) + theirs[...].astype(F32)).astype(BF16)


def grads_body(
    parts,
    accept_sum,
    donor_hot,
    query_grad,
    hidden,
    w_query,
    w_key,
    w_value,
    w_junction,
    weight_term,
    input_term,
):
    tokens, width = hidden.shape
    chips = parts.shape[0]
    total = jnp.zeros((tokens, KV), F32)
    for chip in range(chips):
        total = total + parts[chip, :tokens, :].astype(F32)
    grads = total.astype(BF16)
    part = parts.shape[1] - tokens
    slot_rows = parts[:, tokens:, :PJ].reshape(chips * part, PJ)
    feature_grad = (accept_sum[...] + contract(donor_hot[...], slot_rows, 0, 0)).astype(BF16)
    value = contract(w_query[...], query_grad[...], 0, 1)
    value = value + contract(w_key[...], grads[:, :HD], 0, 1)
    value = value + contract(w_value[...], grads[:, HD:], 0, 1)
    value = value + contract(w_junction[...], feature_grad, 1, 1)
    input_term[...] = value.astype(BF16).reshape(input_term.shape)
    cut = width // CORES
    first = 0
    for grad in (query_grad[...], grads):
        value = contract(grad, hidden[...], 0, 0).astype(BF16)
        for core in range(CORES):
            weight_term[core, first : first + value.shape[0], :] = value[
                :, core * cut : (core + 1) * cut
            ]
        first += value.shape[0]


def tiles_of(rows, columns, count):
    high, wide = rows * 2 // count, columns // 2
    return [(i, pl.ds(i // 2 * high, high), pl.ds(i % 2 * wide, wide)) for i in range(count)]


def sum_body(parts, total):
    value = parts[0].astype(F32)
    for i in range(1, parts.shape[0]):
        value = value + parts[i].astype(F32)
    total[...] = value.astype(total.dtype)


def cut_body(parts, tiles, whole):
    value = parts[0].astype(F32)
    for i in range(1, parts.shape[0]):
        value = value + parts[i].astype(F32)
    whole[...] = value
    for i, rows, columns in tiles_of(*whole.shape, tiles.shape[0]):
        tiles[i] = whole[rows, columns].astype(BF16)


def spread_body(parts, copies):
    value = parts[0].astype(F32)
    for i in range(1, parts.shape[0]):
        value = value + parts[i].astype(F32)
    value = value.astype(BF16)
    for i in range(copies.shape[0]):
        copies[i] = value


def join_body(tiles, joined, whole):
    for i, rows, columns in tiles_of(*whole.shape, tiles.shape[0]):
        whole[rows, columns] = tiles[i].astype(F32)
    joined[...] = whole[...].astype(BF16)


def place_body(mine, theirs, *outs):
    core = lax.axis_index("core")
    cut = mine.shape[1]
    for i, out in enumerate(outs):
        a, b = mine[i * HD : (i + 1) * HD, :], theirs[i * HD : (i + 1) * HD, :]
        out[:, :cut] = jnp.where(core == 0, a, b)
        out[:, cut:] = jnp.where(core == 0, b, a)


def swap_cores(value):
    return lax.ppermute(value, "core", [(0, 1), (1, 0)])


def exchange(value, axis):
    return lax.all_to_all(value, axis, 0, 0, tiled=True)


def on_device(
    hidden_in,
    ctx_grad,
    w_query,
    w_key,
    w_value,
    w_junction,
    donor_pos,
    acceptor_pos,
    junction_counts,
    pred_grad,
):
    hidden = hidden_in[0]
    tokens, width = hidden.shape
    chips = lax.axis_size("x")
    intervals = lax.axis_size("interval")
    heads = lax.axis_size("head")
    half = chips * tokens
    buckets, per = donor_pos.shape[2:]
    slots = buckets * per
    height = tokens + slots // chips

    message, features, donor_hot = local_call(
        project_body,
        [((chips, height, KV), BF16), ((tokens, PJ), BF16), ((slots, tokens), BF16)],
        operands=8,
        fetched=8,
        scratch=[
            pltpu.VMEM((tokens, width), BF16),
            pltpu.VMEM((KV, width), BF16),
            pltpu.VMEM((width, PJ), BF16),
            pltpu.VMEM((buckets, per), jnp.int32),
            pltpu.VMEM((buckets, per), jnp.int32),
            pltpu.VMEM((1, buckets), jnp.int32),
            pltpu.VMEM((buckets, per), F32),
            pltpu.SemaphoreType.DMA((8,)),
        ],
    )(
        hidden,
        w_key,
        w_value,
        w_junction,
        donor_pos[0, 0],
        acceptor_pos[0, 0],
        junction_counts[0],
        pred_grad[0, 0],
    )
    mine = exchange(message, "x")
    theirs = swap_cores(mine)
    queries, ctx = local_call(query_body, [((tokens, LANES), BF16)] * 2, operands=3)(
        hidden, w_query, ctx_grad[0].T
    )
    terms_mine, terms_theirs, query_grad, accept_sum = local_call(
        attend_body,
        [
            ((chips, height, KV), BF16),
            ((chips, height, KV), BF16),
            ((tokens, HD), BF16),
            ((tokens, PJ), F32),
        ],
        operands=5,
        scratch=[pltpu.VMEM((CORES, tokens, half), BF16)] * 2,
    )(queries, ctx, features, mine, theirs)
    (pair_sum,) = local_call(pair_body, [((chips, height, KV), BF16)], operands=2)(
        terms_mine, swap_cores(terms_theirs)
    )
    parts = exchange(pair_sum, "x")
    rows = 3 * HD
    cut = width // CORES
    weight_term, input_term = local_call(
        grads_body,
        [((CORES, rows, cut), BF16), ((heads, width // heads, tokens), BF16)],
        operands=9,
    )(
        parts,
        accept_sum,
        donor_hot,
        query_grad,
        hidden,
        w_query,
        w_key,
        w_value,
        w_junction,
    )
    input_parts = exchange(input_term, "head")

    (term,) = local_call(sum_body, [((rows, cut), BF16)], operands=1)(
        exchange(weight_term, "core")
    )
    part = rows // chips
    tile = (part * 2 // intervals, cut // 2)
    (tiles,) = local_call(
        cut_body, [((intervals,) + tile, BF16)], operands=1, scratch=[pltpu.VMEM((part, cut), F32)]
    )(exchange(term.reshape(chips, part, cut), "x"))
    (copies,) = local_call(spread_body, [((intervals,) + tile, BF16)], operands=1)(
        exchange(tiles, "interval")
    )
    (term,) = local_call(
        join_body, [((part, cut), BF16)], operands=1, scratch=[pltpu.VMEM((part, cut), F32)]
    )(exchange(copies, "interval"))
    term, input_parts = lax.optimization_barrier((term, input_parts))
    term = lax.all_gather(term, "x", axis=0, tiled=True)
    (grad_input,) = local_call(sum_body, [((width // heads, tokens), BF16)], operands=1)(
        input_parts
    )
    grads = local_call(place_body, [((HD, width), BF16)] * 3, operands=2)(term, swap_cores(term))
    return (grad_input.T[None],) + tuple(grads)


def solution(mesh):
    axes = (mesh.shape["interval"], mesh.shape["seq"] // CORES, CORES, mesh.shape["head"])
    split = Mesh(mesh.devices.reshape(axes), ("interval", "x", "core", "head"))
    seq = ("x", "core")
    placed = (
        P("interval", seq, None),
        P("interval", seq, "head"),
        P("head", None),
        P("head", None),
        P("head", None),
        P(),
        P("interval", seq, None, "head"),
        P("interval", seq, None, "head"),
        P("interval", seq, None),
        P("interval", seq, None, "head"),
    )
    return jax.shard_map(
        on_device,
        mesh=split,
        in_specs=placed,
        out_specs=(P("interval", seq, "head"), P("head", None), P("head", None), P("head", None)),
        check_vma=False,
    )
```

```python
import functools

import jax
import jax.numpy as jnp
from jax import lax
from jax.experimental import pallas as pl
from jax.experimental.pallas import tpu as pltpu
from jax.sharding import Mesh
from jax.sharding import PartitionSpec as P

HD = 192
PJ = 128
CORES = 2
LANES = 256
KV = 2 * HD
SHIFT = KV - LANES
F32 = jnp.float32
BF16 = jnp.bfloat16
VMEM_BYTES = 48 * 1024 * 1024


def contract(a, b, dim_a, dim_b, precision=None):
    return lax.dot_general(
        a, b, (((dim_a,), (dim_b,)), ((), ())), precision=precision, preferred_element_type=F32
    )


def iota(shape, axis):
    return lax.broadcasted_iota(jnp.int32, shape, axis)


def local_call(body, outs, operands, scratch=(), fetched=0):
    specs = [pl.BlockSpec(memory_space=pltpu.HBM)] * fetched
    specs += [pl.BlockSpec(memory_space=pltpu.VMEM)] * (operands - fetched)
    return pl.pallas_call(
        body,
        out_shape=tuple(jax.ShapeDtypeStruct(shape, kind) for shape, kind in outs),
        in_specs=specs,
        out_specs=tuple(pl.BlockSpec(memory_space=pltpu.VMEM) for _ in outs),
        scratch_shapes=list(scratch),
        compiler_params=pltpu.CompilerParams(vmem_limit_bytes=VMEM_BYTES),
    )


def split_terms(term, count=2):
    pieces = []
    for _ in range(count):
        piece = term.astype(BF16)
        pieces.append(piece)
        term = term - piece.astype(F32)
    return pieces


def project_body(
    hidden_hbm,
    w_key_hbm,
    w_value_hbm,
    w_junction_hbm,
    donor_hbm,
    acceptor_hbm,
    counts_hbm,
    pred_hbm,
    message,
    features,
    donor_hot,
    hidden,
    weights,
    w_junction,
    donor_pos,
    acceptor_pos,
    counts,
    pred_grad,
    sems,
):
    targets = (
        hidden,
        weights.at[pl.ds(0, HD)],
        weights.at[pl.ds(HD, HD)],
        w_junction,
        donor_pos,
        acceptor_pos,
        counts,
        pred_grad,
    )
    sources = (
        hidden_hbm,
        w_key_hbm,
        w_value_hbm,
        w_junction_hbm,
        donor_hbm,
        acceptor_hbm,
        counts_hbm,
        pred_hbm,
    )
    copies = [
        pltpu.make_async_copy(source, target, sems.at[i])
        for i, (source, target) in enumerate(zip(sources, targets))
    ]
    for copy in copies:
        copy.start()
    for copy in copies:
        copy.wait()
    chips = message.shape[0]
    tokens = hidden.shape[0]
    x = hidden[...]
    feats = contract(x, w_junction[...], 1, 0).astype(BF16)
    features[...] = feats
    rows = contract(x, weights[...], 1, 1).astype(BF16)

    buckets, per = donor_pos.shape
    slots = buckets * per
    square = iota((buckets, buckets), 0) == iota((buckets, buckets), 1)
    limit = jnp.sum(
        jnp.where(square, counts[...].astype(F32), 0.0), axis=1, keepdims=True
    )
    slot_ids = lax.axis_index("head") * per + iota((buckets, per), 1)
    live_grad = jnp.where(slot_ids.astype(F32) < limit, pred_grad[...], 0.0)
    pick_bucket = (iota((slots, buckets), 0) // per == iota((slots, buckets), 1)).astype(F32)
    own_slot = iota((slots, per), 0) % per == iota((slots, per), 1)

    def to_column(value):
        wide = contract(pick_bucket, value.astype(F32), 1, 0, lax.Precision.HIGHEST)
        return jnp.sum(jnp.where(own_slot, wide, 0.0), axis=1, keepdims=True)

    donor = to_column(donor_pos[...])
    hot = jnp.where(iota((slots, tokens), 1).astype(F32) == donor, 1.0, 0.0).astype(BF16)
    donor_hot[...] = hot
    lane = iota((slots, PJ), 1)
    scalars = [to_column(acceptor_pos[...])]
    scalars += [piece.astype(F32) for piece in split_terms(to_column(live_grad), 3)]
    extra = jnp.zeros((slots, PJ), F32)
    for i, column in enumerate(scalars):
        extra = jnp.where(lane == i, column, extra)
    slot_rows = jnp.concatenate(
        [
            contract(hot, feats, 1, 0).astype(BF16),
            extra.astype(BF16),
            jnp.zeros((slots, KV - 2 * PJ), BF16),
        ],
        axis=1,
    )
    part = slots // chips
    for chip in range(chips):
        message[chip, :tokens, :] = rows
        message[chip, tokens:, :] = slot_rows[chip * part : (chip + 1) * part, :]


def query_body(hidden, w_query, ctx_t, queries, ctx):
    tokens = hidden.shape[0]
    pad = jnp.zeros((tokens, LANES - HD), BF16)
    value = contract(hidden[...], w_query[...], 1, 1).astype(BF16)
    queries[...] = jnp.concatenate([value, pad], axis=1)
    ctx[...] = jnp.concatenate([pad, jnp.transpose(ctx_t[...].astype(F32)).astype(BF16)], axis=1)


def attend_body(
    queries,
    ctx,
    features,
    mine,
    theirs,
    terms_mine,
    terms_theirs,
    query_grad,
    accept_sum,
    probs_b,
    dscores_b,
):
    tokens = queries.shape[0]
    chips, height, _ = mine.shape
    half = chips * tokens
    scale = HD ** (-0.5)
    sides = [ref[:, :tokens, :].reshape(half, KV) for ref in (mine, theirs)]
    rows = 64
    for start in range(0, tokens, rows):
        band = pl.ds(start, rows)
        q, g = queries[band, :], ctx[band, :]
        scores = [contract(q, side[:, :LANES], 1, 1) * scale for side in sides]
        row_max = jnp.maximum(
            jnp.max(scores[0], axis=-1, keepdims=True), jnp.max(scores[1], axis=-1, keepdims=True)
        )
        expd = [jnp.exp(score - row_max) for score in scores]
        inverse = 1.0 / (
            jnp.sum(expd[0], axis=-1, keepdims=True) + jnp.sum(expd[1], axis=-1, keepdims=True)
        )
        probs = [value * inverse for value in expd]
        dprobs = [contract(g, side[:, SHIFT:], 1, 1) for side in sides]
        row_delta = jnp.sum(probs[0] * dprobs[0], axis=-1, keepdims=True) + jnp.sum(
            probs[1] * dprobs[1], axis=-1, keepdims=True
        )
        for i in range(2):
            probs_b[i, band, :] = probs[i].astype(BF16)
            dscores_b[i, band, :] = (probs[i] * (dprobs[i] - row_delta)).astype(BF16)

    core = lax.axis_index("core")
    part = height - tokens
    per = part // CORES

    def own_rows(ref):
        block = ref[:, tokens:, :].astype(F32)
        return jnp.where(core == 0, block[:, :per, :], block[:, per:, :]).reshape(chips * per, KV)

    slot_rows = jnp.concatenate([own_rows(mine), own_rows(theirs)], axis=0)
    slots = slot_rows.shape[0]
    donor_feat = slot_rows[:, :PJ]
    extra = slot_rows[:, PJ : 2 * PJ]
    acceptor = extra[:, 0:1]
    slot_scale = extra[:, 1:2] + extra[:, 2:3] + extra[:, 3:4]
    hot = jnp.where(iota((slots, tokens), 1).astype(F32) == acceptor, 1.0, 0.0).astype(BF16)
    accept_feat = contract(hot, features[...], 1, 0)
    pair_scale = PJ ** (-0.5)
    pair_score = jnp.sum(donor_feat * accept_feat, axis=-1, keepdims=True) * pair_scale
    slot_grad = slot_scale * jax.nn.sigmoid(pair_score) * pair_scale
    total = jnp.zeros((tokens, PJ), F32)
    for piece in split_terms(slot_grad * donor_feat):
        total = total + contract(hot, piece, 0, 0)
    accept_sum[...] = total
    back = (slot_grad * accept_feat).reshape(2, chips, per, PJ)
    blank = jnp.zeros((chips, per, PJ), F32)

    for i, terms in ((1, terms_theirs), (0, terms_mine)):
        key_term = contract(dscores_b[i], queries[...], 0, 0) * scale
        value_term = contract(probs_b[i], ctx[...], 0, 0)
        middle = key_term[:, SHIFT:] + value_term[:, :SHIFT]
        for first, value in (
            (0, key_term[:, :SHIFT]),
            (SHIFT, middle),
            (LANES, value_term[:, SHIFT:]),
        ):
            terms[:, :tokens, first : first + SHIFT] = value.astype(BF16).reshape(
                chips, tokens, SHIFT
            )
        upper = jnp.where(core == 0, back[i], blank)
        lower = jnp.where(core == 0, blank, back[i])
        terms[:, tokens:, :PJ] = jnp.concatenate([upper, lower], axis=1).astype(BF16)
        terms[:, tokens:, PJ:] = jnp.zeros((chips, part, KV - PJ), BF16)
    query_grad[...] = (
        (
            contract(dscores_b[0], sides[0][:, :LANES], 1, 0)
            + contract(dscores_b[1], sides[1][:, :LANES], 1, 0)
        )[:, :HD]
        * scale
    ).astype(BF16)


def pair_body(mine, theirs, total):
    total[...] = (mine[...].astype(F32) + theirs[...].astype(F32)).astype(BF16)


def halve(value, kept, sent, index):
    count = kept.shape[0]
    blocks = value.reshape((count, 2) + kept.shape[1:])
    odd = lax.rem(index, 2) == 1
    kept[...] = jnp.where(odd, blocks[:, 1], blocks[:, 0])
    sent[...] = jnp.where(odd, blocks[:, 0], blocks[:, 1]).astype(sent.dtype)


def halve_body(level, held, got, kept, sent):
    halve(held[...] + got[...].astype(F32), kept, sent, lax.axis_index("head") // 2**level)


def last_body(held, got, total):
    total[...] = (held[0] + got[0].astype(F32)).astype(total.dtype)


def grads_body(
    parts,
    accept_sum,
    donor_hot,
    query_grad,
    hidden,
    w_query,
    w_key,
    w_value,
    w_junction,
    weight_term,
    kept,
    sent,
):
    tokens, width = hidden.shape
    chips = parts.shape[0]
    total = jnp.zeros((tokens, KV), F32)
    for chip in range(chips):
        total = total + parts[chip, :tokens, :].astype(F32)
    grads = total.astype(BF16)
    part = parts.shape[1] - tokens
    slot_rows = parts[:, tokens:, :PJ].reshape(chips * part, PJ)
    feature_grad = (accept_sum[...] + contract(donor_hot[...], slot_rows, 0, 0)).astype(BF16)
    value = contract(w_query[...], query_grad[...], 0, 1)
    value = value + contract(w_key[...], grads[:, :HD], 0, 1)
    value = value + contract(w_value[...], grads[:, HD:], 0, 1)
    value = value + contract(w_junction[...], feature_grad, 1, 1)
    halve(value, kept, sent, lax.axis_index("head"))
    cut = width // CORES
    first = 0
    for grad in (query_grad[...], grads):
        value = contract(grad, hidden[...], 0, 0).astype(BF16)
        for core in range(CORES):
            weight_term[core, first : first + value.shape[0], :] = value[
                :, core * cut : (core + 1) * cut
            ]
        first += value.shape[0]


def tiles_of(rows, columns, count):
    high, wide = rows * 2 // count, columns // 2
    return [(i, pl.ds(i // 2 * high, high), pl.ds(i % 2 * wide, wide)) for i in range(count)]


def sum_body(parts, total):
    value = parts[0].astype(F32)
    for i in range(1, parts.shape[0]):
        value = value + parts[i].astype(F32)
    total[...] = value.astype(total.dtype)


def cut_body(parts, tiles, whole):
    value = parts[0].astype(F32)
    for i in range(1, parts.shape[0]):
        value = value + parts[i].astype(F32)
    whole[...] = value
    for i, rows, columns in tiles_of(*whole.shape, tiles.shape[0]):
        tiles[i] = whole[rows, columns].astype(BF16)


def spread_body(parts, copies):
    value = parts[0].astype(F32)
    for i in range(1, parts.shape[0]):
        value = value + parts[i].astype(F32)
    value = value.astype(BF16)
    for i in range(copies.shape[0]):
        copies[i] = value


def join_body(tiles, joined, whole):
    for i, rows, columns in tiles_of(*whole.shape, tiles.shape[0]):
        whole[rows, columns] = tiles[i].astype(F32)
    joined[...] = whole[...].astype(BF16)


def place_body(mine, theirs, *outs):
    core = lax.axis_index("core")
    cut = mine.shape[1]
    for i, out in enumerate(outs):
        a, b = mine[i * HD : (i + 1) * HD, :], theirs[i * HD : (i + 1) * HD, :]
        out[:, :cut] = jnp.where(core == 0, a, b)
        out[:, cut:] = jnp.where(core == 0, b, a)


def swap_cores(value):
    return lax.ppermute(value, "core", [(0, 1), (1, 0)])


def exchange(value, axis):
    return lax.all_to_all(value, axis, 0, 0, tiled=True)


def on_device(
    hidden_in,
    ctx_grad,
    w_query,
    w_key,
    w_value,
    w_junction,
    donor_pos,
    acceptor_pos,
    junction_counts,
    pred_grad,
):
    hidden = hidden_in[0]
    tokens, width = hidden.shape
    chips = lax.axis_size("x")
    intervals = lax.axis_size("interval")
    heads = lax.axis_size("head")
    half = chips * tokens
    buckets, per = donor_pos.shape[2:]
    slots = buckets * per
    height = tokens + slots // chips

    message, features, donor_hot = local_call(
        project_body,
        [((chips, height, KV), BF16), ((tokens, PJ), BF16), ((slots, tokens), BF16)],
        operands=8,
        fetched=8,
        scratch=[
            pltpu.VMEM((tokens, width), BF16),
            pltpu.VMEM((KV, width), BF16),
            pltpu.VMEM((width, PJ), BF16),
            pltpu.VMEM((buckets, per), jnp.int32),
            pltpu.VMEM((buckets, per), jnp.int32),
            pltpu.VMEM((1, buckets), jnp.int32),
            pltpu.VMEM((buckets, per), F32),
            pltpu.SemaphoreType.DMA((8,)),
        ],
    )(
        *(
            pltpu.with_memory_space_constraint(value, pltpu.HBM)
            for value in (
                hidden,
                w_key,
                w_value,
                w_junction,
                donor_pos[0, 0],
                acceptor_pos[0, 0],
                junction_counts[0],
                pred_grad[0, 0],
            )
        )
    )
    mine = exchange(message, "x")
    theirs = swap_cores(mine)
    queries, ctx = local_call(query_body, [((tokens, LANES), BF16)] * 2, operands=3)(
        hidden, w_query, ctx_grad[0].T
    )
    terms_mine, terms_theirs, query_grad, accept_sum = local_call(
        attend_body,
        [
            ((chips, height, KV), BF16),
            ((chips, height, KV), BF16),
            ((tokens, HD), BF16),
            ((tokens, PJ), F32),
        ],
        operands=5,
        scratch=[pltpu.VMEM((CORES, tokens, half), BF16)] * 2,
    )(queries, ctx, features, mine, theirs)
    (pair_sum,) = local_call(pair_body, [((chips, height, KV), BF16)], operands=2)(
        terms_mine, swap_cores(terms_theirs)
    )
    parts = exchange(pair_sum, "x")
    rows = 3 * HD
    cut = width // CORES
    block = (width // heads, tokens)
    weight_term, held, sent = local_call(
        grads_body,
        [
            ((CORES, rows, cut), BF16),
            ((heads // 2,) + block, F32),
            ((heads // 2,) + block, BF16),
        ],
        operands=9,
    )(
        parts,
        accept_sum,
        donor_hot,
        query_grad,
        hidden,
        w_query,
        w_key,
        w_value,
        w_junction,
    )

    def flip(value, level):
        return lax.ppermute(value, "head", [(i, i ^ 2**level) for i in range(heads)])

    def fold(level, held, got):
        count = heads // 2 ** (level + 1)
        return local_call(
            functools.partial(halve_body, level),
            [((count,) + block, F32), ((count,) + block, BF16)],
            operands=2,
        )(held, got)

    (term,) = local_call(sum_body, [((rows, cut), BF16)], operands=1)(
        exchange(weight_term, "core")
    )
    part = rows // chips
    tile = (part * 2 // intervals, cut // 2)
    (tiles,) = local_call(
        cut_body, [((intervals,) + tile, BF16)], operands=1, scratch=[pltpu.VMEM((part, cut), F32)]
    )(exchange(term.reshape(chips, part, cut), "x"))
    tiles, got = lax.optimization_barrier((tiles, flip(sent, 0)))
    held, sent = fold(1, held, got)
    (copies,) = local_call(spread_body, [((intervals,) + tile, BF16)], operands=1)(
        exchange(tiles, "interval")
    )
    copies, got = lax.optimization_barrier((copies, flip(sent, 1)))
    held, sent = fold(2, held, got)
    (term,) = local_call(
        join_body, [((part, cut), BF16)], operands=1, scratch=[pltpu.VMEM((part, cut), F32)]
    )(exchange(copies, "interval"))
    term, got = lax.optimization_barrier((term, flip(sent, 2)))
    term = lax.all_gather(term, "x", axis=0, tiled=True)
    (grad_input,) = local_call(last_body, [(block, BF16)], operands=2)(held, got)
    grads = local_call(place_body, [((HD, width), BF16)] * 3, operands=2)(term, swap_cores(term))
    return (grad_input.T[None],) + tuple(grads)


def solution(mesh):
    axes = (mesh.shape["interval"], mesh.shape["seq"] // CORES, CORES, mesh.shape["head"])
    split = Mesh(mesh.devices.reshape(axes), ("interval", "x", "core", "head"))
    seq = ("x", "core")
    placed = (
        P("interval", seq, None),
        P("interval", seq, "head"),
        P("head", None),
        P("head", None),
        P("head", None),
        P(),
        P("interval", seq, None, "head"),
        P("interval", seq, None, "head"),
        P("interval", seq, None),
        P("interval", seq, None, "head"),
    )
    return jax.shard_map(
        on_device,
        mesh=split,
        in_specs=placed,
        out_specs=(P("interval", seq, "head"), P("head", None), P("head", None), P("head", None)),
        check_vma=False,
    )
```

```python
import functools

import jax
import jax.numpy as jnp
from jax import lax
from jax.experimental import pallas as pl
from jax.experimental.pallas import tpu as pltpu
from jax.sharding import Mesh
from jax.sharding import PartitionSpec as P

HD = 192
PJ = 128
CORES = 2
LANES = 256
KV = 2 * HD
SHIFT = KV - LANES
F32 = jnp.float32
BF16 = jnp.bfloat16
VMEM_BYTES = 48 * 1024 * 1024


def contract(a, b, dim_a, dim_b, precision=None):
    return lax.dot_general(
        a, b, (((dim_a,), (dim_b,)), ((), ())), precision=precision, preferred_element_type=F32
    )


def iota(shape, axis):
    return lax.broadcasted_iota(jnp.int32, shape, axis)


def local_call(body, outs, operands, scratch=(), fetched=0):
    specs = [pl.BlockSpec(memory_space=pltpu.HBM)] * fetched
    specs += [pl.BlockSpec(memory_space=pltpu.VMEM)] * (operands - fetched)
    return pl.pallas_call(
        body,
        out_shape=tuple(jax.ShapeDtypeStruct(shape, kind) for shape, kind in outs),
        in_specs=specs,
        out_specs=tuple(pl.BlockSpec(memory_space=pltpu.VMEM) for _ in outs),
        scratch_shapes=list(scratch),
        compiler_params=pltpu.CompilerParams(vmem_limit_bytes=VMEM_BYTES),
    )


def split_terms(term, count=2):
    pieces = []
    for _ in range(count):
        piece = term.astype(BF16)
        pieces.append(piece)
        term = term - piece.astype(F32)
    return pieces


def project_body(
    hidden_hbm,
    w_key_hbm,
    w_value_hbm,
    w_junction_hbm,
    donor_hbm,
    acceptor_hbm,
    counts_hbm,
    pred_hbm,
    message,
    features,
    donor_hot,
    hidden,
    weights,
    w_junction,
    donor_pos,
    acceptor_pos,
    counts,
    pred_grad,
    sems,
):
    targets = (
        hidden,
        weights.at[pl.ds(0, HD)],
        weights.at[pl.ds(HD, HD)],
        w_junction,
        donor_pos,
        acceptor_pos,
        counts,
        pred_grad,
    )
    sources = (
        hidden_hbm,
        w_key_hbm,
        w_value_hbm,
        w_junction_hbm,
        donor_hbm,
        acceptor_hbm,
        counts_hbm,
        pred_hbm,
    )
    copies = [
        pltpu.make_async_copy(source, target, sems.at[i])
        for i, (source, target) in enumerate(zip(sources, targets))
    ]
    for copy in copies:
        copy.start()
    for copy in copies[:3]:
        copy.wait()
    chips = message.shape[0]
    tokens = hidden.shape[0]
    x = hidden[...]
    rows = contract(x, weights[...], 1, 1).astype(BF16)
    for copy in copies[3:]:
        copy.wait()
    feats = contract(x, w_junction[...], 1, 0).astype(BF16)
    features[...] = feats

    buckets, per = donor_pos.shape
    slots = buckets * per
    square = iota((buckets, buckets), 0) == iota((buckets, buckets), 1)
    limit = jnp.sum(
        jnp.where(square, counts[...].astype(F32), 0.0), axis=1, keepdims=True
    )
    slot_ids = lax.axis_index("head") * per + iota((buckets, per), 1)
    live_grad = jnp.where(slot_ids.astype(F32) < limit, pred_grad[...], 0.0)
    pick_bucket = (iota((slots, buckets), 0) // per == iota((slots, buckets), 1)).astype(F32)
    own_slot = iota((slots, per), 0) % per == iota((slots, per), 1)

    def to_column(value):
        wide = contract(pick_bucket, value.astype(F32), 1, 0, lax.Precision.HIGHEST)
        return jnp.sum(jnp.where(own_slot, wide, 0.0), axis=1, keepdims=True)

    donor = to_column(donor_pos[...])
    hot = jnp.where(iota((slots, tokens), 1).astype(F32) == donor, 1.0, 0.0).astype(BF16)
    donor_hot[...] = hot
    lane = iota((slots, PJ), 1)
    scalars = [to_column(acceptor_pos[...])]
    scalars += [piece.astype(F32) for piece in split_terms(to_column(live_grad), 3)]
    extra = jnp.zeros((slots, PJ), F32)
    for i, column in enumerate(scalars):
        extra = jnp.where(lane == i, column, extra)
    slot_rows = jnp.concatenate(
        [
            contract(hot, feats, 1, 0).astype(BF16),
            extra.astype(BF16),
            jnp.zeros((slots, KV - 2 * PJ), BF16),
        ],
        axis=1,
    )
    part = slots // chips
    for chip in range(chips):
        message[chip, :tokens, :] = rows
        message[chip, tokens:, :] = slot_rows[chip * part : (chip + 1) * part, :]


def query_body(hidden, w_query, ctx_t, queries, ctx):
    tokens = hidden.shape[0]
    pad = jnp.zeros((tokens, LANES - HD), BF16)
    value = contract(hidden[...], w_query[...], 1, 1).astype(BF16)
    queries[...] = jnp.concatenate([value, pad], axis=1)
    ctx[...] = jnp.concatenate([pad, jnp.transpose(ctx_t[...].astype(F32)).astype(BF16)], axis=1)


def attend_body(
    queries,
    ctx,
    features,
    mine,
    theirs,
    terms_theirs,
    back_mine,
    accept_sum,
    probs_b,
    dscores_b,
):
    tokens = queries.shape[0]
    chips, height, _ = mine.shape
    half = chips * tokens
    scale = HD ** (-0.5)
    sides = [ref[:, :tokens, :].reshape(half, KV) for ref in (mine, theirs)]
    rows = 64
    for start in range(0, tokens, rows):
        band = pl.ds(start, rows)
        q, g = queries[band, :], ctx[band, :]
        scores = [contract(q, side[:, :LANES], 1, 1) * scale for side in sides]
        row_max = jnp.maximum(
            jnp.max(scores[0], axis=-1, keepdims=True), jnp.max(scores[1], axis=-1, keepdims=True)
        )
        expd = [jnp.exp(score - row_max) for score in scores]
        inverse = 1.0 / (
            jnp.sum(expd[0], axis=-1, keepdims=True) + jnp.sum(expd[1], axis=-1, keepdims=True)
        )
        probs = [value * inverse for value in expd]
        dprobs = [contract(g, side[:, SHIFT:], 1, 1) for side in sides]
        row_delta = jnp.sum(probs[0] * dprobs[0], axis=-1, keepdims=True) + jnp.sum(
            probs[1] * dprobs[1], axis=-1, keepdims=True
        )
        for i in range(2):
            probs_b[i, band, :] = probs[i].astype(BF16)
            dscores_b[i, band, :] = (probs[i] * (dprobs[i] - row_delta)).astype(BF16)

    core = lax.axis_index("core")
    part = height - tokens
    per = part // CORES

    def own_rows(ref):
        block = ref[:, tokens:, :].astype(F32)
        return jnp.where(core == 0, block[:, :per, :], block[:, per:, :]).reshape(chips * per, KV)

    slot_rows = jnp.concatenate([own_rows(mine), own_rows(theirs)], axis=0)
    slots = slot_rows.shape[0]
    donor_feat = slot_rows[:, :PJ]
    extra = slot_rows[:, PJ : 2 * PJ]
    acceptor = extra[:, 0:1]
    slot_scale = extra[:, 1:2] + extra[:, 2:3] + extra[:, 3:4]
    hot = jnp.where(iota((slots, tokens), 1).astype(F32) == acceptor, 1.0, 0.0).astype(BF16)
    accept_feat = contract(hot, features[...], 1, 0)
    pair_scale = PJ ** (-0.5)
    pair_score = jnp.sum(donor_feat * accept_feat, axis=-1, keepdims=True) * pair_scale
    slot_grad = slot_scale * jax.nn.sigmoid(pair_score) * pair_scale
    total = jnp.zeros((tokens, PJ), F32)
    for piece in split_terms(slot_grad * donor_feat):
        total = total + contract(hot, piece, 0, 0)
    accept_sum[...] = total
    back = (slot_grad * accept_feat).reshape(2, chips, per, PJ)
    blank = jnp.zeros((2, chips, per, PJ), F32)

    upper = jnp.where(core == 0, back, blank)
    lower = jnp.where(core == 0, blank, back)
    back = jnp.concatenate([upper, lower], axis=2).astype(BF16)
    back_mine[...] = back[0]
    write_terms(terms_theirs, dscores_b[1], probs_b[1], queries[...], ctx[...], back[1])


def write_terms(terms, dscores, probs, queries, ctx, back):
    chips, height, _ = terms.shape
    part = back.shape[1]
    tokens = height - part
    key_term = contract(dscores, queries, 0, 0) * HD ** (-0.5)
    value_term = contract(probs, ctx, 0, 0)
    middle = key_term[:, SHIFT:] + value_term[:, :SHIFT]
    for first, value in (
        (0, key_term[:, :SHIFT]),
        (SHIFT, middle),
        (LANES, value_term[:, SHIFT:]),
    ):
        terms[:, :tokens, first : first + SHIFT] = value.astype(BF16).reshape(
            chips, tokens, SHIFT
        )
    terms[:, tokens:, :PJ] = back
    terms[:, tokens:, PJ:] = jnp.zeros((chips, part, KV - PJ), BF16)


def own_body(queries, ctx, mine, theirs, back, probs_b, dscores_b, terms_mine, query_grad):
    write_terms(terms_mine, dscores_b[0], probs_b[0], queries[...], ctx[...], back[...])
    chips, _, _ = mine.shape
    tokens = queries.shape[0]
    total = jnp.zeros((tokens, LANES), F32)
    for i, side in enumerate((mine, theirs)):
        keys = side[:, :tokens, :LANES].reshape(chips * tokens, LANES)
        total = total + contract(dscores_b[i], keys, 1, 0)
    query_grad[...] = (total[:, :HD] * HD ** (-0.5)).astype(BF16)


def halve(value, kept, sent, index):
    count = kept.shape[0]
    blocks = value.reshape((count, 2) + kept.shape[1:])
    odd = lax.rem(index, 2) == 1
    kept[...] = jnp.where(odd, blocks[:, 1], blocks[:, 0])
    sent[...] = jnp.where(odd, blocks[:, 0], blocks[:, 1]).astype(sent.dtype)


def quarter_body(held, got, *outs):
    place = lax.axis_index("head") // 2
    value = held[...] + got[...].astype(F32)
    for i, out in enumerate(outs):
        block = value[i]
        for other in range(1, len(outs)):
            block = jnp.where(place == other, value[i ^ other], block)
        out[...] = block.astype(out.dtype)


def total_body(*refs):
    value = refs[0][...].astype(F32)
    for ref in refs[1:-1]:
        value = value + ref[...].astype(F32)
    refs[-1][...] = value.astype(refs[-1].dtype)


def grads_body(parts, query_grad, hidden, grads, kept, sent):
    tokens, width = hidden.shape
    total = jnp.zeros((tokens, KV), F32)
    for chip in range(parts.shape[0]):
        total = total + parts[chip, :tokens, :].astype(F32)
    grads[...] = total.astype(BF16)
    core = lax.axis_index("core")
    cut = width // CORES
    first = 0
    for grad in (query_grad[...], grads[...]):
        value = contract(grad, hidden[...], 0, 0)
        rows = pl.ds(first, value.shape[0])
        left, right = value[:, :cut], value[:, cut:]
        kept[rows, :] = jnp.where(core == 0, left, right)
        sent[rows, :] = jnp.where(core == 0, right, left).astype(BF16)
        first += value.shape[0]


def input_body(
    parts,
    accept_sum,
    donor_hot,
    grads,
    query_grad,
    w_query,
    w_key,
    w_value,
    w_junction,
    kept,
    sent,
):
    chips, height, _ = parts.shape
    tokens = grads.shape[0]
    part = height - tokens
    slot_rows = parts[:, tokens:, :PJ].reshape(chips * part, PJ)
    feature_grad = (accept_sum[...] + contract(donor_hot[...], slot_rows, 0, 0)).astype(BF16)
    value = contract(w_query[...], query_grad[...], 0, 1)
    value = value + contract(w_key[...], grads[:, :HD], 0, 1)
    value = value + contract(w_value[...], grads[:, HD:], 0, 1)
    value = value + contract(w_junction[...], feature_grad, 1, 1)
    halve(value, kept, sent, lax.axis_index("head"))


def tiles_of(rows, columns, count):
    high, wide = rows * 2 // count, columns // 2
    return [(i, pl.ds(i // 2 * high, high), pl.ds(i % 2 * wide, wide)) for i in range(count)]


def cut_body(parts, tiles, whole):
    value = parts[0].astype(F32)
    for i in range(1, parts.shape[0]):
        value = value + parts[i].astype(F32)
    whole[...] = value
    for i, rows, columns in tiles_of(*whole.shape, tiles.shape[0]):
        tiles[i] = whole[rows, columns].astype(BF16)


def spread_body(parts, copies):
    value = parts[0].astype(F32)
    for i in range(1, parts.shape[0]):
        value = value + parts[i].astype(F32)
    value = value.astype(BF16)
    for i in range(copies.shape[0]):
        copies[i] = value


def join_body(tiles, joined, whole):
    for i, rows, columns in tiles_of(*whole.shape, tiles.shape[0]):
        whole[rows, columns] = tiles[i].astype(F32)
    joined[...] = whole[...].astype(BF16)


def place_body(mine, theirs, *outs):
    core = lax.axis_index("core")
    cut = mine.shape[1]
    for i, out in enumerate(outs):
        a, b = mine[i * HD : (i + 1) * HD, :], theirs[i * HD : (i + 1) * HD, :]
        out[:, :cut] = jnp.where(core == 0, a, b)
        out[:, cut:] = jnp.where(core == 0, b, a)


def swap_cores(value):
    return lax.ppermute(value, "core", [(0, 1), (1, 0)])


def exchange(value, axis):
    return lax.all_to_all(value, axis, 0, 0, tiled=True)


def on_device(
    hidden_in,
    ctx_grad,
    w_query,
    w_key,
    w_value,
    w_junction,
    donor_pos,
    acceptor_pos,
    junction_counts,
    pred_grad,
):
    hidden = hidden_in[0]
    tokens, width = hidden.shape
    chips = lax.axis_size("x")
    intervals = lax.axis_size("interval")
    heads = lax.axis_size("head")
    half = chips * tokens
    buckets, per = donor_pos.shape[2:]
    slots = buckets * per
    height = tokens + slots // chips

    message, features, donor_hot = local_call(
        project_body,
        [((chips, height, KV), BF16), ((tokens, PJ), BF16), ((slots, tokens), BF16)],
        operands=8,
        fetched=8,
        scratch=[
            pltpu.VMEM((tokens, width), BF16),
            pltpu.VMEM((KV, width), BF16),
            pltpu.VMEM((width, PJ), BF16),
            pltpu.VMEM((buckets, per), jnp.int32),
            pltpu.VMEM((buckets, per), jnp.int32),
            pltpu.VMEM((1, buckets), jnp.int32),
            pltpu.VMEM((buckets, per), F32),
            pltpu.SemaphoreType.DMA((8,)),
        ],
    )(
        *(
            pltpu.with_memory_space_constraint(value, pltpu.HBM)
            for value in (
                hidden,
                w_key,
                w_value,
                w_junction,
                donor_pos[0, 0],
                acceptor_pos[0, 0],
                junction_counts[0],
                pred_grad[0, 0],
            )
        )
    )
    mine = exchange(message, "x")
    theirs = swap_cores(mine)
    queries, ctx = local_call(query_body, [((tokens, LANES), BF16)] * 2, operands=3)(
        hidden, w_query, ctx_grad[0].T
    )
    terms_theirs, back_mine, accept_sum, probs_b, dscores_b = local_call(
        attend_body,
        [
            ((chips, height, KV), BF16),
            ((chips, height - tokens, PJ), BF16),
            ((tokens, PJ), F32),
            ((CORES, tokens, half), BF16),
            ((CORES, tokens, half), BF16),
        ],
        operands=5,
    )(queries, ctx, features, mine, theirs)
    terms_theirs = swap_cores(terms_theirs)
    terms_mine, query_grad = local_call(
        own_body, [((chips, height, KV), BF16), ((tokens, HD), BF16)], operands=7
    )(queries, ctx, mine, theirs, back_mine, probs_b, dscores_b)
    (pair_sum,) = local_call(total_body, [((chips, height, KV), BF16)], operands=2)(
        terms_mine, terms_theirs
    )
    parts = exchange(pair_sum, "x")
    rows = 3 * HD
    cut = width // CORES
    block = (width // heads, tokens)
    grads, weight_held, weight_sent = local_call(
        grads_body,
        [((tokens, KV), BF16), ((rows, cut), F32), ((rows, cut), BF16)],
        operands=3,
    )(parts, query_grad, hidden)
    weight_got = swap_cores(weight_sent)
    held, sent = local_call(
        input_body,
        [((heads // 2,) + block, F32), ((heads // 2,) + block, BF16)],
        operands=9,
    )(
        parts,
        accept_sum,
        donor_hot,
        grads,
        query_grad,
        w_query,
        w_key,
        w_value,
        w_junction,
    )

    def flip(value, mask):
        return lax.ppermute(value, "head", [(i, i ^ mask) for i in range(heads)])

    (term,) = local_call(total_body, [((rows, cut), BF16)], operands=2)(weight_held, weight_got)
    part = rows // chips
    tile = (part * 2 // intervals, cut // 2)
    (tiles,) = local_call(
        cut_body, [((intervals,) + tile, BF16)], operands=1, scratch=[pltpu.VMEM((part, cut), F32)]
    )(exchange(term.reshape(chips, part, cut), "x"))
    tiles, got = lax.optimization_barrier((tiles, flip(sent, 1)))
    held, *sent = local_call(
        quarter_body, [(block, F32)] + [(block, BF16)] * (heads // 2 - 1), operands=2
    )(held, got)
    (copies,) = local_call(spread_body, [((intervals,) + tile, BF16)], operands=1)(
        exchange(tiles, "interval")
    )
    (term,) = local_call(
        join_body, [((part, cut), BF16)], operands=1, scratch=[pltpu.VMEM((part, cut), F32)]
    )(exchange(copies, "interval"))
    got = [flip(value, 2 * (i + 1)) for i, value in enumerate(sent)]
    term, *got = lax.optimization_barrier((term, *got))
    term = lax.all_gather(term, "x", axis=0, tiled=True)
    (grad_input,) = local_call(total_body, [(block, BF16)], operands=heads // 2)(held, *got)
    grads = local_call(place_body, [((HD, width), BF16)] * 3, operands=2)(term, swap_cores(term))
    return (grad_input.T[None],) + tuple(grads)


def solution(mesh):
    axes = (mesh.shape["interval"], mesh.shape["seq"] // CORES, CORES, mesh.shape["head"])
    split = Mesh(mesh.devices.reshape(axes), ("interval", "x", "core", "head"))
    seq = ("x", "core")
    placed = (
        P("interval", seq, None),
        P("interval", seq, "head"),
        P("head", None),
        P("head", None),
        P("head", None),
        P(),
        P("interval", seq, None, "head"),
        P("interval", seq, None, "head"),
        P("interval", seq, None),
        P("interval", seq, None, "head"),
    )
    return jax.shard_map(
        on_device,
        mesh=split,
        in_specs=placed,
        out_specs=(P("interval", seq, "head"), P("head", None), P("head", None), P("head", None)),
        check_vma=False,
    )
```

```python
import functools

import jax
import jax.numpy as jnp
from jax import lax
from jax.experimental import pallas as pl
from jax.experimental.pallas import tpu as pltpu
from jax.sharding import Mesh
from jax.sharding import PartitionSpec as P

HD = 192
PJ = 128
CORES = 2
LANES = 256
KV = 2 * HD
SHIFT = KV - LANES
F32 = jnp.float32
BF16 = jnp.bfloat16
VMEM_BYTES = 20 * 1024 * 1024


def contract(a, b, dim_a, dim_b, precision=None):
    return lax.dot_general(
        a, b, (((dim_a,), (dim_b,)), ((), ())), precision=precision, preferred_element_type=F32
    )


def iota(shape, axis):
    return lax.broadcasted_iota(jnp.int32, shape, axis)


def local_call(body, outs, operands, scratch=(), fetched=0):
    specs = [pl.BlockSpec(memory_space=pltpu.HBM)] * fetched
    specs += [pl.BlockSpec(memory_space=pltpu.VMEM)] * (operands - fetched)
    return pl.pallas_call(
        body,
        out_shape=tuple(jax.ShapeDtypeStruct(shape, kind) for shape, kind in outs),
        in_specs=specs,
        out_specs=tuple(pl.BlockSpec(memory_space=pltpu.VMEM) for _ in outs),
        scratch_shapes=list(scratch),
        compiler_params=pltpu.CompilerParams(vmem_limit_bytes=VMEM_BYTES),
    )


def split_terms(term, count=2):
    pieces = []
    for _ in range(count):
        piece = term.astype(BF16)
        pieces.append(piece)
        term = term - piece.astype(F32)
    return pieces


def project_body(
    hidden_hbm,
    w_key_hbm,
    w_value_hbm,
    w_junction_hbm,
    donor_hbm,
    acceptor_hbm,
    counts_hbm,
    pred_hbm,
    message,
    features,
    donor_hot,
    hidden,
    weights,
    w_junction,
    donor_pos,
    acceptor_pos,
    counts,
    pred_grad,
    sems,
):
    targets = (
        hidden,
        weights.at[pl.ds(0, HD)],
        weights.at[pl.ds(HD, HD)],
        w_junction,
        donor_pos,
        acceptor_pos,
        counts,
        pred_grad,
    )
    sources = (
        hidden_hbm,
        w_key_hbm,
        w_value_hbm,
        w_junction_hbm,
        donor_hbm,
        acceptor_hbm,
        counts_hbm,
        pred_hbm,
    )
    copies = [
        pltpu.make_async_copy(source, target, sems.at[i])
        for i, (source, target) in enumerate(zip(sources, targets))
    ]
    for copy in copies:
        copy.start()
    for copy in copies[:3]:
        copy.wait()
    chips = message.shape[0]
    tokens = hidden.shape[0]
    x = hidden[...]
    rows = contract(x, weights[...], 1, 1).astype(BF16)
    for copy in copies[3:]:
        copy.wait()
    feats = contract(x, w_junction[...], 1, 0).astype(BF16)
    features[...] = feats

    buckets, per = donor_pos.shape
    slots = buckets * per
    square = iota((buckets, buckets), 0) == iota((buckets, buckets), 1)
    limit = jnp.sum(
        jnp.where(square, counts[...].astype(F32), 0.0), axis=1, keepdims=True
    )
    slot_ids = lax.axis_index("head") * per + iota((buckets, per), 1)
    live_grad = jnp.where(slot_ids.astype(F32) < limit, pred_grad[...], 0.0)
    pick_bucket = (iota((slots, buckets), 0) // per == iota((slots, buckets), 1)).astype(F32)
    own_slot = iota((slots, per), 0) % per == iota((slots, per), 1)

    def to_column(value):
        wide = contract(pick_bucket, value.astype(F32), 1, 0, lax.Precision.HIGHEST)
        return jnp.sum(jnp.where(own_slot, wide, 0.0), axis=1, keepdims=True)

    donor = to_column(donor_pos[...])
    hot = jnp.where(iota((slots, tokens), 1).astype(F32) == donor, 1.0, 0.0).astype(BF16)
    donor_hot[...] = hot
    lane = iota((slots, PJ), 1)
    scalars = [to_column(acceptor_pos[...])]
    scalars += [piece.astype(F32) for piece in split_terms(to_column(live_grad), 3)]
    extra = jnp.zeros((slots, PJ), F32)
    for i, column in enumerate(scalars):
        extra = jnp.where(lane == i, column, extra)
    slot_rows = jnp.concatenate(
        [
            contract(hot, feats, 1, 0).astype(BF16),
            extra.astype(BF16),
            jnp.zeros((slots, KV - 2 * PJ), BF16),
        ],
        axis=1,
    )
    part = slots // chips
    for chip in range(chips):
        message[chip, :tokens, :] = rows
        message[chip, tokens:, :] = slot_rows[chip * part : (chip + 1) * part, :]


def query_body(hidden, w_query, ctx_t, queries, ctx):
    tokens = hidden.shape[0]
    pad = jnp.zeros((tokens, LANES - HD), BF16)
    value = contract(hidden[...], w_query[...], 1, 1).astype(BF16)
    queries[...] = jnp.concatenate([value, pad], axis=1)
    ctx[...] = jnp.concatenate([pad, jnp.transpose(ctx_t[...].astype(F32)).astype(BF16)], axis=1)


def attend_body(
    queries,
    ctx,
    features,
    mine,
    theirs,
    terms_theirs,
    back_mine,
    accept_sum,
    probs_b,
    dscores_b,
):
    tokens = queries.shape[0]
    chips, height, _ = mine.shape
    half = chips * tokens
    scale = HD ** (-0.5)
    sides = [ref[:, :tokens, :].reshape(half, KV) for ref in (mine, theirs)]
    rows = 64
    for start in range(0, tokens, rows):
        band = pl.ds(start, rows)
        q, g = queries[band, :], ctx[band, :]
        scores = [contract(q, side[:, :LANES], 1, 1) * scale for side in sides]
        row_max = jnp.maximum(
            jnp.max(scores[0], axis=-1, keepdims=True), jnp.max(scores[1], axis=-1, keepdims=True)
        )
        expd = [jnp.exp(score - row_max) for score in scores]
        inverse = 1.0 / (
            jnp.sum(expd[0], axis=-1, keepdims=True) + jnp.sum(expd[1], axis=-1, keepdims=True)
        )
        probs = [value * inverse for value in expd]
        dprobs = [contract(g, side[:, SHIFT:], 1, 1) for side in sides]
        row_delta = jnp.sum(probs[0] * dprobs[0], axis=-1, keepdims=True) + jnp.sum(
            probs[1] * dprobs[1], axis=-1, keepdims=True
        )
        for i in range(2):
            probs_b[i, band, :] = probs[i].astype(BF16)
            dscores_b[i, band, :] = (probs[i] * (dprobs[i] - row_delta)).astype(BF16)

    core = lax.axis_index("core")
    part = height - tokens
    per = part // CORES

    def own_rows(ref):
        block = ref[:, tokens:, :].astype(F32)
        return jnp.where(core == 0, block[:, :per, :], block[:, per:, :]).reshape(chips * per, KV)

    slot_rows = jnp.concatenate([own_rows(mine), own_rows(theirs)], axis=0)
    slots = slot_rows.shape[0]
    donor_feat = slot_rows[:, :PJ]
    extra = slot_rows[:, PJ : 2 * PJ]
    acceptor = extra[:, 0:1]
    slot_scale = extra[:, 1:2] + extra[:, 2:3] + extra[:, 3:4]
    hot = jnp.where(iota((slots, tokens), 1).astype(F32) == acceptor, 1.0, 0.0).astype(BF16)
    accept_feat = contract(hot, features[...], 1, 0)
    pair_scale = PJ ** (-0.5)
    pair_score = jnp.sum(donor_feat * accept_feat, axis=-1, keepdims=True) * pair_scale
    slot_grad = slot_scale * jax.nn.sigmoid(pair_score) * pair_scale
    total = jnp.zeros((tokens, PJ), F32)
    for piece in split_terms(slot_grad * donor_feat):
        total = total + contract(hot, piece, 0, 0)
    accept_sum[...] = total
    back = (slot_grad * accept_feat).reshape(2, chips, per, PJ)
    blank = jnp.zeros((2, chips, per, PJ), F32)

    upper = jnp.where(core == 0, back, blank)
    lower = jnp.where(core == 0, blank, back)
    back = jnp.concatenate([upper, lower], axis=2).astype(BF16)
    back_mine[...] = back[0]
    write_terms(terms_theirs, dscores_b[1], probs_b[1], queries[...], ctx[...], back[1])


def write_terms(terms, dscores, probs, queries, ctx, back):
    chips, height, _ = terms.shape
    part = back.shape[1]
    tokens = height - part
    key_term = contract(dscores, queries, 0, 0) * HD ** (-0.5)
    value_term = contract(probs, ctx, 0, 0)
    middle = key_term[:, SHIFT:] + value_term[:, :SHIFT]
    for first, value in (
        (0, key_term[:, :SHIFT]),
        (SHIFT, middle),
        (LANES, value_term[:, SHIFT:]),
    ):
        terms[:, :tokens, first : first + SHIFT] = value.astype(BF16).reshape(
            chips, tokens, SHIFT
        )
    terms[:, tokens:, :PJ] = back
    terms[:, tokens:, PJ:] = jnp.zeros((chips, part, KV - PJ), BF16)


def own_body(queries, ctx, mine, theirs, back, probs_b, dscores_b, terms_mine, query_grad):
    write_terms(terms_mine, dscores_b[0], probs_b[0], queries[...], ctx[...], back[...])
    chips, _, _ = mine.shape
    tokens = queries.shape[0]
    total = jnp.zeros((tokens, LANES), F32)
    for i, side in enumerate((mine, theirs)):
        keys = side[:, :tokens, :LANES].reshape(chips * tokens, LANES)
        total = total + contract(dscores_b[i], keys, 1, 0)
    query_grad[...] = (total[:, :HD] * HD ** (-0.5)).astype(BF16)


def halve(value, kept, sent, index):
    count = kept.shape[0]
    blocks = value.reshape((count, 2) + kept.shape[1:])
    odd = lax.rem(index, 2) == 1
    kept[...] = jnp.where(odd, blocks[:, 1], blocks[:, 0])
    sent[...] = jnp.where(odd, blocks[:, 0], blocks[:, 1]).astype(sent.dtype)


def halve_body(level, held, got, kept, sent):
    halve(held[...] + got[...].astype(F32), kept, sent, lax.axis_index("head") // 2**level)


def total_body(*refs):
    value = refs[0][...].astype(F32)
    for ref in refs[1:-1]:
        value = value + ref[...].astype(F32)
    refs[-1][...] = value.astype(refs[-1].dtype)


def grads_body(parts, query_grad, hidden, grads, kept, sent):
    tokens, width = hidden.shape
    total = jnp.zeros((tokens, KV), F32)
    for chip in range(parts.shape[0]):
        total = total + parts[chip, :tokens, :].astype(F32)
    grads[...] = total.astype(BF16)
    core = lax.axis_index("core")
    cut = width // CORES
    first = 0
    for grad in (query_grad[...], grads[...]):
        value = contract(grad, hidden[...], 0, 0)
        rows = pl.ds(first, value.shape[0])
        left, right = value[:, :cut], value[:, cut:]
        kept[rows, :] = jnp.where(core == 0, left, right)
        sent[rows, :] = jnp.where(core == 0, right, left).astype(BF16)
        first += value.shape[0]


def input_body(
    parts,
    accept_sum,
    donor_hot,
    grads,
    query_grad,
    w_query,
    w_key,
    w_value,
    w_junction,
    kept,
    sent,
):
    chips, height, _ = parts.shape
    tokens = grads.shape[0]
    part = height - tokens
    slot_rows = parts[:, tokens:, :PJ].reshape(chips * part, PJ)
    feature_grad = (accept_sum[...] + contract(donor_hot[...], slot_rows, 0, 0)).astype(BF16)
    value = contract(w_query[...], query_grad[...], 0, 1)
    value = value + contract(w_key[...], grads[:, :HD], 0, 1)
    value = value + contract(w_value[...], grads[:, HD:], 0, 1)
    value = value + contract(w_junction[...], feature_grad, 1, 1)
    halve(value, kept, sent, lax.axis_index("head"))


def tiles_of(rows, columns, count):
    high, wide = rows * 2 // count, columns // 2
    return [(i, pl.ds(i // 2 * high, high), pl.ds(i % 2 * wide, wide)) for i in range(count)]


def cut_body(parts, tiles, whole):
    value = parts[0].astype(F32)
    for i in range(1, parts.shape[0]):
        value = value + parts[i].astype(F32)
    whole[...] = value
    for i, rows, columns in tiles_of(*whole.shape, tiles.shape[0]):
        tiles[i] = whole[rows, columns].astype(BF16)


def spread_body(parts, copies):
    value = parts[0].astype(F32)
    for i in range(1, parts.shape[0]):
        value = value + parts[i].astype(F32)
    value = value.astype(BF16)
    for i in range(copies.shape[0]):
        copies[i] = value


def join_body(tiles, joined, whole):
    for i, rows, columns in tiles_of(*whole.shape, tiles.shape[0]):
        whole[rows, columns] = tiles[i].astype(F32)
    joined[...] = whole[...].astype(BF16)


def place_body(mine, theirs, *outs):
    core = lax.axis_index("core")
    cut = mine.shape[1]
    for i, out in enumerate(outs):
        a, b = mine[i * HD : (i + 1) * HD, :], theirs[i * HD : (i + 1) * HD, :]
        out[:, :cut] = jnp.where(core == 0, a, b)
        out[:, cut:] = jnp.where(core == 0, b, a)


def swap_cores(value):
    return lax.ppermute(value, "core", [(0, 1), (1, 0)])


def exchange(value, axis):
    return lax.all_to_all(value, axis, 0, 0, tiled=True)


def on_device(
    hidden_in,
    ctx_grad,
    w_query,
    w_key,
    w_value,
    w_junction,
    donor_pos,
    acceptor_pos,
    junction_counts,
    pred_grad,
):
    hidden = hidden_in[0]
    tokens, width = hidden.shape
    chips = lax.axis_size("x")
    intervals = lax.axis_size("interval")
    heads = lax.axis_size("head")
    half = chips * tokens
    buckets, per = donor_pos.shape[2:]
    slots = buckets * per
    height = tokens + slots // chips

    message, features, donor_hot = local_call(
        project_body,
        [((chips, height, KV), BF16), ((tokens, PJ), BF16), ((slots, tokens), BF16)],
        operands=8,
        fetched=8,
        scratch=[
            pltpu.VMEM((tokens, width), BF16),
            pltpu.VMEM((KV, width), BF16),
            pltpu.VMEM((width, PJ), BF16),
            pltpu.VMEM((buckets, per), jnp.int32),
            pltpu.VMEM((buckets, per), jnp.int32),
            pltpu.VMEM((1, buckets), jnp.int32),
            pltpu.VMEM((buckets, per), F32),
            pltpu.SemaphoreType.DMA((8,)),
        ],
    )(
        *(
            pltpu.with_memory_space_constraint(value, pltpu.HBM)
            for value in (
                hidden,
                w_key,
                w_value,
                w_junction,
                donor_pos[0, 0],
                acceptor_pos[0, 0],
                junction_counts[0],
                pred_grad[0, 0],
            )
        )
    )
    mine = exchange(message, "x")
    theirs = swap_cores(mine)
    queries, ctx = local_call(query_body, [((tokens, LANES), BF16)] * 2, operands=3)(
        hidden, w_query, ctx_grad[0].T
    )
    terms_theirs, back_mine, accept_sum, probs_b, dscores_b = local_call(
        attend_body,
        [
            ((chips, height, KV), BF16),
            ((chips, height - tokens, PJ), BF16),
            ((tokens, PJ), F32),
            ((CORES, tokens, half), BF16),
            ((CORES, tokens, half), BF16),
        ],
        operands=5,
    )(queries, ctx, features, mine, theirs)
    terms_theirs = swap_cores(terms_theirs)
    terms_mine, query_grad = local_call(
        own_body, [((chips, height, KV), BF16), ((tokens, HD), BF16)], operands=7
    )(queries, ctx, mine, theirs, back_mine, probs_b, dscores_b)
    (pair_sum,) = local_call(total_body, [((chips, height, KV), BF16)], operands=2)(
        terms_mine, terms_theirs
    )
    parts = exchange(pair_sum, "x")
    rows = 3 * HD
    cut = width // CORES
    block = (width // heads, tokens)
    grads, weight_held, weight_sent = local_call(
        grads_body,
        [((tokens, KV), BF16), ((rows, cut), F32), ((rows, cut), BF16)],
        operands=3,
    )(parts, query_grad, hidden)
    held, sent = local_call(
        input_body,
        [((heads // 2,) + block, F32), ((heads // 2,) + block, BF16)],
        operands=9,
    )(
        parts,
        accept_sum,
        donor_hot,
        grads,
        query_grad,
        w_query,
        w_key,
        w_value,
        w_junction,
    )

    def flip(value, level):
        return lax.ppermute(value, "head", [(i, i ^ 2**level) for i in range(heads)])

    def fold(level, held, got):
        count = heads // 2 ** (level + 1)
        return local_call(
            functools.partial(halve_body, level),
            [((count,) + block, F32), ((count,) + block, BF16)],
            operands=2,
        )(held, got)

    weight_got, sent = lax.optimization_barrier((swap_cores(weight_sent), sent))
    (term,) = local_call(total_body, [((rows, cut), BF16)], operands=2)(weight_held, weight_got)
    part = rows // chips
    tile = (part * 2 // intervals, cut // 2)
    (tiles,) = local_call(
        cut_body, [((intervals,) + tile, BF16)], operands=1, scratch=[pltpu.VMEM((part, cut), F32)]
    )(exchange(term.reshape(chips, part, cut), "x"))
    tiles, got = lax.optimization_barrier((tiles, flip(sent, 0)))
    held, sent = fold(1, held, got)
    got = flip(sent, 1)
    (copies,) = local_call(spread_body, [((intervals,) + tile, BF16)], operands=1)(
        exchange(tiles, "interval")
    )
    (term,) = local_call(
        join_body, [((part, cut), BF16)], operands=1, scratch=[pltpu.VMEM((part, cut), F32)]
    )(exchange(copies, "interval"))
    term, got = lax.optimization_barrier((term, got))
    held, sent = fold(2, held, got)
    term, sent = lax.optimization_barrier((term, sent))
    got = flip(sent, 2)
    term = lax.all_gather(term, "x", axis=0, tiled=True)
    term, got = lax.optimization_barrier((term, got))
    (grad_input,) = local_call(total_body, [((1,) + block, BF16)], operands=2)(held, got)
    grad_input = grad_input[0]
    grads = local_call(place_body, [((HD, width), BF16)] * 3, operands=2)(term, swap_cores(term))
    return (grad_input.T[None],) + tuple(grads)


def solution(mesh):
    axes = (mesh.shape["interval"], mesh.shape["seq"] // CORES, CORES, mesh.shape["head"])
    split = Mesh(mesh.devices.reshape(axes), ("interval", "x", "core", "head"))
    seq = ("x", "core")
    placed = (
        P("interval", seq, None),
        P("interval", seq, "head"),
        P("head", None),
        P("head", None),
        P("head", None),
        P(),
        P("interval", seq, None, "head"),
        P("interval", seq, None, "head"),
        P("interval", seq, None),
        P("interval", seq, None, "head"),
    )
    return jax.shard_map(
        on_device,
        mesh=split,
        in_specs=placed,
        out_specs=(P("interval", seq, "head"), P("head", None), P("head", None), P("head", None)),
        check_vma=False,
    )
```

```python
import jax
import jax.numpy as jnp
from jax import lax
from jax.experimental import pallas as pl
from jax.experimental.pallas import tpu as pltpu
from jax.sharding import Mesh
from jax.sharding import PartitionSpec as P

HD = 192
PJ = 128
CORES = 2
LANES = 256
KV = 2 * HD
SHIFT = KV - LANES
F32 = jnp.float32
BF16 = jnp.bfloat16
VMEM_BYTES = 20 * 1024 * 1024


def contract(a, b, dim_a, dim_b, precision=None):
    return lax.dot_general(
        a, b, (((dim_a,), (dim_b,)), ((), ())), precision=precision, preferred_element_type=F32
    )


def iota(shape, axis):
    return lax.broadcasted_iota(jnp.int32, shape, axis)


def local_call(body, outs, operands, scratch=(), fetched=0, space=pltpu.VMEM):
    specs = [pl.BlockSpec(memory_space=pltpu.HBM)] * fetched
    specs += [pl.BlockSpec(memory_space=space)] * (operands - fetched)
    return pl.pallas_call(
        body,
        out_shape=tuple(jax.ShapeDtypeStruct(shape, kind) for shape, kind in outs),
        in_specs=specs,
        out_specs=tuple(pl.BlockSpec(memory_space=space) for _ in outs),
        scratch_shapes=list(scratch),
        compiler_params=pltpu.CompilerParams(vmem_limit_bytes=VMEM_BYTES),
    )


def split_terms(term, count=2):
    pieces = []
    for _ in range(count):
        piece = term.astype(BF16)
        pieces.append(piece)
        term = term - piece.astype(F32)
    return pieces


def project_body(
    hidden_hbm,
    w_key_hbm,
    w_value_hbm,
    w_junction_hbm,
    donor_hbm,
    acceptor_hbm,
    counts_hbm,
    pred_hbm,
    message,
    features,
    donor_hot,
    hidden,
    weights,
    w_junction,
    donor_pos,
    acceptor_pos,
    counts,
    pred_grad,
    sems,
):
    targets = (
        donor_pos,
        acceptor_pos,
        counts,
        pred_grad,
        hidden,
        weights.at[pl.ds(0, HD)],
        weights.at[pl.ds(HD, HD)],
        w_junction,
    )
    sources = (
        donor_hbm,
        acceptor_hbm,
        counts_hbm,
        pred_hbm,
        hidden_hbm,
        w_key_hbm,
        w_value_hbm,
        w_junction_hbm,
    )
    copies = [
        pltpu.make_async_copy(source, target, sems.at[i])
        for i, (source, target) in enumerate(zip(sources, targets))
    ]
    for copy in copies:
        copy.start()
    for copy in copies[:4]:
        copy.wait()
    chips = message.shape[0]
    tokens = hidden.shape[0]
    buckets, per = donor_pos.shape
    slots = buckets * per
    square = iota((buckets, buckets), 0) == iota((buckets, buckets), 1)
    limit = jnp.sum(
        jnp.where(square, counts[...].astype(F32), 0.0), axis=1, keepdims=True
    )
    slot_ids = lax.axis_index("head") * per + iota((buckets, per), 1)
    live_grad = jnp.where(slot_ids.astype(F32) < limit, pred_grad[...], 0.0)
    pick_bucket = (iota((slots, buckets), 0) // per == iota((slots, buckets), 1)).astype(F32)
    own_slot = iota((slots, per), 0) % per == iota((slots, per), 1)

    def to_column(value):
        wide = contract(pick_bucket, value.astype(F32), 1, 0, lax.Precision.HIGHEST)
        return jnp.sum(jnp.where(own_slot, wide, 0.0), axis=1, keepdims=True)

    donor = to_column(donor_pos[...])
    hot = jnp.where(iota((slots, tokens), 1).astype(F32) == donor, 1.0, 0.0).astype(BF16)
    donor_hot[...] = hot
    lane = iota((slots, PJ), 1)
    scalars = [to_column(acceptor_pos[...])]
    scalars += [piece.astype(F32) for piece in split_terms(to_column(live_grad), 3)]
    extra = jnp.zeros((slots, PJ), F32)
    for i, column in enumerate(scalars):
        extra = jnp.where(lane == i, column, extra)
    for copy in copies[4:]:
        copy.wait()
    x = hidden[...]
    rows = contract(x, weights[...], 1, 1).astype(BF16)
    feats = contract(x, w_junction[...], 1, 0).astype(BF16)
    features[...] = feats
    slot_rows = jnp.concatenate(
        [
            contract(hot, feats, 1, 0).astype(BF16),
            extra.astype(BF16),
            jnp.zeros((slots, KV - 2 * PJ), BF16),
        ],
        axis=1,
    )
    part = slots // chips
    for chip in range(chips):
        message[chip, :tokens, :] = rows
        message[chip, tokens:, :] = slot_rows[chip * part : (chip + 1) * part, :]


def query_body(hidden, w_query, ctx_t, queries, ctx):
    tokens = hidden.shape[0]
    pad = jnp.zeros((tokens, LANES - HD), BF16)
    value = contract(hidden[...], w_query[...], 1, 1).astype(BF16)
    queries[...] = jnp.concatenate([value, pad], axis=1)
    ctx[...] = jnp.concatenate([pad, jnp.transpose(ctx_t[...].astype(F32)).astype(BF16)], axis=1)


def attend_body(
    queries,
    ctx,
    features,
    mine,
    theirs,
    terms_theirs,
    back_mine,
    accept_sum,
    probs_b,
    dscores_b,
):
    tokens = queries.shape[0]
    chips, height, _ = mine.shape
    half = chips * tokens
    scale = HD ** (-0.5)
    sides = [ref[:, :tokens, :].reshape(half, KV) for ref in (mine, theirs)]
    rows = 64
    for start in range(0, tokens, rows):
        band = pl.ds(start, rows)
        q, g = queries[band, :], ctx[band, :]
        scores = [contract(q, side[:, :LANES], 1, 1) * scale for side in sides]
        row_max = jnp.maximum(
            jnp.max(scores[0], axis=-1, keepdims=True), jnp.max(scores[1], axis=-1, keepdims=True)
        )
        expd = [jnp.exp(score - row_max) for score in scores]
        inverse = 1.0 / (
            jnp.sum(expd[0], axis=-1, keepdims=True) + jnp.sum(expd[1], axis=-1, keepdims=True)
        )
        probs = [value * inverse for value in expd]
        dprobs = [contract(g, side[:, SHIFT:], 1, 1) for side in sides]
        row_delta = jnp.sum(probs[0] * dprobs[0], axis=-1, keepdims=True) + jnp.sum(
            probs[1] * dprobs[1], axis=-1, keepdims=True
        )
        for i in range(2):
            probs_b[i, band, :] = probs[i].astype(BF16)
            dscores_b[i, band, :] = (probs[i] * (dprobs[i] - row_delta)).astype(BF16)

    core = lax.axis_index("core")
    part = height - tokens
    per = part // CORES

    def own_rows(ref):
        block = ref[:, tokens:, :].astype(F32)
        return jnp.where(core == 0, block[:, :per, :], block[:, per:, :]).reshape(chips * per, KV)

    slot_rows = jnp.concatenate([own_rows(mine), own_rows(theirs)], axis=0)
    slots = slot_rows.shape[0]
    donor_feat = slot_rows[:, :PJ]
    extra = slot_rows[:, PJ : 2 * PJ]
    acceptor = extra[:, 0:1]
    slot_scale = extra[:, 1:2] + extra[:, 2:3] + extra[:, 3:4]
    hot = jnp.where(iota((slots, tokens), 1).astype(F32) == acceptor, 1.0, 0.0).astype(BF16)
    accept_feat = contract(hot, features[...], 1, 0)
    pair_scale = PJ ** (-0.5)
    pair_score = jnp.sum(donor_feat * accept_feat, axis=-1, keepdims=True) * pair_scale
    slot_grad = slot_scale * jax.nn.sigmoid(pair_score) * pair_scale
    total = jnp.zeros((tokens, PJ), F32)
    for piece in split_terms(slot_grad * donor_feat):
        total = total + contract(hot, piece, 0, 0)
    accept_sum[...] = total
    back = (slot_grad * accept_feat).reshape(2, chips, per, PJ)
    blank = jnp.zeros((2, chips, per, PJ), F32)

    upper = jnp.where(core == 0, back, blank)
    lower = jnp.where(core == 0, blank, back)
    back = jnp.concatenate([upper, lower], axis=2).astype(BF16)
    back_mine[...] = back[0]
    write_terms(terms_theirs, dscores_b[1], probs_b[1], queries[...], ctx[...], back[1])


def write_terms(terms, dscores, probs, queries, ctx, back):
    chips, height, _ = terms.shape
    part = back.shape[1]
    tokens = height - part
    key_term = contract(dscores, queries, 0, 0) * HD ** (-0.5)
    value_term = contract(probs, ctx, 0, 0)
    middle = key_term[:, SHIFT:] + value_term[:, :SHIFT]
    for first, value in (
        (0, key_term[:, :SHIFT]),
        (SHIFT, middle),
        (LANES, value_term[:, SHIFT:]),
    ):
        terms[:, :tokens, first : first + SHIFT] = value.astype(BF16).reshape(
            chips, tokens, SHIFT
        )
    terms[:, tokens:, :PJ] = back
    terms[:, tokens:, PJ:] = jnp.zeros((chips, part, KV - PJ), BF16)


def own_body(queries, ctx, mine, theirs, back, probs_b, dscores_b, terms_mine, query_grad):
    write_terms(terms_mine, dscores_b[0], probs_b[0], queries[...], ctx[...], back[...])
    chips, _, _ = mine.shape
    tokens = queries.shape[0]
    total = jnp.zeros((tokens, LANES), F32)
    for i, side in enumerate((mine, theirs)):
        keys = side[:, :tokens, :LANES].reshape(chips * tokens, LANES)
        total = total + contract(dscores_b[i], keys, 1, 0)
    query_grad[...] = (total[:, :HD] * HD ** (-0.5)).astype(BF16)


def halve(value, index):
    blocks = value.reshape((value.shape[0] // 2, 2) + value.shape[1:])
    odd = lax.rem(index, 2) == 1
    kept = jnp.where(odd, blocks[:, 1], blocks[:, 0])
    sent = jnp.where(odd, blocks[:, 0], blocks[:, 1])
    return kept, sent.astype(BF16)


def second_body(held, got, kept, near, far):
    value, sent = halve(held[...] + got[...].astype(F32), lax.axis_index("head") // 2)
    kept[...] = value
    side = near.shape[-1]
    near[...] = sent[:, :, :side]
    far[...] = sent[:, :, side:]


def third_body(held, near, far, kept, sent):
    got = jnp.concatenate([near[...], far[...]], axis=2).astype(F32)
    value, leaving = halve(held[...] + got, lax.axis_index("head") // 4)
    kept[...] = value[0]
    sent[...] = leaving[0]


def total_body(*refs):
    value = refs[0][...].astype(F32)
    for ref in refs[1:-1]:
        value = value + ref[...].astype(F32)
    refs[-1][...] = value.astype(refs[-1].dtype)


def grads_body(parts, query_grad, hidden, grads, kept, sent):
    tokens, width = hidden.shape
    total = jnp.zeros((tokens, KV), F32)
    for chip in range(parts.shape[0]):
        total = total + parts[chip, :tokens, :].astype(F32)
    grads[...] = total.astype(BF16)
    core = lax.axis_index("core")
    cut = width // CORES
    first = 0
    for grad in (query_grad[...], grads[...]):
        value = contract(grad, hidden[...], 0, 0)
        rows = pl.ds(first, value.shape[0])
        left, right = value[:, :cut], value[:, cut:]
        kept[rows, :] = jnp.where(core == 0, left, right)
        sent[rows, :] = jnp.where(core == 0, right, left).astype(BF16)
        first += value.shape[0]


def input_body(
    parts,
    accept_sum,
    donor_hot,
    grads,
    query_grad,
    w_query,
    w_key,
    w_value,
    w_junction,
    kept,
    sent,
):
    chips, height, _ = parts.shape
    tokens = grads.shape[0]
    part = height - tokens
    slot_rows = parts[:, tokens:, :PJ].reshape(chips * part, PJ)
    feature_grad = (accept_sum[...] + contract(donor_hot[...], slot_rows, 0, 0)).astype(BF16)
    value = contract(w_query[...], query_grad[...], 0, 1)
    value = value + contract(w_key[...], grads[:, :HD], 0, 1)
    value = value + contract(w_value[...], grads[:, HD:], 0, 1)
    value = value + contract(w_junction[...], feature_grad, 1, 1)
    blocks = value.reshape((2 * kept.shape[0],) + kept.shape[1:])
    kept[...], sent[...] = halve(blocks, lax.axis_index("head"))


def tiles_of(rows, columns, count):
    high, wide = rows * 2 // count, columns // 2
    return [(i, pl.ds(i // 2 * high, high), pl.ds(i % 2 * wide, wide)) for i in range(count)]


def cut_body(parts, tiles, whole):
    value = parts[0].astype(F32)
    for i in range(1, parts.shape[0]):
        value = value + parts[i].astype(F32)
    whole[...] = value
    for i, rows, columns in tiles_of(*whole.shape, tiles.shape[0]):
        tiles[i] = whole[rows, columns].astype(BF16)


def spread_body(parts, copies):
    value = parts[0].astype(F32)
    for i in range(1, parts.shape[0]):
        value = value + parts[i].astype(F32)
    value = value.astype(BF16)
    for i in range(copies.shape[0]):
        copies[i] = value


def join_body(tiles, joined, whole):
    for i, rows, columns in tiles_of(*whole.shape, tiles.shape[0]):
        whole[rows, columns] = tiles[i].astype(F32)
    joined[...] = whole[...].astype(BF16)


def place_body(mine, theirs, *refs):
    outs, sems = refs[:-1], refs[-1]
    core = lax.axis_index("core")
    cut = mine.shape[1]
    copies = []
    for i, out in enumerate(outs):
        for j, (source, place) in enumerate(((mine, core), (theirs, 1 - core))):
            columns = pl.ds(pl.multiple_of(place * cut, cut), cut)
            copies.append(
                pltpu.make_async_copy(
                    source.at[pl.ds(i * HD, HD)], out.at[:, columns], sems.at[2 * i + j]
                )
            )
    for copy in copies:
        copy.start()
    for copy in copies:
        copy.wait()


def swap_cores(value):
    return lax.ppermute(value, "core", [(0, 1), (1, 0)])


def exchange(value, axis):
    return lax.all_to_all(value, axis, 0, 0, tiled=True)


def on_device(
    hidden_in,
    ctx_grad,
    w_query,
    w_key,
    w_value,
    w_junction,
    donor_pos,
    acceptor_pos,
    junction_counts,
    pred_grad,
):
    hidden = hidden_in[0]
    tokens, width = hidden.shape
    chips = lax.axis_size("x")
    intervals = lax.axis_size("interval")
    heads = lax.axis_size("head")
    half = chips * tokens
    buckets, per = donor_pos.shape[2:]
    slots = buckets * per
    height = tokens + slots // chips

    message, features, donor_hot = local_call(
        project_body,
        [((chips, height, KV), BF16), ((tokens, PJ), BF16), ((slots, tokens), BF16)],
        operands=8,
        fetched=8,
        scratch=[
            pltpu.VMEM((tokens, width), BF16),
            pltpu.VMEM((KV, width), BF16),
            pltpu.VMEM((width, PJ), BF16),
            pltpu.VMEM((buckets, per), jnp.int32),
            pltpu.VMEM((buckets, per), jnp.int32),
            pltpu.VMEM((1, buckets), jnp.int32),
            pltpu.VMEM((buckets, per), F32),
            pltpu.SemaphoreType.DMA((8,)),
        ],
    )(
        *(
            pltpu.with_memory_space_constraint(value, pltpu.HBM)
            for value in (
                hidden,
                w_key,
                w_value,
                w_junction,
                donor_pos[0, 0],
                acceptor_pos[0, 0],
                junction_counts[0],
                pred_grad[0, 0],
            )
        )
    )
    mine = exchange(message, "x")
    theirs = swap_cores(mine)
    queries, ctx = local_call(query_body, [((tokens, LANES), BF16)] * 2, operands=3)(
        hidden, w_query, ctx_grad[0].T
    )
    terms_theirs, back_mine, accept_sum, probs_b, dscores_b = local_call(
        attend_body,
        [
            ((chips, height, KV), BF16),
            ((chips, height - tokens, PJ), BF16),
            ((tokens, PJ), F32),
            ((CORES, tokens, half), BF16),
            ((CORES, tokens, half), BF16),
        ],
        operands=5,
    )(queries, ctx, features, mine, theirs)
    terms_theirs = swap_cores(terms_theirs)
    terms_mine, query_grad = local_call(
        own_body, [((chips, height, KV), BF16), ((tokens, HD), BF16)], operands=7
    )(queries, ctx, mine, theirs, back_mine, probs_b, dscores_b)
    (pair_sum,) = local_call(total_body, [((chips, height, KV), BF16)], operands=2)(
        terms_mine, terms_theirs
    )
    parts = exchange(pair_sum, "x")
    rows = 3 * HD
    cut = width // CORES
    block = (width // heads, tokens)
    grads, weight_held, weight_sent = local_call(
        grads_body,
        [((tokens, KV), BF16), ((rows, cut), F32), ((rows, cut), BF16)],
        operands=3,
    )(parts, query_grad, hidden)
    held, sent = local_call(
        input_body,
        [((heads // 2,) + block, F32), ((heads // 2,) + block, BF16)],
        operands=9,
    )(
        parts,
        accept_sum,
        donor_hot,
        grads,
        query_grad,
        w_query,
        w_key,
        w_value,
        w_junction,
    )

    def flip(value, mask):
        return lax.ppermute(value, "head", [(i, i ^ mask) for i in range(heads)])

    weight_got, sent = lax.optimization_barrier((swap_cores(weight_sent), sent))
    (term,) = local_call(total_body, [((rows, cut), BF16)], operands=2)(weight_held, weight_got)
    part = rows // chips
    tile = (part * 2 // intervals, cut // 2)
    (tiles,) = local_call(
        cut_body, [((intervals,) + tile, BF16)], operands=1, scratch=[pltpu.VMEM((part, cut), F32)]
    )(exchange(term.reshape(chips, part, cut), "x"))
    tiles, got = lax.optimization_barrier((tiles, flip(sent, 1)))
    side = tokens // 2
    held, near, far = local_call(
        second_body,
        [((heads // 4,) + block, F32)] + [((heads // 4, block[0], side), BF16)] * 2,
        operands=2,
    )(held, got)
    got = (flip(near, 2), flip(far, 6))
    (copies,) = local_call(spread_body, [((intervals,) + tile, BF16)], operands=1)(
        exchange(tiles, "interval")
    )
    (term,) = local_call(
        join_body, [((part, cut), BF16)], operands=1, scratch=[pltpu.VMEM((part, cut), F32)]
    )(exchange(copies, "interval"))
    term, *got = lax.optimization_barrier((term, *got))
    held, sent = local_call(third_body, [(block, F32), (block, BF16)], operands=3)(held, *got)
    term, sent = lax.optimization_barrier((term, sent))
    got = flip(sent, 4)
    term = lax.all_gather(term, "x", axis=0, tiled=True)
    term, got = lax.optimization_barrier((term, got))
    (grad_input,) = local_call(total_body, [(block, BF16)], operands=2)(held, got)
    grads = local_call(
        place_body,
        [((HD, width), BF16)] * 3,
        operands=2,
        scratch=[pltpu.SemaphoreType.DMA((2 * 3,))],
        space=pl.ANY,
    )(term, swap_cores(term))
    return (grad_input.T[None],) + tuple(grads)


def solution(mesh):
    axes = (mesh.shape["interval"], mesh.shape["seq"] // CORES, CORES, mesh.shape["head"])
    split = Mesh(mesh.devices.reshape(axes), ("interval", "x", "core", "head"))
    seq = ("x", "core")
    placed = (
        P("interval", seq, None),
        P("interval", seq, "head"),
        P("head", None),
        P("head", None),
        P("head", None),
        P(),
        P("interval", seq, None, "head"),
        P("interval", seq, None, "head"),
        P("interval", seq, None),
        P("interval", seq, None, "head"),
    )
    return jax.shard_map(
        on_device,
        mesh=split,
        in_specs=placed,
        out_specs=(P("interval", seq, "head"), P("head", None), P("head", None), P("head", None)),
        check_vma=False,
    )
```

```python
import jax
import jax.numpy as jnp
from jax import lax
from jax.experimental import pallas as pl
from jax.experimental.pallas import tpu as pltpu
from jax.sharding import Mesh
from jax.sharding import PartitionSpec as P

HD = 192
PJ = 128
CORES = 2
SIDES = 2
LANES = 256
KV = 2 * HD
SHIFT = KV - LANES
F32 = jnp.float32
BF16 = jnp.bfloat16
VMEM_BYTES = 20 * 1024 * 1024


def contract(a, b, dim_a, dim_b, precision=None):
    return lax.dot_general(
        a, b, (((dim_a,), (dim_b,)), ((), ())), precision=precision, preferred_element_type=F32
    )


def iota(shape, axis):
    return lax.broadcasted_iota(jnp.int32, shape, axis)


def local_call(body, outs, operands, scratch=(), fetched=0, space=pltpu.VMEM):
    specs = [pl.BlockSpec(memory_space=pltpu.HBM)] * fetched
    specs += [pl.BlockSpec(memory_space=space)] * (operands - fetched)
    return pl.pallas_call(
        body,
        out_shape=tuple(jax.ShapeDtypeStruct(shape, kind) for shape, kind in outs),
        in_specs=specs,
        out_specs=tuple(pl.BlockSpec(memory_space=space) for _ in outs),
        scratch_shapes=list(scratch),
        compiler_params=pltpu.CompilerParams(vmem_limit_bytes=VMEM_BYTES),
    )


def split_terms(term, count=2):
    pieces = []
    for _ in range(count):
        piece = term.astype(BF16)
        pieces.append(piece)
        term = term - piece.astype(F32)
    return pieces


def project_body(
    hidden_hbm,
    w_key_hbm,
    w_value_hbm,
    w_junction_hbm,
    donor_hbm,
    acceptor_hbm,
    counts_hbm,
    pred_hbm,
    message,
    features,
    donor_hot,
    hidden,
    weights,
    w_junction,
    donor_pos,
    acceptor_pos,
    counts,
    pred_grad,
    sems,
):
    targets = (
        donor_pos,
        acceptor_pos,
        counts,
        pred_grad,
        hidden,
        weights.at[pl.ds(0, HD)],
        weights.at[pl.ds(HD, HD)],
        w_junction,
    )
    sources = (
        donor_hbm,
        acceptor_hbm,
        counts_hbm,
        pred_hbm,
        hidden_hbm,
        w_key_hbm,
        w_value_hbm,
        w_junction_hbm,
    )
    copies = [
        pltpu.make_async_copy(source, target, sems.at[i])
        for i, (source, target) in enumerate(zip(sources, targets))
    ]
    for copy in copies:
        copy.start()
    for copy in copies[:4]:
        copy.wait()
    chips = message.shape[0]
    tokens = hidden.shape[0]
    buckets, per = donor_pos.shape
    slots = buckets * per
    square = iota((buckets, buckets), 0) == iota((buckets, buckets), 1)
    limit = jnp.sum(
        jnp.where(square, counts[...].astype(F32), 0.0), axis=1, keepdims=True
    )
    head = lax.axis_index("pair") * SIDES + lax.axis_index("side")
    slot_ids = head * per + iota((buckets, per), 1)
    live_grad = jnp.where(slot_ids.astype(F32) < limit, pred_grad[...], 0.0)
    pick_bucket = (iota((slots, buckets), 0) // per == iota((slots, buckets), 1)).astype(F32)
    own_slot = iota((slots, per), 0) % per == iota((slots, per), 1)

    def to_column(value):
        wide = contract(pick_bucket, value.astype(F32), 1, 0, lax.Precision.HIGHEST)
        return jnp.sum(jnp.where(own_slot, wide, 0.0), axis=1, keepdims=True)

    donor = to_column(donor_pos[...])
    hot = jnp.where(iota((slots, tokens), 1).astype(F32) == donor, 1.0, 0.0).astype(BF16)
    donor_hot[...] = hot
    lane = iota((slots, PJ), 1)
    scalars = [to_column(acceptor_pos[...])]
    scalars += [piece.astype(F32) for piece in split_terms(to_column(live_grad), 3)]
    extra = jnp.zeros((slots, PJ), F32)
    for i, column in enumerate(scalars):
        extra = jnp.where(lane == i, column, extra)
    for copy in copies[4:]:
        copy.wait()
    x = hidden[...]
    rows = contract(x, weights[...], 1, 1).astype(BF16)
    feats = contract(x, w_junction[...], 1, 0).astype(BF16)
    features[...] = feats
    slot_rows = jnp.concatenate(
        [
            contract(hot, feats, 1, 0).astype(BF16),
            extra.astype(BF16),
            jnp.zeros((slots, KV - 2 * PJ), BF16),
        ],
        axis=1,
    )
    part = slots // chips
    for chip in range(chips):
        message[chip, :tokens, :] = rows
        message[chip, tokens:, :] = slot_rows[chip * part : (chip + 1) * part, :]


def query_body(hidden, w_query, ctx_t, queries, ctx):
    tokens = hidden.shape[0]
    pad = jnp.zeros((tokens, LANES - HD), BF16)
    value = contract(hidden[...], w_query[...], 1, 1).astype(BF16)
    queries[...] = jnp.concatenate([value, pad], axis=1)
    ctx[...] = jnp.concatenate([pad, jnp.transpose(ctx_t[...].astype(F32)).astype(BF16)], axis=1)


def attend_body(
    queries,
    ctx,
    features,
    mine,
    theirs,
    terms_theirs,
    back_mine,
    accept_sum,
    probs_b,
    dscores_b,
):
    tokens = queries.shape[0]
    chips, height, _ = mine.shape
    half = chips * tokens
    scale = HD ** (-0.5)
    sides = [ref[:, :tokens, :].reshape(half, KV) for ref in (mine, theirs)]
    rows = 64
    for start in range(0, tokens, rows):
        band = pl.ds(start, rows)
        q, g = queries[band, :], ctx[band, :]
        scores = [contract(q, side[:, :LANES], 1, 1) * scale for side in sides]
        row_max = jnp.maximum(
            jnp.max(scores[0], axis=-1, keepdims=True), jnp.max(scores[1], axis=-1, keepdims=True)
        )
        expd = [jnp.exp(score - row_max) for score in scores]
        inverse = 1.0 / (
            jnp.sum(expd[0], axis=-1, keepdims=True) + jnp.sum(expd[1], axis=-1, keepdims=True)
        )
        probs = [value * inverse for value in expd]
        dprobs = [contract(g, side[:, SHIFT:], 1, 1) for side in sides]
        row_delta = jnp.sum(probs[0] * dprobs[0], axis=-1, keepdims=True) + jnp.sum(
            probs[1] * dprobs[1], axis=-1, keepdims=True
        )
        for i in range(2):
            probs_b[i, band, :] = probs[i].astype(BF16)
            dscores_b[i, band, :] = (probs[i] * (dprobs[i] - row_delta)).astype(BF16)

    core = lax.axis_index("core")
    part = height - tokens
    per = part // CORES

    def own_rows(ref):
        block = ref[:, tokens:, :].astype(F32)
        return jnp.where(core == 0, block[:, :per, :], block[:, per:, :]).reshape(chips * per, KV)

    slot_rows = jnp.concatenate([own_rows(mine), own_rows(theirs)], axis=0)
    slots = slot_rows.shape[0]
    donor_feat = slot_rows[:, :PJ]
    extra = slot_rows[:, PJ : 2 * PJ]
    acceptor = extra[:, 0:1]
    slot_scale = extra[:, 1:2] + extra[:, 2:3] + extra[:, 3:4]
    hot = jnp.where(iota((slots, tokens), 1).astype(F32) == acceptor, 1.0, 0.0).astype(BF16)
    accept_feat = contract(hot, features[...], 1, 0)
    pair_scale = PJ ** (-0.5)
    pair_score = jnp.sum(donor_feat * accept_feat, axis=-1, keepdims=True) * pair_scale
    slot_grad = slot_scale * jax.nn.sigmoid(pair_score) * pair_scale
    total = jnp.zeros((tokens, PJ), F32)
    for piece in split_terms(slot_grad * donor_feat):
        total = total + contract(hot, piece, 0, 0)
    accept_sum[...] = total
    back = (slot_grad * accept_feat).reshape(2, chips, per, PJ)
    blank = jnp.zeros((2, chips, per, PJ), F32)

    upper = jnp.where(core == 0, back, blank)
    lower = jnp.where(core == 0, blank, back)
    back = jnp.concatenate([upper, lower], axis=2).astype(BF16)
    back_mine[...] = back[0]
    write_terms(terms_theirs, dscores_b[1], probs_b[1], queries[...], ctx[...], back[1])


def write_terms(terms, dscores, probs, queries, ctx, back):
    chips, height, _ = terms.shape
    part = back.shape[1]
    tokens = height - part
    key_term = contract(dscores, queries, 0, 0) * HD ** (-0.5)
    value_term = contract(probs, ctx, 0, 0)
    middle = key_term[:, SHIFT:] + value_term[:, :SHIFT]
    for first, value in (
        (0, key_term[:, :SHIFT]),
        (SHIFT, middle),
        (LANES, value_term[:, SHIFT:]),
    ):
        terms[:, :tokens, first : first + SHIFT] = value.astype(BF16).reshape(
            chips, tokens, SHIFT
        )
    terms[:, tokens:, :PJ] = back
    terms[:, tokens:, PJ:] = jnp.zeros((chips, part, KV - PJ), BF16)


def own_body(queries, ctx, mine, theirs, back, probs_b, dscores_b, terms_mine, query_grad):
    write_terms(terms_mine, dscores_b[0], probs_b[0], queries[...], ctx[...], back[...])
    chips, _, _ = mine.shape
    tokens = queries.shape[0]
    total = jnp.zeros((tokens, LANES), F32)
    for i, side in enumerate((mine, theirs)):
        keys = side[:, :tokens, :LANES].reshape(chips * tokens, LANES)
        total = total + contract(dscores_b[i], keys, 1, 0)
    query_grad[...] = (total[:, :HD] * HD ** (-0.5)).astype(BF16)


def halve(value, side):
    blocks = value.reshape((value.shape[0] // 2, 2) + value.shape[1:])
    odd = side == 1
    kept = jnp.where(odd, blocks[:, 1], blocks[:, 0])
    sent = jnp.where(odd, blocks[:, 0], blocks[:, 1])
    return kept, sent.astype(BF16)


def total_body(*refs):
    value = refs[0][...].astype(F32)
    for ref in refs[1:-1]:
        value = value + ref[...].astype(F32)
    refs[-1][...] = value.astype(refs[-1].dtype)


def grads_body(parts, query_grad, hidden, grads, kept, sent):
    tokens, width = hidden.shape
    total = jnp.zeros((tokens, KV), F32)
    for chip in range(parts.shape[0]):
        total = total + parts[chip, :tokens, :].astype(F32)
    grads[...] = total.astype(BF16)
    core = lax.axis_index("core")
    cut = width // CORES
    first = 0
    for grad in (query_grad[...], grads[...]):
        value = contract(grad, hidden[...], 0, 0)
        rows = pl.ds(first, value.shape[0])
        left, right = value[:, :cut], value[:, cut:]
        kept[rows, :] = jnp.where(core == 0, left, right)
        sent[rows, :] = jnp.where(core == 0, right, left).astype(BF16)
        first += value.shape[0]


def input_body(
    parts,
    accept_sum,
    donor_hot,
    grads,
    query_grad,
    w_query,
    w_key,
    w_value,
    w_junction,
    kept,
    sent,
):
    chips, height, _ = parts.shape
    tokens = grads.shape[0]
    part = height - tokens
    slot_rows = parts[:, tokens:, :PJ].reshape(chips * part, PJ)
    feature_grad = (accept_sum[...] + contract(donor_hot[...], slot_rows, 0, 0)).astype(BF16)
    value = contract(w_query[...], query_grad[...], 0, 1)
    value = value + contract(w_key[...], grads[:, :HD], 0, 1)
    value = value + contract(w_value[...], grads[:, HD:], 0, 1)
    value = value + contract(w_junction[...], feature_grad, 1, 1)
    blocks = value.reshape((2 * kept.shape[0],) + kept.shape[1:])
    kept[...], sent[...] = halve(blocks, lax.axis_index("side"))


def tiles_of(rows, columns, count):
    high, wide = rows * 2 // count, columns // 2
    return [(i, pl.ds(i // 2 * high, high), pl.ds(i % 2 * wide, wide)) for i in range(count)]


def sum_body(parts, total):
    value = parts[0].astype(F32)
    for i in range(1, parts.shape[0]):
        value = value + parts[i].astype(F32)
    total[...] = value.astype(total.dtype)


def cut_body(parts, tiles, whole):
    value = parts[0].astype(F32)
    for i in range(1, parts.shape[0]):
        value = value + parts[i].astype(F32)
    whole[...] = value
    for i, rows, columns in tiles_of(*whole.shape, tiles.shape[0]):
        tiles[i] = whole[rows, columns].astype(BF16)


def spread_body(parts, copies):
    value = parts[0].astype(F32)
    for i in range(1, parts.shape[0]):
        value = value + parts[i].astype(F32)
    value = value.astype(BF16)
    for i in range(copies.shape[0]):
        copies[i] = value


def join_body(tiles, joined, whole):
    for i, rows, columns in tiles_of(*whole.shape, tiles.shape[0]):
        whole[rows, columns] = tiles[i].astype(F32)
    joined[...] = whole[...].astype(BF16)


def place_body(mine, theirs, *refs):
    outs, sems = refs[:-1], refs[-1]
    core = lax.axis_index("core")
    cut = mine.shape[1]
    copies = []
    for i, out in enumerate(outs):
        for j, (source, place) in enumerate(((mine, core), (theirs, 1 - core))):
            columns = pl.ds(pl.multiple_of(place * cut, cut), cut)
            copies.append(
                pltpu.make_async_copy(
                    source.at[pl.ds(i * HD, HD)], out.at[:, columns], sems.at[2 * i + j]
                )
            )
    for copy in copies:
        copy.start()
    for copy in copies:
        copy.wait()


def swap(value, axis="core"):
    return lax.ppermute(value, axis, [(0, 1), (1, 0)])


def exchange(value, axis):
    return lax.all_to_all(value, axis, 0, 0, tiled=True)


def on_device(
    hidden_in,
    ctx_grad,
    w_query,
    w_key,
    w_value,
    w_junction,
    donor_pos,
    acceptor_pos,
    junction_counts,
    pred_grad,
):
    hidden = hidden_in[0]
    tokens, width = hidden.shape
    chips = lax.axis_size("x")
    intervals = lax.axis_size("interval")
    heads = lax.axis_size("pair") * SIDES
    half = chips * tokens
    buckets, per = donor_pos.shape[2:]
    slots = buckets * per
    height = tokens + slots // chips

    message, features, donor_hot = local_call(
        project_body,
        [((chips, height, KV), BF16), ((tokens, PJ), BF16), ((slots, tokens), BF16)],
        operands=8,
        fetched=8,
        scratch=[
            pltpu.VMEM((tokens, width), BF16),
            pltpu.VMEM((KV, width), BF16),
            pltpu.VMEM((width, PJ), BF16),
            pltpu.VMEM((buckets, per), jnp.int32),
            pltpu.VMEM((buckets, per), jnp.int32),
            pltpu.VMEM((1, buckets), jnp.int32),
            pltpu.VMEM((buckets, per), F32),
            pltpu.SemaphoreType.DMA((8,)),
        ],
    )(
        *(
            pltpu.with_memory_space_constraint(value, pltpu.HBM)
            for value in (
                hidden,
                w_key,
                w_value,
                w_junction,
                donor_pos[0, 0],
                acceptor_pos[0, 0],
                junction_counts[0],
                pred_grad[0, 0],
            )
        )
    )
    mine = exchange(message, "x")
    theirs = swap(mine)
    queries, ctx = local_call(query_body, [((tokens, LANES), BF16)] * 2, operands=3)(
        hidden, w_query, ctx_grad[0].T
    )
    terms_theirs, back_mine, accept_sum, probs_b, dscores_b = local_call(
        attend_body,
        [
            ((chips, height, KV), BF16),
            ((chips, height - tokens, PJ), BF16),
            ((tokens, PJ), F32),
            ((CORES, tokens, half), BF16),
            ((CORES, tokens, half), BF16),
        ],
        operands=5,
    )(queries, ctx, features, mine, theirs)
    terms_theirs = swap(terms_theirs)
    terms_mine, query_grad = local_call(
        own_body, [((chips, height, KV), BF16), ((tokens, HD), BF16)], operands=7
    )(queries, ctx, mine, theirs, back_mine, probs_b, dscores_b)
    (pair_sum,) = local_call(total_body, [((chips, height, KV), BF16)], operands=2)(
        terms_mine, terms_theirs
    )
    parts = exchange(pair_sum, "x")
    rows = 3 * HD
    cut = width // CORES
    block = (width // heads, tokens)
    grads, weight_held, weight_sent = local_call(
        grads_body,
        [((tokens, KV), BF16), ((rows, cut), F32), ((rows, cut), BF16)],
        operands=3,
    )(parts, query_grad, hidden)
    held, sent = local_call(
        input_body,
        [((heads // 2,) + block, F32), ((heads // 2,) + block, BF16)],
        operands=9,
    )(
        parts,
        accept_sum,
        donor_hot,
        grads,
        query_grad,
        w_query,
        w_key,
        w_value,
        w_junction,
    )

    weight_got, sent = lax.optimization_barrier((swap(weight_sent), sent))
    (term,) = local_call(total_body, [((rows, cut), BF16)], operands=2)(weight_held, weight_got)
    part = rows // chips
    tile = (part * 2 // intervals, cut // 2)
    (tiles,) = local_call(
        cut_body, [((intervals,) + tile, BF16)], operands=1, scratch=[pltpu.VMEM((part, cut), F32)]
    )(exchange(term.reshape(chips, part, cut), "x"))
    tiles, got = lax.optimization_barrier((tiles, swap(sent, "side")))
    (blocks,) = local_call(total_body, [((heads // SIDES,) + block, BF16)], operands=2)(held, got)
    (copies,) = local_call(spread_body, [((intervals,) + tile, BF16)], operands=1)(
        exchange(tiles, "interval")
    )
    (term,) = local_call(
        join_body, [((part, cut), BF16)], operands=1, scratch=[pltpu.VMEM((part, cut), F32)]
    )(exchange(copies, "interval"))
    blocks = exchange(blocks, "pair")
    term = lax.all_gather(term, "x", axis=0, tiled=True)
    term, blocks = lax.optimization_barrier((term, blocks))
    (grad_input,) = local_call(sum_body, [(block, BF16)], operands=1)(blocks)
    grads = local_call(
        place_body,
        [((HD, width), BF16)] * 3,
        operands=2,
        scratch=[pltpu.SemaphoreType.DMA((2 * 3,))],
        space=pl.ANY,
    )(term, swap(term))
    return (grad_input.T[None],) + tuple(grads)


def solution(mesh):
    axes = (mesh.shape["interval"], mesh.shape["seq"] // CORES, CORES)
    axes += (mesh.shape["head"] // SIDES, SIDES)
    split = Mesh(mesh.devices.reshape(axes), ("interval", "x", "core", "pair", "side"))
    seq, head = ("x", "core"), ("pair", "side")
    placed = (
        P("interval", seq, None),
        P("interval", seq, head),
        P(head, None),
        P(head, None),
        P(head, None),
        P(),
        P("interval", seq, None, head),
        P("interval", seq, None, head),
        P("interval", seq, None),
        P("interval", seq, None, head),
    )
    return jax.shard_map(
        on_device,
        mesh=split,
        in_specs=placed,
        out_specs=(P("interval", seq, head), P(head, None), P(head, None), P(head, None)),
        check_vma=False,
    )
```

```python
import jax
import jax.numpy as jnp
from jax import lax
from jax.experimental import pallas as pl
from jax.experimental.pallas import tpu as pltpu
from jax.sharding import Mesh
from jax.sharding import PartitionSpec as P

HD = 192
PJ = 128
CORES = 2
SIDES = 2
LANES = 256
BAND = 128
KV = 2 * HD
SHIFT = KV - LANES
F32 = jnp.float32
BF16 = jnp.bfloat16
VMEM_BYTES = 20 * 1024 * 1024


def contract(a, b, dim_a, dim_b, precision=None):
    return lax.dot_general(
        a, b, (((dim_a,), (dim_b,)), ((), ())), precision=precision, preferred_element_type=F32
    )


def iota(shape, axis):
    return lax.broadcasted_iota(jnp.int32, shape, axis)


def local_call(body, outs, operands, scratch=(), fetched=0, space=pltpu.VMEM):
    specs = [pl.BlockSpec(memory_space=pltpu.HBM)] * fetched
    specs += [pl.BlockSpec(memory_space=space)] * (operands - fetched)
    return pl.pallas_call(
        body,
        out_shape=tuple(jax.ShapeDtypeStruct(shape, kind) for shape, kind in outs),
        in_specs=specs,
        out_specs=tuple(pl.BlockSpec(memory_space=space) for _ in outs),
        scratch_shapes=list(scratch),
        compiler_params=pltpu.CompilerParams(vmem_limit_bytes=VMEM_BYTES),
    )


def split_terms(term, count=2):
    pieces = []
    for _ in range(count):
        piece = term.astype(BF16)
        pieces.append(piece)
        term = term - piece.astype(F32)
    return pieces


def project_body(
    hidden_hbm,
    w_key_hbm,
    w_value_hbm,
    w_junction_hbm,
    donor_hbm,
    acceptor_hbm,
    counts_hbm,
    pred_hbm,
    message,
    donor_hot,
    hidden,
    weights,
    w_junction,
    donor_pos,
    acceptor_pos,
    counts,
    pred_grad,
    sems,
):
    targets = (
        donor_pos,
        acceptor_pos,
        counts,
        pred_grad,
        hidden,
        weights.at[pl.ds(0, HD)],
        weights.at[pl.ds(HD, HD)],
        w_junction,
    )
    sources = (
        donor_hbm,
        acceptor_hbm,
        counts_hbm,
        pred_hbm,
        hidden_hbm,
        w_key_hbm,
        w_value_hbm,
        w_junction_hbm,
    )
    copies = [
        pltpu.make_async_copy(source, target, sems.at[i])
        for i, (source, target) in enumerate(zip(sources, targets))
    ]
    for copy in copies:
        copy.start()
    for copy in copies[:4]:
        copy.wait()
    chips = message.shape[0]
    tokens = hidden.shape[0]
    buckets, per = donor_pos.shape
    slots = buckets * per
    square = iota((buckets, buckets), 0) == iota((buckets, buckets), 1)
    limit = jnp.sum(
        jnp.where(square, counts[...].astype(F32), 0.0), axis=1, keepdims=True
    )
    head = lax.axis_index("pair") * SIDES + lax.axis_index("side")
    slot_ids = head * per + iota((buckets, per), 1)
    live_grad = jnp.where(slot_ids.astype(F32) < limit, pred_grad[...], 0.0)
    pick_bucket = (iota((slots, buckets), 0) // per == iota((slots, buckets), 1)).astype(F32)
    own_slot = iota((slots, per), 0) % per == iota((slots, per), 1)

    def to_column(value):
        wide = contract(pick_bucket, value.astype(F32), 1, 0, lax.Precision.HIGHEST)
        return jnp.sum(jnp.where(own_slot, wide, 0.0), axis=1, keepdims=True)

    donor = to_column(donor_pos[...])
    hot = jnp.where(iota((slots, tokens), 1).astype(F32) == donor, 1.0, 0.0).astype(BF16)
    donor_hot[...] = hot
    lane = iota((slots, PJ), 1)
    scalars = [to_column(acceptor_pos[...])]
    scalars += [piece.astype(F32) for piece in split_terms(to_column(live_grad), 3)]
    extra = jnp.zeros((slots, PJ), F32)
    for i, column in enumerate(scalars):
        extra = jnp.where(lane == i, column, extra)
    for copy in copies[4:]:
        copy.wait()
    x = hidden[...]
    rows = contract(x, weights[...], 1, 1).astype(BF16)
    feats = contract(x, w_junction[...], 1, 0).astype(BF16)
    slot_rows = jnp.concatenate(
        [
            contract(hot, feats, 1, 0).astype(BF16),
            extra.astype(BF16),
            jnp.zeros((slots, KV - 2 * PJ), BF16),
        ],
        axis=1,
    )
    part = slots // chips
    for chip in range(chips):
        message[chip, :tokens, :] = rows
        message[chip, tokens:, :] = slot_rows[chip * part : (chip + 1) * part, :]


def query_body(hidden, w_query, w_junction, ctx_t, rows):
    tokens = hidden.shape[0]
    pad = jnp.zeros((tokens, LANES - HD), BF16)
    value = contract(hidden[...], w_query[...], 1, 1).astype(BF16)
    rows[:, :LANES] = jnp.concatenate([value, pad], axis=1)
    ctx = jnp.transpose(ctx_t[...].astype(F32)).astype(BF16)
    rows[:, LANES : 2 * LANES] = jnp.concatenate([pad, ctx], axis=1)
    rows[:, 2 * LANES :] = contract(hidden[...], w_junction[...], 1, 0).astype(BF16)


def diagonal(size):
    return iota((size, size), 0) == iota((size, size), 1)


def score_body(own, other, mine, expd, dprobs, stats):
    tokens = own.shape[0]
    half = mine.shape[0] * tokens
    keys = mine[:, :tokens, :].reshape(half, KV)
    square = diagonal(BAND)
    blank = jnp.zeros((8 - 3, BAND), F32)
    for i, rows in enumerate((own, other)):
        for start in range(0, tokens, BAND):
            band = pl.ds(start, BAND)
            score = contract(rows[band, :LANES], keys[:, :LANES], 1, 1) * HD ** (-0.5)
            row_max = jnp.max(score, axis=-1, keepdims=True)
            value = jnp.exp(score - row_max)
            dprob = contract(rows[band, LANES : 2 * LANES], keys[:, SHIFT:], 1, 1)
            expd[i, band, :] = value
            dprobs[i, band, :] = dprob
            columns = (
                row_max,
                jnp.sum(value, axis=-1, keepdims=True),
                jnp.sum(value * dprob, axis=-1, keepdims=True),
            )
            lines = [
                jnp.sum(jnp.where(square, column, 0.0), axis=0, keepdims=True)
                for column in columns
            ]
            stats[i, :, band] = jnp.concatenate(lines + [blank], axis=0)


def slot_body(own, other, mine, back, kept_sum, sent_sum):
    tokens = own.shape[0]
    chips, height, _ = mine.shape
    part = height - tokens
    slots = chips * part
    slot_rows = mine[:, tokens:, :].astype(F32).reshape(slots, KV)
    donor_feat = slot_rows[:, :PJ]
    extra = slot_rows[:, PJ : 2 * PJ]
    acceptor = extra[:, 0:1]
    slot_scale = extra[:, 1:2] + extra[:, 2:3] + extra[:, 3:4]
    shard = iota((slots, 1), 0) % part // (part // CORES)
    here = shard == lax.axis_index("core")
    place = iota((slots, tokens), 1).astype(F32) == acceptor
    hots = [
        jnp.where(place, jnp.where(chosen, 1.0, 0.0), 0.0).astype(BF16)
        for chosen in (here, jnp.logical_not(here))
    ]
    accept_feat = contract(hots[0], own[:, 2 * LANES :], 1, 0) + contract(
        hots[1], other[:, 2 * LANES :], 1, 0
    )
    pair_scale = PJ ** (-0.5)
    pair_score = jnp.sum(donor_feat * accept_feat, axis=-1, keepdims=True) * pair_scale
    slot_grad = slot_scale * jax.nn.sigmoid(pair_score) * pair_scale
    pieces = split_terms(slot_grad * donor_feat)
    for hot, total in zip(hots, (kept_sum, sent_sum)):
        total[...] = contract(hot, pieces[0], 0, 0) + contract(hot, pieces[1], 0, 0)
    back[...] = (slot_grad * accept_feat).astype(BF16).reshape(chips, part, PJ)


def grad_body(
    own, other, mine, expd, dprobs, stats, got, back, sent_sum, terms, kept, sent, probs_b, dscores_b
):
    tokens = own.shape[0]
    chips, height, _ = mine.shape
    part = height - tokens
    half = chips * tokens
    scale = HD ** (-0.5)
    square = diagonal(BAND)
    for i in range(CORES):
        for start in range(0, tokens, BAND):
            band = pl.ds(start, BAND)
            here, there = stats[i, :, band], got[1 - i, :, band]
            top = jnp.maximum(here[0:1], there[0:1])
            near, far = jnp.exp(here[0:1] - top), jnp.exp(there[0:1] - top)
            inverse = 1.0 / (here[1:2] * near + there[1:2] * far)
            delta = (here[2:3] * near + there[2:3] * far) * inverse
            factor, delta = (
                jnp.sum(jnp.where(square, line, 0.0), axis=1, keepdims=True)
                for line in (near * inverse, delta)
            )
            probs = expd[i, band, :] * factor
            rows = pl.ds(i * tokens + start, BAND)
            probs_b[rows, :] = probs.astype(BF16)
            dscores_b[rows, :] = (probs * (dprobs[i, band, :] - delta)).astype(BF16)
    rows = jnp.concatenate([own[:, : 2 * LANES], other[:, : 2 * LANES]], axis=0)
    key_term = contract(dscores_b[...], rows[:, :LANES], 0, 0) * scale
    value_term = contract(probs_b[...], rows[:, LANES:], 0, 0)
    middle = key_term[:, SHIFT:] + value_term[:, :SHIFT]
    for first, value in (
        (0, key_term[:, :SHIFT]),
        (SHIFT, middle),
        (LANES, value_term[:, SHIFT:]),
    ):
        terms[:, :tokens, first : first + SHIFT] = value.astype(BF16).reshape(
            chips, tokens, SHIFT
        )
    terms[:, tokens:, :PJ] = back[...]
    terms[:, tokens:, PJ:] = jnp.zeros((chips, part, KV - PJ), BF16)
    keys = mine[:, :tokens, :LANES].reshape(half, LANES)
    query_term = contract(dscores_b[...], keys, 1, 0) * scale
    kept[...] = query_term[:tokens, :]
    sent[:, :LANES] = query_term[tokens:, :].astype(BF16)
    sent[:, LANES:] = sent_sum[...].astype(BF16)


def halve(value, side):
    blocks = value.reshape((value.shape[0] // 2, 2) + value.shape[1:])
    odd = side == 1
    kept = jnp.where(odd, blocks[:, 1], blocks[:, 0])
    sent = jnp.where(odd, blocks[:, 0], blocks[:, 1])
    return kept, sent.astype(BF16)


def total_body(*refs):
    value = refs[0][...].astype(F32)
    for ref in refs[1:-1]:
        value = value + ref[...].astype(F32)
    refs[-1][...] = value.astype(refs[-1].dtype)


def grads_body(parts, query_held, query_got, hidden, grads, query_grad, kept, sent):
    tokens, width = hidden.shape
    query = query_held[:, :HD] + query_got[:, :HD].astype(F32)
    query_grad[...] = query.astype(BF16)
    total = jnp.zeros((tokens, KV), F32)
    for chip in range(parts.shape[0]):
        total = total + parts[chip, :tokens, :].astype(F32)
    grads[...] = total.astype(BF16)
    core = lax.axis_index("core")
    cut = width // CORES
    first = 0
    for grad in (query_grad[...], grads[...]):
        value = contract(grad, hidden[...], 0, 0)
        rows = pl.ds(first, value.shape[0])
        left, right = value[:, :cut], value[:, cut:]
        kept[rows, :] = jnp.where(core == 0, left, right)
        sent[rows, :] = jnp.where(core == 0, right, left).astype(BF16)
        first += value.shape[0]


def input_body(
    parts,
    kept_sum,
    query_got,
    donor_hot,
    grads,
    query_grad,
    w_query,
    w_key,
    w_value,
    w_junction,
    kept,
    sent,
):
    chips, height, _ = parts.shape
    tokens = grads.shape[0]
    part = height - tokens
    slot_rows = parts[:, tokens:, :PJ].reshape(chips * part, PJ)
    feature_grad = kept_sum[...] + query_got[:, LANES:].astype(F32)
    feature_grad = (feature_grad + contract(donor_hot[...], slot_rows, 0, 0)).astype(BF16)
    value = contract(w_query[...], query_grad[...], 0, 1)
    value = value + contract(w_key[...], grads[:, :HD], 0, 1)
    value = value + contract(w_value[...], grads[:, HD:], 0, 1)
    value = value + contract(w_junction[...], feature_grad, 1, 1)
    blocks = value.reshape((2 * kept.shape[0],) + kept.shape[1:])
    kept[...], sent[...] = halve(blocks, lax.axis_index("side"))


def tiles_of(rows, columns, count):
    high, wide = rows * 2 // count, columns // 2
    return [(i, pl.ds(i // 2 * high, high), pl.ds(i % 2 * wide, wide)) for i in range(count)]


def sum_body(parts, total):
    value = parts[0].astype(F32)
    for i in range(1, parts.shape[0]):
        value = value + parts[i].astype(F32)
    total[...] = value.astype(total.dtype)


def cut_body(parts, tiles, whole):
    value = parts[0].astype(F32)
    for i in range(1, parts.shape[0]):
        value = value + parts[i].astype(F32)
    whole[...] = value
    for i, rows, columns in tiles_of(*whole.shape, tiles.shape[0]):
        tiles[i] = whole[rows, columns].astype(BF16)


def spread_body(parts, copies):
    value = parts[0].astype(F32)
    for i in range(1, parts.shape[0]):
        value = value + parts[i].astype(F32)
    value = value.astype(BF16)
    for i in range(copies.shape[0]):
        copies[i] = value


def join_body(tiles, joined, whole):
    for i, rows, columns in tiles_of(*whole.shape, tiles.shape[0]):
        whole[rows, columns] = tiles[i].astype(F32)
    joined[...] = whole[...].astype(BF16)


def place_body(mine, theirs, *refs):
    outs, sems = refs[:-1], refs[-1]
    core = lax.axis_index("core")
    cut = mine.shape[1]
    copies = []
    for i, out in enumerate(outs):
        for j, (source, place) in enumerate(((mine, core), (theirs, 1 - core))):
            columns = pl.ds(pl.multiple_of(place * cut, cut), cut)
            copies.append(
                pltpu.make_async_copy(
                    source.at[pl.ds(i * HD, HD)], out.at[:, columns], sems.at[2 * i + j]
                )
            )
    for copy in copies:
        copy.start()
    for copy in copies:
        copy.wait()


def swap(value, axis="core"):
    return lax.ppermute(value, axis, [(0, 1), (1, 0)])


def exchange(value, axis):
    return lax.all_to_all(value, axis, 0, 0, tiled=True)


def on_device(
    hidden_in,
    ctx_grad,
    w_query,
    w_key,
    w_value,
    w_junction,
    donor_pos,
    acceptor_pos,
    junction_counts,
    pred_grad,
):
    hidden = hidden_in[0]
    tokens, width = hidden.shape
    chips = lax.axis_size("x")
    intervals = lax.axis_size("interval")
    heads = lax.axis_size("pair") * SIDES
    half = chips * tokens
    buckets, per = donor_pos.shape[2:]
    slots = buckets * per
    height = tokens + slots // chips

    message, donor_hot = local_call(
        project_body,
        [((chips, height, KV), BF16), ((slots, tokens), BF16)],
        operands=8,
        fetched=8,
        scratch=[
            pltpu.VMEM((tokens, width), BF16),
            pltpu.VMEM((KV, width), BF16),
            pltpu.VMEM((width, PJ), BF16),
            pltpu.VMEM((buckets, per), jnp.int32),
            pltpu.VMEM((buckets, per), jnp.int32),
            pltpu.VMEM((1, buckets), jnp.int32),
            pltpu.VMEM((buckets, per), F32),
            pltpu.SemaphoreType.DMA((8,)),
        ],
    )(
        *(
            pltpu.with_memory_space_constraint(value, pltpu.HBM)
            for value in (
                hidden,
                w_key,
                w_value,
                w_junction,
                donor_pos[0, 0],
                acceptor_pos[0, 0],
                junction_counts[0],
                pred_grad[0, 0],
            )
        )
    )
    mine = exchange(message, "x")
    (own,) = local_call(query_body, [((tokens, 2 * LANES + PJ), BF16)], operands=4)(
        hidden, w_query, w_junction, ctx_grad[0].T
    )
    other = swap(own)
    expd, dprobs, stats = local_call(
        score_body,
        [((CORES, tokens, half), F32), ((CORES, tokens, half), F32), ((CORES, 8, tokens), F32)],
        operands=3,
    )(own, other, mine)
    got = swap(stats)
    back, kept_sum, sent_sum = local_call(
        slot_body,
        [((chips, height - tokens, PJ), BF16), ((tokens, PJ), F32), ((tokens, PJ), F32)],
        operands=3,
    )(own, other, mine)
    terms, query_held, query_sent = local_call(
        grad_body,
        [
            ((chips, height, KV), BF16),
            ((tokens, LANES), F32),
            ((tokens, LANES + PJ), BF16),
        ],
        operands=9,
        scratch=[pltpu.VMEM((CORES * tokens, half), BF16)] * 2,
    )(own, other, mine, expd, dprobs, stats, got, back, sent_sum)
    query_got = swap(query_sent)
    parts = exchange(terms, "x")
    parts, query_got = lax.optimization_barrier((parts, query_got))
    rows = 3 * HD
    cut = width // CORES
    block = (width // heads, tokens)
    grads, query_grad, weight_held, weight_sent = local_call(
        grads_body,
        [((tokens, KV), BF16), ((tokens, HD), BF16), ((rows, cut), F32), ((rows, cut), BF16)],
        operands=4,
    )(parts, query_held, query_got, hidden)
    held, sent = local_call(
        input_body,
        [((heads // 2,) + block, F32), ((heads // 2,) + block, BF16)],
        operands=10,
    )(
        parts,
        kept_sum,
        query_got,
        donor_hot,
        grads,
        query_grad,
        w_query,
        w_key,
        w_value,
        w_junction,
    )

    weight_got, sent = lax.optimization_barrier((swap(weight_sent), sent))
    (term,) = local_call(total_body, [((rows, cut), BF16)], operands=2)(weight_held, weight_got)
    part = rows // chips
    tile = (part * 2 // intervals, cut // 2)
    (tiles,) = local_call(
        cut_body, [((intervals,) + tile, BF16)], operands=1, scratch=[pltpu.VMEM((part, cut), F32)]
    )(exchange(term.reshape(chips, part, cut), "x"))
    tiles, got = lax.optimization_barrier((tiles, swap(sent, "side")))
    (blocks,) = local_call(total_body, [((heads // SIDES,) + block, BF16)], operands=2)(held, got)
    (copies,) = local_call(spread_body, [((intervals,) + tile, BF16)], operands=1)(
        exchange(tiles, "interval")
    )
    (term,) = local_call(
        join_body, [((part, cut), BF16)], operands=1, scratch=[pltpu.VMEM((part, cut), F32)]
    )(exchange(copies, "interval"))
    blocks = exchange(blocks, "pair")
    term = lax.all_gather(term, "x", axis=0, tiled=True)
    term, blocks = lax.optimization_barrier((term, blocks))
    (grad_input,) = local_call(sum_body, [(block, BF16)], operands=1)(blocks)
    grads = local_call(
        place_body,
        [((HD, width), BF16)] * 3,
        operands=2,
        scratch=[pltpu.SemaphoreType.DMA((2 * 3,))],
        space=pl.ANY,
    )(term, swap(term))
    return (grad_input.T[None],) + tuple(grads)


def solution(mesh):
    axes = (mesh.shape["interval"], mesh.shape["seq"] // CORES, CORES)
    axes += (mesh.shape["head"] // SIDES, SIDES)
    split = Mesh(mesh.devices.reshape(axes), ("interval", "x", "core", "pair", "side"))
    seq, head = ("x", "core"), ("pair", "side")
    placed = (
        P("interval", seq, None),
        P("interval", seq, head),
        P(head, None),
        P(head, None),
        P(head, None),
        P(),
        P("interval", seq, None, head),
        P("interval", seq, None, head),
        P("interval", seq, None),
        P("interval", seq, None, head),
    )
    return jax.shard_map(
        on_device,
        mesh=split,
        in_specs=placed,
        out_specs=(P("interval", seq, head), P(head, None), P(head, None), P(head, None)),
        check_vma=False,
    )
```

```python
import jax
import jax.numpy as jnp
from jax import lax
from jax.experimental import pallas as pl
from jax.experimental.pallas import tpu as pltpu
from jax.sharding import Mesh
from jax.sharding import PartitionSpec as P

HD = 192
PJ = 128
CORES = 2
SIDES = 2
LANES = 256
BAND = 128
KV = 2 * HD
SHIFT = KV - LANES
F32 = jnp.float32
BF16 = jnp.bfloat16
VMEM_BYTES = 20 * 1024 * 1024


def contract(a, b, dim_a, dim_b, precision=None):
    return lax.dot_general(
        a, b, (((dim_a,), (dim_b,)), ((), ())), precision=precision, preferred_element_type=F32
    )


def iota(shape, axis):
    return lax.broadcasted_iota(jnp.int32, shape, axis)


def local_call(body, outs, operands, scratch=(), fetched=0, space=pltpu.VMEM):
    specs = [pl.BlockSpec(memory_space=pltpu.HBM)] * fetched
    specs += [pl.BlockSpec(memory_space=space)] * (operands - fetched)
    shapes = [
        (pltpu.HBM if len(out) > 2 else jax.ShapeDtypeStruct)(out[0], out[1]) for out in outs
    ]
    return pl.pallas_call(
        body,
        out_shape=tuple(shapes),
        in_specs=specs,
        out_specs=tuple(
            pl.BlockSpec(memory_space=pltpu.HBM if len(out) > 2 else space) for out in outs
        ),
        scratch_shapes=list(scratch),
        compiler_params=pltpu.CompilerParams(vmem_limit_bytes=VMEM_BYTES),
    )


def split_terms(term, count=2):
    pieces = []
    for _ in range(count):
        piece = term.astype(BF16)
        pieces.append(piece)
        term = term - piece.astype(F32)
    return pieces


def project_body(
    hidden_hbm,
    w_key_hbm,
    w_value_hbm,
    w_junction_hbm,
    donor_hbm,
    acceptor_hbm,
    counts_hbm,
    pred_hbm,
    message,
    donor_hot,
    rows,
    slot_rows,
    hidden,
    weights,
    w_junction,
    donor_pos,
    acceptor_pos,
    counts,
    pred_grad,
    sems,
    row_sems,
):
    targets = (
        donor_pos,
        acceptor_pos,
        counts,
        pred_grad,
        hidden,
        weights.at[pl.ds(0, HD)],
        weights.at[pl.ds(HD, HD)],
        w_junction,
    )
    sources = (
        donor_hbm,
        acceptor_hbm,
        counts_hbm,
        pred_hbm,
        hidden_hbm,
        w_key_hbm,
        w_value_hbm,
        w_junction_hbm,
    )
    copies = [
        pltpu.make_async_copy(source, target, sems.at[i])
        for i, (source, target) in enumerate(zip(sources, targets))
    ]
    for copy in copies:
        copy.start()
    for copy in copies[:4]:
        copy.wait()
    chips = message.shape[0]
    tokens = hidden.shape[0]
    buckets, per = donor_pos.shape
    slots = buckets * per
    square = iota((buckets, buckets), 0) == iota((buckets, buckets), 1)
    limit = jnp.sum(
        jnp.where(square, counts[...].astype(F32), 0.0), axis=1, keepdims=True
    )
    head = lax.axis_index("pair") * SIDES + lax.axis_index("side")
    slot_ids = head * per + iota((buckets, per), 1)
    live_grad = jnp.where(slot_ids.astype(F32) < limit, pred_grad[...], 0.0)
    pick_bucket = (iota((slots, buckets), 0) // per == iota((slots, buckets), 1)).astype(F32)
    own_slot = iota((slots, per), 0) % per == iota((slots, per), 1)

    def to_column(value):
        wide = contract(pick_bucket, value.astype(F32), 1, 0, lax.Precision.HIGHEST)
        return jnp.sum(jnp.where(own_slot, wide, 0.0), axis=1, keepdims=True)

    donor = to_column(donor_pos[...])
    hot = jnp.where(iota((slots, tokens), 1).astype(F32) == donor, 1.0, 0.0).astype(BF16)
    donor_hot[...] = hot
    lane = iota((slots, PJ), 1)
    scalars = [to_column(acceptor_pos[...])]
    scalars += [piece.astype(F32) for piece in split_terms(to_column(live_grad), 3)]
    extra = jnp.zeros((slots, PJ), F32)
    for i, column in enumerate(scalars):
        extra = jnp.where(lane == i, column, extra)
    for copy in copies[4:]:
        copy.wait()
    x = hidden[...]
    rows[...] = contract(x, weights[...], 1, 1).astype(BF16)
    part = slots // chips
    leaving = [
        pltpu.make_async_copy(rows, message.at[chip, pl.ds(0, tokens)], row_sems.at[chip])
        for chip in range(chips)
    ]
    for copy in leaving:
        copy.start()
    feats = contract(x, w_junction[...], 1, 0).astype(BF16)
    slot_rows[...] = jnp.concatenate(
        [
            contract(hot, feats, 1, 0).astype(BF16),
            extra.astype(BF16),
            jnp.zeros((slots, KV - 2 * PJ), BF16),
        ],
        axis=1,
    )
    last = [
        pltpu.make_async_copy(
            slot_rows.at[pl.ds(chip * part, part)],
            message.at[chip, pl.ds(tokens, part)],
            row_sems.at[chips + chip],
        )
        for chip in range(chips)
    ]
    for copy in last:
        copy.start()
    for copy in leaving + last:
        copy.wait()


def query_body(hidden, w_query, w_junction, ctx_t, rows):
    tokens = hidden.shape[0]
    pad = jnp.zeros((tokens, LANES - HD), BF16)
    value = contract(hidden[...], w_query[...], 1, 1).astype(BF16)
    rows[:, :LANES] = jnp.concatenate([value, pad], axis=1)
    ctx = jnp.transpose(ctx_t[...].astype(F32)).astype(BF16)
    rows[:, LANES : 2 * LANES] = jnp.concatenate([pad, ctx], axis=1)
    rows[:, 2 * LANES :] = contract(hidden[...], w_junction[...], 1, 0).astype(BF16)


def diagonal(size):
    return iota((size, size), 0) == iota((size, size), 1)


def score_body(own, other, mine, expd, dprobs, stats):
    tokens = own.shape[0]
    half = mine.shape[0] * tokens
    keys = mine[:, :tokens, :].reshape(half, KV)
    square = diagonal(BAND)
    blank = jnp.zeros((8 - 3, BAND), F32)
    for i, rows in enumerate((own, other)):
        for start in range(0, tokens, BAND):
            band = pl.ds(start, BAND)
            score = contract(rows[band, :LANES], keys[:, :LANES], 1, 1) * HD ** (-0.5)
            row_max = jnp.max(score, axis=-1, keepdims=True)
            value = jnp.exp(score - row_max)
            dprob = contract(rows[band, LANES : 2 * LANES], keys[:, SHIFT:], 1, 1)
            expd[i, band, :] = value
            dprobs[i, band, :] = dprob
            columns = (
                row_max,
                jnp.sum(value, axis=-1, keepdims=True),
                jnp.sum(value * dprob, axis=-1, keepdims=True),
            )
            lines = [
                jnp.sum(jnp.where(square, column, 0.0), axis=0, keepdims=True)
                for column in columns
            ]
            stats[i, :, band] = jnp.concatenate(lines + [blank], axis=0)


def slot_body(own, other, mine, back, kept_sum, sent_sum):
    tokens = own.shape[0]
    chips, height, _ = mine.shape
    part = height - tokens
    slots = chips * part
    slot_rows = mine[:, tokens:, :].astype(F32).reshape(slots, KV)
    donor_feat = slot_rows[:, :PJ]
    extra = slot_rows[:, PJ : 2 * PJ]
    acceptor = extra[:, 0:1]
    slot_scale = extra[:, 1:2] + extra[:, 2:3] + extra[:, 3:4]
    shard = iota((slots, 1), 0) % part // (part // CORES)
    here = shard == lax.axis_index("core")
    place = iota((slots, tokens), 1).astype(F32) == acceptor
    hots = [
        jnp.where(place, jnp.where(chosen, 1.0, 0.0), 0.0).astype(BF16)
        for chosen in (here, jnp.logical_not(here))
    ]
    accept_feat = contract(hots[0], own[:, 2 * LANES :], 1, 0) + contract(
        hots[1], other[:, 2 * LANES :], 1, 0
    )
    pair_scale = PJ ** (-0.5)
    pair_score = jnp.sum(donor_feat * accept_feat, axis=-1, keepdims=True) * pair_scale
    slot_grad = slot_scale * jax.nn.sigmoid(pair_score) * pair_scale
    pieces = split_terms(slot_grad * donor_feat)
    for hot, total in zip(hots, (kept_sum, sent_sum)):
        total[...] = contract(hot, pieces[0], 0, 0) + contract(hot, pieces[1], 0, 0)
    back[...] = (slot_grad * accept_feat).astype(BF16).reshape(chips, part, PJ)


def grad_body(
    own,
    other,
    mine,
    expd,
    dprobs,
    stats,
    got,
    back,
    sent_sum,
    terms_out,
    sent_out,
    kept,
    terms,
    sent,
    probs_b,
    dscores_b,
    sems,
):
    tokens = own.shape[0]
    chips, height, _ = mine.shape
    part = height - tokens
    half = chips * tokens
    scale = HD ** (-0.5)
    square = diagonal(BAND)
    for i in range(CORES):
        for start in range(0, tokens, BAND):
            band = pl.ds(start, BAND)
            here, there = stats[i, :, band], got[1 - i, :, band]
            top = jnp.maximum(here[0:1], there[0:1])
            near, far = jnp.exp(here[0:1] - top), jnp.exp(there[0:1] - top)
            inverse = 1.0 / (here[1:2] * near + there[1:2] * far)
            delta = (here[2:3] * near + there[2:3] * far) * inverse
            factor, delta = (
                jnp.sum(jnp.where(square, line, 0.0), axis=1, keepdims=True)
                for line in (near * inverse, delta)
            )
            probs = expd[i, band, :] * factor
            rows = pl.ds(i * tokens + start, BAND)
            probs_b[rows, :] = probs.astype(BF16)
            dscores_b[rows, :] = (probs * (dprobs[i, band, :] - delta)).astype(BF16)
    rows = jnp.concatenate([own[:, : 2 * LANES], other[:, : 2 * LANES]], axis=0)
    key_term = contract(dscores_b[...], rows[:, :LANES], 0, 0) * scale
    value_term = contract(probs_b[...], rows[:, LANES:], 0, 0)
    middle = key_term[:, SHIFT:] + value_term[:, :SHIFT]
    for first, value in (
        (0, key_term[:, :SHIFT]),
        (SHIFT, middle),
        (LANES, value_term[:, SHIFT:]),
    ):
        terms[:, :tokens, first : first + SHIFT] = value.astype(BF16).reshape(
            chips, tokens, SHIFT
        )
    terms[:, tokens:, :PJ] = back[...]
    terms[:, tokens:, PJ:] = jnp.zeros((chips, part, KV - PJ), BF16)
    first = pltpu.make_async_copy(terms, terms_out, sems.at[0])
    first.start()
    keys = mine[:, :tokens, :LANES].reshape(half, LANES)
    query_term = contract(dscores_b[...], keys, 1, 0) * scale
    kept[...] = query_term[:tokens, :]
    sent[:, :LANES] = query_term[tokens:, :].astype(BF16)
    sent[:, LANES:] = sent_sum[...].astype(BF16)
    second = pltpu.make_async_copy(sent, sent_out, sems.at[1])
    second.start()
    first.wait()
    second.wait()


def halve(value, side):
    blocks = value.reshape((value.shape[0] // 2, 2) + value.shape[1:])
    odd = side == 1
    kept = jnp.where(odd, blocks[:, 1], blocks[:, 0])
    sent = jnp.where(odd, blocks[:, 0], blocks[:, 1])
    return kept, sent.astype(BF16)


def total_body(*refs):
    value = refs[0][...].astype(F32)
    for ref in refs[1:-1]:
        value = value + ref[...].astype(F32)
    refs[-1][...] = value.astype(refs[-1].dtype)


def grads_body(parts, query_held, query_got, hidden, grads, query_grad, kept, sent):
    tokens, width = hidden.shape
    query = query_held[:, :HD] + query_got[:, :HD].astype(F32)
    query_grad[...] = query.astype(BF16)
    total = jnp.zeros((tokens, KV), F32)
    for chip in range(parts.shape[0]):
        total = total + parts[chip, :tokens, :].astype(F32)
    grads[...] = total.astype(BF16)
    core = lax.axis_index("core")
    cut = width // CORES
    first = 0
    for grad in (query_grad[...], grads[...]):
        value = contract(grad, hidden[...], 0, 0)
        rows = pl.ds(first, value.shape[0])
        left, right = value[:, :cut], value[:, cut:]
        kept[rows, :] = jnp.where(core == 0, left, right)
        sent[rows, :] = jnp.where(core == 0, right, left).astype(BF16)
        first += value.shape[0]


def input_body(
    w_query_hbm,
    w_key_hbm,
    w_value_hbm,
    w_junction_hbm,
    parts,
    kept_sum,
    query_got,
    donor_hot,
    grads,
    query_grad,
    kept,
    sent,
    w_query,
    w_key,
    w_value,
    w_junction,
    sems,
):
    sources = (w_junction_hbm, w_query_hbm, w_key_hbm, w_value_hbm)
    targets = (w_junction, w_query, w_key, w_value)
    copies = [
        pltpu.make_async_copy(source, target, sems.at[i])
        for i, (source, target) in enumerate(zip(sources, targets))
    ]
    for copy in copies:
        copy.start()
    chips, height, _ = parts.shape
    tokens = grads.shape[0]
    part = height - tokens
    slot_rows = parts[:, tokens:, :PJ].reshape(chips * part, PJ)
    feature_grad = kept_sum[...] + query_got[:, LANES:].astype(F32)
    feature_grad = (feature_grad + contract(donor_hot[...], slot_rows, 0, 0)).astype(BF16)
    for copy in copies:
        copy.wait()
    value = contract(w_query[...], query_grad[...], 0, 1)
    value = value + contract(w_key[...], grads[:, :HD], 0, 1)
    value = value + contract(w_value[...], grads[:, HD:], 0, 1)
    value = value + contract(w_junction[...], feature_grad, 1, 1)
    blocks = value.reshape((2 * kept.shape[0],) + kept.shape[1:])
    kept[...], sent[...] = halve(blocks, lax.axis_index("side"))


def tiles_of(rows, columns, count):
    high, wide = rows * 2 // count, columns // 2
    return [(i, pl.ds(i // 2 * high, high), pl.ds(i % 2 * wide, wide)) for i in range(count)]


def sum_body(parts, total):
    value = parts[0].astype(F32)
    for i in range(1, parts.shape[0]):
        value = value + parts[i].astype(F32)
    total[...] = value.astype(total.dtype)


def cut_body(parts, tiles, whole):
    value = parts[0].astype(F32)
    for i in range(1, parts.shape[0]):
        value = value + parts[i].astype(F32)
    whole[...] = value
    for i, rows, columns in tiles_of(*whole.shape, tiles.shape[0]):
        tiles[i] = whole[rows, columns].astype(BF16)


def spread_body(parts, copies):
    value = parts[0].astype(F32)
    for i in range(1, parts.shape[0]):
        value = value + parts[i].astype(F32)
    value = value.astype(BF16)
    for i in range(copies.shape[0]):
        copies[i] = value


def join_body(tiles, joined, whole):
    for i, rows, columns in tiles_of(*whole.shape, tiles.shape[0]):
        whole[rows, columns] = tiles[i].astype(F32)
    joined[...] = whole[...].astype(BF16)


def place_body(mine, theirs, *refs):
    outs, sems = refs[:-1], refs[-1]
    core = lax.axis_index("core")
    cut = mine.shape[1]
    copies = []
    for i, out in enumerate(outs):
        for j, (source, place) in enumerate(((mine, core), (theirs, 1 - core))):
            columns = pl.ds(pl.multiple_of(place * cut, cut), cut)
            copies.append(
                pltpu.make_async_copy(
                    source.at[pl.ds(i * HD, HD)], out.at[:, columns], sems.at[2 * i + j]
                )
            )
    for copy in copies:
        copy.start()
    for copy in copies:
        copy.wait()


def swap(value, axis="core"):
    return lax.ppermute(value, axis, [(0, 1), (1, 0)])


def in_hbm(*values):
    return [pltpu.with_memory_space_constraint(value, pltpu.HBM) for value in values]


def exchange(value, axis):
    return lax.all_to_all(value, axis, 0, 0, tiled=True)


def on_device(
    hidden_in,
    ctx_grad,
    w_query,
    w_key,
    w_value,
    w_junction,
    donor_pos,
    acceptor_pos,
    junction_counts,
    pred_grad,
):
    hidden = hidden_in[0]
    tokens, width = hidden.shape
    chips = lax.axis_size("x")
    intervals = lax.axis_size("interval")
    heads = lax.axis_size("pair") * SIDES
    half = chips * tokens
    buckets, per = donor_pos.shape[2:]
    slots = buckets * per
    height = tokens + slots // chips

    message, donor_hot = local_call(
        project_body,
        [((chips, height, KV), BF16, True), ((slots, tokens), BF16)],
        operands=8,
        fetched=8,
        scratch=[
            pltpu.VMEM((tokens, KV), BF16),
            pltpu.VMEM((slots, KV), BF16),
            pltpu.VMEM((tokens, width), BF16),
            pltpu.VMEM((KV, width), BF16),
            pltpu.VMEM((width, PJ), BF16),
            pltpu.VMEM((buckets, per), jnp.int32),
            pltpu.VMEM((buckets, per), jnp.int32),
            pltpu.VMEM((1, buckets), jnp.int32),
            pltpu.VMEM((buckets, per), F32),
            pltpu.SemaphoreType.DMA((8,)),
            pltpu.SemaphoreType.DMA((2 * chips,)),
        ],
    )(
        *in_hbm(
            hidden,
            w_key,
            w_value,
            w_junction,
            donor_pos[0, 0],
            acceptor_pos[0, 0],
            junction_counts[0],
            pred_grad[0, 0],
        )
    )
    mine = exchange(message, "x")
    (own,) = local_call(query_body, [((tokens, 2 * LANES + PJ), BF16)], operands=4)(
        hidden, w_query, w_junction, ctx_grad[0].T
    )
    other = swap(own)
    expd, dprobs, stats = local_call(
        score_body,
        [((CORES, tokens, half), F32), ((CORES, tokens, half), F32), ((CORES, 8, tokens), F32)],
        operands=3,
    )(own, other, mine)
    got = swap(stats)
    back, kept_sum, sent_sum = local_call(
        slot_body,
        [((chips, height - tokens, PJ), BF16), ((tokens, PJ), F32), ((tokens, PJ), F32)],
        operands=3,
    )(own, other, mine)
    terms, query_sent, query_held = local_call(
        grad_body,
        [
            ((chips, height, KV), BF16, True),
            ((tokens, LANES + PJ), BF16, True),
            ((tokens, LANES), F32),
        ],
        operands=9,
        scratch=[
            pltpu.VMEM((chips, height, KV), BF16),
            pltpu.VMEM((tokens, LANES + PJ), BF16),
        ]
        + [pltpu.VMEM((CORES * tokens, half), BF16)] * 2
        + [pltpu.SemaphoreType.DMA((2,))],
    )(own, other, mine, expd, dprobs, stats, got, back, sent_sum)
    query_got = swap(query_sent)
    parts = exchange(terms, "x")
    parts, query_got = lax.optimization_barrier((parts, query_got))
    rows = 3 * HD
    cut = width // CORES
    block = (width // heads, tokens)
    grads, query_grad, weight_held, weight_sent = local_call(
        grads_body,
        [((tokens, KV), BF16), ((tokens, HD), BF16), ((rows, cut), F32), ((rows, cut), BF16)],
        operands=4,
    )(parts, query_held, query_got, hidden)
    held, sent = local_call(
        input_body,
        [((heads // 2,) + block, F32), ((heads // 2,) + block, BF16)],
        operands=10,
        fetched=4,
        scratch=[pltpu.VMEM((HD, width), BF16)] * 3
        + [pltpu.VMEM((width, PJ), BF16), pltpu.SemaphoreType.DMA((4,))],
    )(
        *in_hbm(w_query, w_key, w_value, w_junction),
        parts,
        kept_sum,
        query_got,
        donor_hot,
        grads,
        query_grad,
    )

    weight_got, sent = lax.optimization_barrier((swap(weight_sent), sent))
    (term,) = local_call(total_body, [((rows, cut), BF16)], operands=2)(weight_held, weight_got)
    part = rows // chips
    tile = (part * 2 // intervals, cut // 2)
    (tiles,) = local_call(
        cut_body, [((intervals,) + tile, BF16)], operands=1, scratch=[pltpu.VMEM((part, cut), F32)]
    )(exchange(term.reshape(chips, part, cut), "x"))
    tiles, got = lax.optimization_barrier((tiles, swap(sent, "side")))
    (blocks,) = local_call(total_body, [((heads // SIDES,) + block, BF16)], operands=2)(held, got)
    (copies,) = local_call(spread_body, [((intervals,) + tile, BF16)], operands=1)(
        exchange(tiles, "interval")
    )
    (term,) = local_call(
        join_body, [((part, cut), BF16)], operands=1, scratch=[pltpu.VMEM((part, cut), F32)]
    )(exchange(copies, "interval"))
    blocks = exchange(blocks, "pair")
    term = lax.all_gather(term, "x", axis=0, tiled=True)
    term, blocks = lax.optimization_barrier((term, blocks))
    (grad_input,) = local_call(sum_body, [(block, BF16)], operands=1)(blocks)
    grads = local_call(
        place_body,
        [((HD, width), BF16)] * 3,
        operands=2,
        scratch=[pltpu.SemaphoreType.DMA((2 * 3,))],
        space=pl.ANY,
    )(term, swap(term))
    return (grad_input.T[None],) + tuple(grads)


def solution(mesh):
    axes = (mesh.shape["interval"], mesh.shape["seq"] // CORES, CORES)
    axes += (mesh.shape["head"] // SIDES, SIDES)
    split = Mesh(mesh.devices.reshape(axes), ("interval", "x", "core", "pair", "side"))
    seq, head = ("x", "core"), ("pair", "side")
    placed = (
        P("interval", seq, None),
        P("interval", seq, head),
        P(head, None),
        P(head, None),
        P(head, None),
        P(),
        P("interval", seq, None, head),
        P("interval", seq, None, head),
        P("interval", seq, None),
        P("interval", seq, None, head),
    )
    return jax.shard_map(
        on_device,
        mesh=split,
        in_specs=placed,
        out_specs=(P("interval", seq, head), P(head, None), P(head, None), P(head, None)),
        check_vma=False,
    )
```

```python
import jax
import jax.numpy as jnp
from jax import lax
from jax.experimental import pallas as pl
from jax.experimental.pallas import tpu as pltpu
from jax.sharding import Mesh
from jax.sharding import PartitionSpec as P

HD = 192
PJ = 128
CORES = 2
SIDES = 2
LANES = 256
BAND = 128
KV = 2 * HD
SHIFT = KV - LANES
F32 = jnp.float32
BF16 = jnp.bfloat16
VMEM_BYTES = 20 * 1024 * 1024


def contract(a, b, dim_a, dim_b, precision=None):
    return lax.dot_general(
        a, b, (((dim_a,), (dim_b,)), ((), ())), precision=precision, preferred_element_type=F32
    )


def iota(shape, axis):
    return lax.broadcasted_iota(jnp.int32, shape, axis)


def local_call(body, outs, operands, scratch=(), fetched=0, space=pltpu.VMEM, aliases={}):
    specs = [pl.BlockSpec(memory_space=pltpu.HBM)] * fetched
    specs += [pl.BlockSpec(memory_space=space)] * (operands - fetched)
    shapes = [
        (pltpu.HBM if len(out) > 2 else jax.ShapeDtypeStruct)(out[0], out[1]) for out in outs
    ]
    return pl.pallas_call(
        body,
        out_shape=tuple(shapes),
        in_specs=specs,
        out_specs=tuple(
            pl.BlockSpec(memory_space=pltpu.HBM if len(out) > 2 else space) for out in outs
        ),
        scratch_shapes=list(scratch),
        input_output_aliases=dict(aliases),
        compiler_params=pltpu.CompilerParams(vmem_limit_bytes=VMEM_BYTES),
    )


def split_terms(term, count=2):
    pieces = []
    for _ in range(count):
        piece = term.astype(BF16)
        pieces.append(piece)
        term = term - piece.astype(F32)
    return pieces


def project_body(
    hidden_hbm,
    w_key_hbm,
    w_value_hbm,
    w_junction_hbm,
    donor_hbm,
    acceptor_hbm,
    counts_hbm,
    pred_hbm,
    message,
    donor_hot,
    rows,
    slot_rows,
    hidden,
    weights,
    w_junction,
    donor_pos,
    acceptor_pos,
    counts,
    pred_grad,
    sems,
    row_sems,
):
    targets = (
        donor_pos,
        acceptor_pos,
        counts,
        pred_grad,
        hidden,
        weights.at[pl.ds(0, HD)],
        weights.at[pl.ds(HD, HD)],
        w_junction,
    )
    sources = (
        donor_hbm,
        acceptor_hbm,
        counts_hbm,
        pred_hbm,
        hidden_hbm,
        w_key_hbm,
        w_value_hbm,
        w_junction_hbm,
    )
    copies = [
        pltpu.make_async_copy(source, target, sems.at[i])
        for i, (source, target) in enumerate(zip(sources, targets))
    ]
    for copy in copies:
        copy.start()
    for copy in copies[:4]:
        copy.wait()
    chips = message.shape[0]
    tokens = hidden.shape[0]
    buckets, per = donor_pos.shape
    slots = buckets * per
    square = iota((buckets, buckets), 0) == iota((buckets, buckets), 1)
    limit = jnp.sum(
        jnp.where(square, counts[...].astype(F32), 0.0), axis=1, keepdims=True
    )
    head = lax.axis_index("pair") * SIDES + lax.axis_index("side")
    slot_ids = head * per + iota((buckets, per), 1)
    live_grad = jnp.where(slot_ids.astype(F32) < limit, pred_grad[...], 0.0)
    pick_bucket = (iota((slots, buckets), 0) // per == iota((slots, buckets), 1)).astype(F32)
    own_slot = iota((slots, per), 0) % per == iota((slots, per), 1)

    def to_column(value):
        wide = contract(pick_bucket, value.astype(F32), 1, 0, lax.Precision.HIGHEST)
        return jnp.sum(jnp.where(own_slot, wide, 0.0), axis=1, keepdims=True)

    donor = to_column(donor_pos[...])
    hot = jnp.where(iota((slots, tokens), 1).astype(F32) == donor, 1.0, 0.0).astype(BF16)
    donor_hot[...] = hot
    lane = iota((slots, PJ), 1)
    scalars = [to_column(acceptor_pos[...])]
    scalars += [piece.astype(F32) for piece in split_terms(to_column(live_grad), 3)]
    extra = jnp.zeros((slots, PJ), F32)
    for i, column in enumerate(scalars):
        extra = jnp.where(lane == i, column, extra)
    for copy in copies[4:]:
        copy.wait()
    x = hidden[...]
    rows[...] = contract(x, weights[...], 1, 1).astype(BF16)
    part = slots // chips
    leaving = [
        pltpu.make_async_copy(rows, message.at[chip, pl.ds(0, tokens)], row_sems.at[chip])
        for chip in range(chips)
    ]
    for copy in leaving:
        copy.start()
    feats = contract(x, w_junction[...], 1, 0).astype(BF16)
    slot_rows[...] = jnp.concatenate(
        [
            contract(hot, feats, 1, 0).astype(BF16),
            extra.astype(BF16),
            jnp.zeros((slots, KV - 2 * PJ), BF16),
        ],
        axis=1,
    )
    last = [
        pltpu.make_async_copy(
            slot_rows.at[pl.ds(chip * part, part)],
            message.at[chip, pl.ds(tokens, part)],
            row_sems.at[chips + chip],
        )
        for chip in range(chips)
    ]
    for copy in last:
        copy.start()
    for copy in leaving + last:
        copy.wait()


def query_body(hidden, w_query, w_junction, ctx_t, rows):
    tokens = hidden.shape[0]
    pad = jnp.zeros((tokens, LANES - HD), BF16)
    value = contract(hidden[...], w_query[...], 1, 1).astype(BF16)
    rows[:, :LANES] = jnp.concatenate([value, pad], axis=1)
    ctx = jnp.transpose(ctx_t[...].astype(F32)).astype(BF16)
    rows[:, LANES : 2 * LANES] = jnp.concatenate([pad, ctx], axis=1)
    rows[:, 2 * LANES :] = contract(hidden[...], w_junction[...], 1, 0).astype(BF16)


def diagonal(size):
    return iota((size, size), 0) == iota((size, size), 1)


def score_body(own, other, mine, expd, dprobs, stats):
    tokens = own.shape[0]
    half = mine.shape[0] * tokens
    keys = mine[:, :tokens, :].reshape(half, KV)
    square = diagonal(BAND)
    blank = jnp.zeros((8 - 3, BAND), F32)
    for i, rows in enumerate((own, other)):
        for start in range(0, tokens, BAND):
            band = pl.ds(start, BAND)
            score = contract(rows[band, :LANES], keys[:, :LANES], 1, 1) * HD ** (-0.5)
            row_max = jnp.max(score, axis=-1, keepdims=True)
            value = jnp.exp(score - row_max)
            dprob = contract(rows[band, LANES : 2 * LANES], keys[:, SHIFT:], 1, 1)
            expd[i, band, :] = value
            dprobs[i, band, :] = dprob
            columns = (
                row_max,
                jnp.sum(value, axis=-1, keepdims=True),
                jnp.sum(value * dprob, axis=-1, keepdims=True),
            )
            lines = [
                jnp.sum(jnp.where(square, column, 0.0), axis=0, keepdims=True)
                for column in columns
            ]
            stats[i, :, band] = jnp.concatenate(lines + [blank], axis=0)


def slot_body(own, other, mine, back, kept_sum, sent_sum):
    tokens = own.shape[0]
    chips, height, _ = mine.shape
    part = height - tokens
    slots = chips * part
    slot_rows = mine[:, tokens:, :].astype(F32).reshape(slots, KV)
    donor_feat = slot_rows[:, :PJ]
    extra = slot_rows[:, PJ : 2 * PJ]
    acceptor = extra[:, 0:1]
    slot_scale = extra[:, 1:2] + extra[:, 2:3] + extra[:, 3:4]
    shard = iota((slots, 1), 0) % part // (part // CORES)
    here = shard == lax.axis_index("core")
    place = iota((slots, tokens), 1).astype(F32) == acceptor
    hots = [
        jnp.where(place, jnp.where(chosen, 1.0, 0.0), 0.0).astype(BF16)
        for chosen in (here, jnp.logical_not(here))
    ]
    accept_feat = contract(hots[0], own[:, 2 * LANES :], 1, 0) + contract(
        hots[1], other[:, 2 * LANES :], 1, 0
    )
    pair_scale = PJ ** (-0.5)
    pair_score = jnp.sum(donor_feat * accept_feat, axis=-1, keepdims=True) * pair_scale
    slot_grad = slot_scale * jax.nn.sigmoid(pair_score) * pair_scale
    pieces = split_terms(slot_grad * donor_feat)
    for hot, total in zip(hots, (kept_sum, sent_sum)):
        total[...] = contract(hot, pieces[0], 0, 0) + contract(hot, pieces[1], 0, 0)
    back[...] = (slot_grad * accept_feat).astype(BF16).reshape(chips, part, PJ)


def grad_body(
    own,
    other,
    mine,
    expd,
    dprobs,
    stats,
    got,
    back,
    sent_sum,
    terms_out,
    sent_out,
    kept,
    terms,
    sent,
    probs_b,
    dscores_b,
    sems,
):
    tokens = own.shape[0]
    chips, height, _ = mine.shape
    part = height - tokens
    half = chips * tokens
    scale = HD ** (-0.5)
    square = diagonal(BAND)
    for i in range(CORES):
        for start in range(0, tokens, BAND):
            band = pl.ds(start, BAND)
            here, there = stats[i, :, band], got[1 - i, :, band]
            top = jnp.maximum(here[0:1], there[0:1])
            near, far = jnp.exp(here[0:1] - top), jnp.exp(there[0:1] - top)
            inverse = 1.0 / (here[1:2] * near + there[1:2] * far)
            delta = (here[2:3] * near + there[2:3] * far) * inverse
            factor, delta = (
                jnp.sum(jnp.where(square, line, 0.0), axis=1, keepdims=True)
                for line in (near * inverse, delta)
            )
            probs = expd[i, band, :] * factor
            rows = pl.ds(i * tokens + start, BAND)
            probs_b[rows, :] = probs.astype(BF16)
            dscores_b[rows, :] = (probs * (dprobs[i, band, :] - delta)).astype(BF16)
    rows = jnp.concatenate([own[:, : 2 * LANES], other[:, : 2 * LANES]], axis=0)
    key_term = contract(dscores_b[...], rows[:, :LANES], 0, 0) * scale
    value_term = contract(probs_b[...], rows[:, LANES:], 0, 0)
    middle = key_term[:, SHIFT:] + value_term[:, :SHIFT]
    for first, value in (
        (0, key_term[:, :SHIFT]),
        (SHIFT, middle),
        (LANES, value_term[:, SHIFT:]),
    ):
        terms[:, :tokens, first : first + SHIFT] = value.astype(BF16).reshape(
            chips, tokens, SHIFT
        )
    terms[:, tokens:, :PJ] = back[...]
    terms[:, tokens:, PJ:] = jnp.zeros((chips, part, KV - PJ), BF16)
    first = pltpu.make_async_copy(terms, terms_out, sems.at[0])
    first.start()
    keys = mine[:, :tokens, :LANES].reshape(half, LANES)
    query_term = contract(dscores_b[...], keys, 1, 0) * scale
    kept[...] = query_term[:tokens, :]
    sent[:, :LANES] = query_term[tokens:, :].astype(BF16)
    sent[:, LANES:] = sent_sum[...].astype(BF16)
    second = pltpu.make_async_copy(sent, sent_out, sems.at[1])
    second.start()
    first.wait()
    second.wait()


def halve(value, side):
    blocks = value.reshape((value.shape[0] // 2, 2) + value.shape[1:])
    odd = side == 1
    kept = jnp.where(odd, blocks[:, 1], blocks[:, 0])
    sent = jnp.where(odd, blocks[:, 0], blocks[:, 1])
    return kept, sent.astype(BF16)


def total_body(*refs):
    value = refs[0][...].astype(F32)
    for ref in refs[1:-1]:
        value = value + ref[...].astype(F32)
    refs[-1][...] = value.astype(refs[-1].dtype)


def grads_body(parts, query_held, query_got, hidden, grads, query_grad, kept, sent):
    tokens, width = hidden.shape
    query = query_held[:, :HD] + query_got[:, :HD].astype(F32)
    query_grad[...] = query.astype(BF16)
    total = jnp.zeros((tokens, KV), F32)
    for chip in range(parts.shape[0]):
        total = total + parts[chip, :tokens, :].astype(F32)
    grads[...] = total.astype(BF16)
    core = lax.axis_index("core")
    cut = width // CORES
    first = 0
    for grad in (query_grad[...], grads[...]):
        value = contract(grad, hidden[...], 0, 0)
        rows = pl.ds(first, value.shape[0])
        left, right = value[:, :cut], value[:, cut:]
        kept[rows, :] = jnp.where(core == 0, left, right).astype(BF16)
        sent[rows, :] = jnp.where(core == 0, right, left).astype(BF16)
        first += value.shape[0]


def input_body(
    w_query_hbm,
    w_key_hbm,
    w_value_hbm,
    w_junction_hbm,
    parts,
    kept_sum,
    query_got,
    donor_hot,
    grads,
    query_grad,
    kept,
    sent,
    w_query,
    w_key,
    w_value,
    w_junction,
    sems,
):
    sources = (w_junction_hbm, w_query_hbm, w_key_hbm, w_value_hbm)
    targets = (w_junction, w_query, w_key, w_value)
    copies = [
        pltpu.make_async_copy(source, target, sems.at[i])
        for i, (source, target) in enumerate(zip(sources, targets))
    ]
    for copy in copies:
        copy.start()
    chips, height, _ = parts.shape
    tokens = grads.shape[0]
    part = height - tokens
    slot_rows = parts[:, tokens:, :PJ].reshape(chips * part, PJ)
    feature_grad = kept_sum[...] + query_got[:, LANES:].astype(F32)
    feature_grad = (feature_grad + contract(donor_hot[...], slot_rows, 0, 0)).astype(BF16)
    copies[0].wait()
    value = contract(w_junction[...], feature_grad, 1, 1)
    copies[1].wait()
    value = value + contract(w_query[...], query_grad[...], 0, 1)
    copies[2].wait()
    value = value + contract(w_key[...], grads[:, :HD], 0, 1)
    copies[3].wait()
    value = value + contract(w_value[...], grads[:, HD:], 0, 1)
    blocks = value.reshape((2 * kept.shape[0],) + kept.shape[1:])
    kept[...], sent[...] = halve(blocks, lax.axis_index("side"))


def tiles_of(rows, columns, count):
    high, wide = rows * 2 // count, columns // 2
    return [(i, pl.ds(i // 2 * high, high), pl.ds(i % 2 * wide, wide)) for i in range(count)]


def pair_body(held, got, out, total, sems):
    chips, part, _ = total.shape
    copies = []
    for chip in range(chips):
        rows = pl.ds(chip * part, part)
        value = held[rows, :].astype(F32) + got[rows, :].astype(F32)
        total[chip] = value.astype(BF16)
        copy = pltpu.make_async_copy(total.at[chip], out.at[chip], sems.at[chip])
        copy.start()
        copies.append(copy)
    for copy in copies:
        copy.wait()


def sum_body(parts, total):
    value = parts[0].astype(F32)
    for i in range(1, parts.shape[0]):
        value = value + parts[i].astype(F32)
    total[...] = value.astype(total.dtype)


def cut_body(parts, tiles, whole):
    value = parts[0].astype(F32)
    for i in range(1, parts.shape[0]):
        value = value + parts[i].astype(F32)
    whole[...] = value
    for i, rows, columns in tiles_of(*whole.shape, tiles.shape[0]):
        tiles[i] = whole[rows, columns].astype(BF16)


def spread_body(parts, copies):
    value = parts[0].astype(F32)
    for i in range(1, parts.shape[0]):
        value = value + parts[i].astype(F32)
    value = value.astype(BF16)
    for i in range(copies.shape[0]):
        copies[i] = value


def join_body(tiles, joined, whole):
    for i, rows, columns in tiles_of(*whole.shape, tiles.shape[0]):
        whole[rows, columns] = tiles[i].astype(F32)
    joined[...] = whole[...].astype(BF16)


def place(source, outs, sems, core):
    cut = source.shape[1]
    columns = pl.ds(pl.multiple_of(core * cut, cut), cut)
    copies = [
        pltpu.make_async_copy(source.at[pl.ds(i * HD, HD)], out.at[:, columns], sems.at[i])
        for i, out in enumerate(outs)
    ]
    for copy in copies:
        copy.start()
    for copy in copies:
        copy.wait()


def own_half_body(mine, *refs):
    place(mine, refs[:3], refs[3], lax.axis_index("core"))


def other_half_body(theirs, *refs):
    place(theirs, refs[3:6], refs[6], 1 - lax.axis_index("core"))


def swap(value, axis="core"):
    return lax.ppermute(value, axis, [(0, 1), (1, 0)])


def in_hbm(*values):
    return [pltpu.with_memory_space_constraint(value, pltpu.HBM) for value in values]


def exchange(value, axis):
    return lax.all_to_all(value, axis, 0, 0, tiled=True)


def on_device(
    hidden_in,
    ctx_grad,
    w_query,
    w_key,
    w_value,
    w_junction,
    donor_pos,
    acceptor_pos,
    junction_counts,
    pred_grad,
):
    hidden = hidden_in[0]
    tokens, width = hidden.shape
    chips = lax.axis_size("x")
    intervals = lax.axis_size("interval")
    heads = lax.axis_size("pair") * SIDES
    half = chips * tokens
    buckets, per = donor_pos.shape[2:]
    slots = buckets * per
    height = tokens + slots // chips

    message, donor_hot = local_call(
        project_body,
        [((chips, height, KV), BF16, True), ((slots, tokens), BF16)],
        operands=8,
        fetched=8,
        scratch=[
            pltpu.VMEM((tokens, KV), BF16),
            pltpu.VMEM((slots, KV), BF16),
            pltpu.VMEM((tokens, width), BF16),
            pltpu.VMEM((KV, width), BF16),
            pltpu.VMEM((width, PJ), BF16),
            pltpu.VMEM((buckets, per), jnp.int32),
            pltpu.VMEM((buckets, per), jnp.int32),
            pltpu.VMEM((1, buckets), jnp.int32),
            pltpu.VMEM((buckets, per), F32),
            pltpu.SemaphoreType.DMA((8,)),
            pltpu.SemaphoreType.DMA((2 * chips,)),
        ],
    )(
        *in_hbm(
            hidden,
            w_key,
            w_value,
            w_junction,
            donor_pos[0, 0],
            acceptor_pos[0, 0],
            junction_counts[0],
            pred_grad[0, 0],
        )
    )
    mine = exchange(message, "x")
    (own,) = local_call(query_body, [((tokens, 2 * LANES + PJ), BF16)], operands=4)(
        hidden, w_query, w_junction, ctx_grad[0].T
    )
    other = swap(own)
    expd, dprobs, stats = local_call(
        score_body,
        [((CORES, tokens, half), F32), ((CORES, tokens, half), F32), ((CORES, 8, tokens), F32)],
        operands=3,
    )(own, other, mine)
    got = swap(stats)
    back, kept_sum, sent_sum = local_call(
        slot_body,
        [((chips, height - tokens, PJ), BF16), ((tokens, PJ), F32), ((tokens, PJ), F32)],
        operands=3,
    )(own, other, mine)
    terms, query_sent, query_held = local_call(
        grad_body,
        [
            ((chips, height, KV), BF16, True),
            ((tokens, LANES + PJ), BF16, True),
            ((tokens, LANES), F32),
        ],
        operands=9,
        scratch=[
            pltpu.VMEM((chips, height, KV), BF16),
            pltpu.VMEM((tokens, LANES + PJ), BF16),
        ]
        + [pltpu.VMEM((CORES * tokens, half), BF16)] * 2
        + [pltpu.SemaphoreType.DMA((2,))],
    )(own, other, mine, expd, dprobs, stats, got, back, sent_sum)
    query_got = swap(query_sent)
    parts = exchange(terms, "x")
    parts, query_got = lax.optimization_barrier((parts, query_got))
    rows = 3 * HD
    cut = width // CORES
    block = (width // heads, tokens)
    grads, query_grad, weight_held, weight_sent = local_call(
        grads_body,
        [((tokens, KV), BF16), ((tokens, HD), BF16), ((rows, cut), BF16), ((rows, cut), BF16)],
        operands=4,
    )(parts, query_held, query_got, hidden)
    held, sent = local_call(
        input_body,
        [((heads // 2,) + block, F32), ((heads // 2,) + block, BF16)],
        operands=10,
        fetched=4,
        scratch=[pltpu.VMEM((HD, width), BF16)] * 3
        + [pltpu.VMEM((width, PJ), BF16), pltpu.SemaphoreType.DMA((4,))],
    )(
        *in_hbm(w_query, w_key, w_value, w_junction),
        parts,
        kept_sum,
        query_got,
        donor_hot,
        grads,
        query_grad,
    )

    weight_got, sent = lax.optimization_barrier((swap(weight_sent), sent))
    part = rows // chips
    (term,) = local_call(
        pair_body,
        [((chips, part, cut), BF16, True)],
        operands=2,
        scratch=[pltpu.VMEM((chips, part, cut), BF16), pltpu.SemaphoreType.DMA((chips,))],
    )(weight_held, weight_got)
    tile = (part * 2 // intervals, cut // 2)
    (tiles,) = local_call(
        cut_body, [((intervals,) + tile, BF16)], operands=1, scratch=[pltpu.VMEM((part, cut), F32)]
    )(exchange(term, "x"))
    tiles, got = lax.optimization_barrier((tiles, swap(sent, "side")))
    (blocks,) = local_call(total_body, [((heads // SIDES,) + block, BF16)], operands=2)(held, got)
    (copies,) = local_call(spread_body, [((intervals,) + tile, BF16)], operands=1)(
        exchange(tiles, "interval")
    )
    (term,) = local_call(
        join_body, [((part, cut), BF16)], operands=1, scratch=[pltpu.VMEM((part, cut), F32)]
    )(exchange(copies, "interval"))
    blocks = exchange(blocks, "pair")
    term = lax.all_gather(term, "x", axis=0, tiled=True)
    term, blocks = lax.optimization_barrier((term, blocks))
    (grad_input,) = local_call(sum_body, [(block, BF16)], operands=1)(blocks)
    wide = [((HD, width), BF16)] * 3
    sems = [pltpu.SemaphoreType.DMA((3,))]
    theirs = swap(term)
    grads = local_call(own_half_body, wide, operands=1, scratch=sems, space=pl.ANY)(term)
    grads = local_call(
        other_half_body,
        wide,
        operands=4,
        scratch=sems,
        space=pl.ANY,
        aliases={i + 1: i for i in range(3)},
    )(theirs, *grads)
    return (grad_input.T[None],) + tuple(grads)


def solution(mesh):
    axes = (mesh.shape["interval"], mesh.shape["seq"] // CORES, CORES)
    axes += (mesh.shape["head"] // SIDES, SIDES)
    split = Mesh(mesh.devices.reshape(axes), ("interval", "x", "core", "pair", "side"))
    seq, head = ("x", "core"), ("pair", "side")
    placed = (
        P("interval", seq, None),
        P("interval", seq, head),
        P(head, None),
        P(head, None),
        P(head, None),
        P(),
        P("interval", seq, None, head),
        P("interval", seq, None, head),
        P("interval", seq, None),
        P("interval", seq, None, head),
    )
    return jax.shard_map(
        on_device,
        mesh=split,
        in_specs=placed,
        out_specs=(P("interval", seq, head), P(head, None), P(head, None), P(head, None)),
        check_vma=False,
    )
```

```python
import jax
import jax.numpy as jnp
from jax import lax
from jax.experimental import pallas as pl
from jax.experimental.pallas import tpu as pltpu
from jax.sharding import Mesh
from jax.sharding import PartitionSpec as P

HD = 192
PJ = 128
CORES = 2
SIDES = 2
LANES = 256
BAND = 128
KV = 2 * HD
SHIFT = KV - LANES
F32 = jnp.float32
BF16 = jnp.bfloat16
VMEM_BYTES = 20 * 1024 * 1024


def contract(a, b, dim_a, dim_b, precision=None):
    return lax.dot_general(
        a, b, (((dim_a,), (dim_b,)), ((), ())), precision=precision, preferred_element_type=F32
    )


def iota(shape, axis):
    return lax.broadcasted_iota(jnp.int32, shape, axis)


def local_call(body, outs, operands, scratch=(), fetched=0, space=pltpu.VMEM, aliases={}):
    specs = [pl.BlockSpec(memory_space=pltpu.HBM)] * fetched
    specs += [pl.BlockSpec(memory_space=space)] * (operands - fetched)
    shapes = [
        (pltpu.HBM if len(out) > 2 else jax.ShapeDtypeStruct)(out[0], out[1]) for out in outs
    ]
    return pl.pallas_call(
        body,
        out_shape=tuple(shapes),
        in_specs=specs,
        out_specs=tuple(
            pl.BlockSpec(memory_space=pltpu.HBM if len(out) > 2 else space) for out in outs
        ),
        scratch_shapes=list(scratch),
        input_output_aliases=dict(aliases),
        compiler_params=pltpu.CompilerParams(vmem_limit_bytes=VMEM_BYTES),
    )


def split_terms(term, count=2):
    pieces = []
    for _ in range(count):
        piece = term.astype(BF16)
        pieces.append(piece)
        term = term - piece.astype(F32)
    return pieces


def project_body(
    hidden_hbm,
    w_key_hbm,
    w_value_hbm,
    w_junction_hbm,
    donor_hbm,
    acceptor_hbm,
    counts_hbm,
    pred_hbm,
    message,
    donor_hot,
    rows,
    slot_rows,
    hidden,
    weights,
    w_junction,
    donor_pos,
    acceptor_pos,
    counts,
    pred_grad,
    sems,
    row_sems,
):
    targets = (
        donor_pos,
        acceptor_pos,
        counts,
        pred_grad,
        hidden,
        weights.at[pl.ds(0, HD)],
        weights.at[pl.ds(HD, HD)],
        w_junction,
    )
    sources = (
        donor_hbm,
        acceptor_hbm,
        counts_hbm,
        pred_hbm,
        hidden_hbm,
        w_key_hbm,
        w_value_hbm,
        w_junction_hbm,
    )
    copies = [
        pltpu.make_async_copy(source, target, sems.at[i])
        for i, (source, target) in enumerate(zip(sources, targets))
    ]
    for copy in copies:
        copy.start()
    for copy in copies[:4]:
        copy.wait()
    chips = message.shape[0]
    tokens = hidden.shape[0]
    buckets, per = donor_pos.shape
    slots = buckets * per
    square = iota((buckets, buckets), 0) == iota((buckets, buckets), 1)
    limit = jnp.sum(
        jnp.where(square, counts[...].astype(F32), 0.0), axis=1, keepdims=True
    )
    head = lax.axis_index("pair") * SIDES + lax.axis_index("side")
    slot_ids = head * per + iota((buckets, per), 1)
    live_grad = jnp.where(slot_ids.astype(F32) < limit, pred_grad[...], 0.0)
    pick_bucket = (iota((slots, buckets), 0) // per == iota((slots, buckets), 1)).astype(F32)
    own_slot = iota((slots, per), 0) % per == iota((slots, per), 1)

    def to_column(value):
        wide = contract(pick_bucket, value.astype(F32), 1, 0, lax.Precision.HIGHEST)
        return jnp.sum(jnp.where(own_slot, wide, 0.0), axis=1, keepdims=True)

    donor = to_column(donor_pos[...])
    hot = jnp.where(iota((slots, tokens), 1).astype(F32) == donor, 1.0, 0.0).astype(BF16)
    donor_hot[...] = hot
    lane = iota((slots, PJ), 1)
    scalars = [to_column(acceptor_pos[...])]
    scalars += [piece.astype(F32) for piece in split_terms(to_column(live_grad), 3)]
    extra = jnp.zeros((slots, PJ), F32)
    for i, column in enumerate(scalars):
        extra = jnp.where(lane == i, column, extra)
    for copy in copies[4:]:
        copy.wait()
    x = hidden[...]
    rows[...] = contract(x, weights[...], 1, 1).astype(BF16)
    part = slots // chips
    leaving = [
        pltpu.make_async_copy(rows, message.at[chip, pl.ds(0, tokens)], row_sems.at[chip])
        for chip in range(chips)
    ]
    for copy in leaving:
        copy.start()
    feats = contract(x, w_junction[...], 1, 0).astype(BF16)
    slot_rows[...] = jnp.concatenate(
        [
            contract(hot, feats, 1, 0).astype(BF16),
            extra.astype(BF16),
            jnp.zeros((slots, KV - 2 * PJ), BF16),
        ],
        axis=1,
    )
    last = [
        pltpu.make_async_copy(
            slot_rows.at[pl.ds(chip * part, part)],
            message.at[chip, pl.ds(tokens, part)],
            row_sems.at[chips + chip],
        )
        for chip in range(chips)
    ]
    for copy in last:
        copy.start()
    for copy in leaving + last:
        copy.wait()


def query_body(hidden, w_query, w_junction, ctx_t, rows):
    tokens = hidden.shape[0]
    pad = jnp.zeros((tokens, LANES - HD), BF16)
    value = contract(hidden[...], w_query[...], 1, 1).astype(BF16)
    rows[:, :LANES] = jnp.concatenate([value, pad], axis=1)
    ctx = jnp.transpose(ctx_t[...].astype(F32)).astype(BF16)
    rows[:, LANES : 2 * LANES] = jnp.concatenate([pad, ctx], axis=1)
    rows[:, 2 * LANES :] = contract(hidden[...], w_junction[...], 1, 0).astype(BF16)


def diagonal(size):
    return iota((size, size), 0) == iota((size, size), 1)


def score_body(own, other, mine, expd, dprobs, stats):
    tokens = own.shape[0]
    half = mine.shape[0] * tokens
    keys = mine[:, :tokens, :].reshape(half, KV)
    square = diagonal(BAND)
    blank = jnp.zeros((8 - 3, BAND), F32)
    for i, rows in enumerate((own, other)):
        for start in range(0, tokens, BAND):
            band = pl.ds(start, BAND)
            score = contract(rows[band, :LANES], keys[:, :LANES], 1, 1) * HD ** (-0.5)
            row_max = jnp.max(score, axis=-1, keepdims=True)
            value = jnp.exp(score - row_max)
            dprob = contract(rows[band, LANES : 2 * LANES], keys[:, SHIFT:], 1, 1)
            expd[i, band, :] = value
            dprobs[i, band, :] = dprob
            columns = (
                row_max,
                jnp.sum(value, axis=-1, keepdims=True),
                jnp.sum(value * dprob, axis=-1, keepdims=True),
            )
            lines = [
                jnp.sum(jnp.where(square, column, 0.0), axis=0, keepdims=True)
                for column in columns
            ]
            stats[i, :, band] = jnp.concatenate(lines + [blank], axis=0)


def slot_body(own, other, mine, back, kept_sum, sent_sum):
    tokens = own.shape[0]
    chips, height, _ = mine.shape
    part = height - tokens
    slots = chips * part
    slot_rows = mine[:, tokens:, :].astype(F32).reshape(slots, KV)
    donor_feat = slot_rows[:, :PJ]
    extra = slot_rows[:, PJ : 2 * PJ]
    acceptor = extra[:, 0:1]
    slot_scale = extra[:, 1:2] + extra[:, 2:3] + extra[:, 3:4]
    shard = iota((slots, 1), 0) % part // (part // CORES)
    here = shard == lax.axis_index("core")
    place = iota((slots, tokens), 1).astype(F32) == acceptor
    hots = [
        jnp.where(place, jnp.where(chosen, 1.0, 0.0), 0.0).astype(BF16)
        for chosen in (here, jnp.logical_not(here))
    ]
    accept_feat = contract(hots[0], own[:, 2 * LANES :], 1, 0) + contract(
        hots[1], other[:, 2 * LANES :], 1, 0
    )
    pair_scale = PJ ** (-0.5)
    pair_score = jnp.sum(donor_feat * accept_feat, axis=-1, keepdims=True) * pair_scale
    slot_grad = slot_scale * jax.nn.sigmoid(pair_score) * pair_scale
    pieces = split_terms(slot_grad * donor_feat)
    for hot, total in zip(hots, (kept_sum, sent_sum)):
        total[...] = contract(hot, pieces[0], 0, 0) + contract(hot, pieces[1], 0, 0)
    back[...] = (slot_grad * accept_feat).astype(BF16).reshape(chips, part, PJ)


def grad_body(
    own,
    other,
    mine,
    expd,
    dprobs,
    stats,
    got,
    back,
    sent_sum,
    terms_out,
    sent_out,
    kept,
    terms,
    sent,
    probs_b,
    dscores_b,
    sems,
):
    tokens = own.shape[0]
    chips, height, _ = mine.shape
    part = height - tokens
    half = chips * tokens
    scale = HD ** (-0.5)
    square = diagonal(BAND)
    for i in range(CORES):
        for start in range(0, tokens, BAND):
            band = pl.ds(start, BAND)
            here, there = stats[i, :, band], got[1 - i, :, band]
            top = jnp.maximum(here[0:1], there[0:1])
            near, far = jnp.exp(here[0:1] - top), jnp.exp(there[0:1] - top)
            inverse = 1.0 / (here[1:2] * near + there[1:2] * far)
            delta = (here[2:3] * near + there[2:3] * far) * inverse
            factor, delta = (
                jnp.sum(jnp.where(square, line, 0.0), axis=1, keepdims=True)
                for line in (near * inverse, delta)
            )
            probs = expd[i, band, :] * factor
            rows = pl.ds(i * tokens + start, BAND)
            probs_b[rows, :] = probs.astype(BF16)
            dscores_b[rows, :] = (probs * (dprobs[i, band, :] - delta)).astype(BF16)
    rows = jnp.concatenate([own[:, : 2 * LANES], other[:, : 2 * LANES]], axis=0)
    key_term = contract(dscores_b[...], rows[:, :LANES], 0, 0) * scale
    value_term = contract(probs_b[...], rows[:, LANES:], 0, 0)
    middle = key_term[:, SHIFT:] + value_term[:, :SHIFT]
    for first, value in (
        (0, key_term[:, :SHIFT]),
        (SHIFT, middle),
        (LANES, value_term[:, SHIFT:]),
    ):
        terms[:, :tokens, first : first + SHIFT] = value.astype(BF16).reshape(
            chips, tokens, SHIFT
        )
    terms[:, tokens:, :PJ] = back[...]
    terms[:, tokens:, PJ:] = jnp.zeros((chips, part, KV - PJ), BF16)
    first = pltpu.make_async_copy(terms, terms_out, sems.at[0])
    first.start()
    keys = mine[:, :tokens, :LANES].reshape(half, LANES)
    query_term = contract(dscores_b[...], keys, 1, 0) * scale
    kept[...] = query_term[:tokens, :]
    sent[:, :LANES] = query_term[tokens:, :].astype(BF16)
    sent[:, LANES:] = sent_sum[...].astype(BF16)
    second = pltpu.make_async_copy(sent, sent_out, sems.at[1])
    second.start()
    first.wait()
    second.wait()


def halve(value, side):
    blocks = value.reshape((value.shape[0] // 2, 2) + value.shape[1:])
    odd = side == 1
    kept = jnp.where(odd, blocks[:, 1], blocks[:, 0])
    sent = jnp.where(odd, blocks[:, 0], blocks[:, 1])
    return kept, sent.astype(BF16)


def total_body(*refs):
    value = refs[0][...].astype(F32)
    for ref in refs[1:-1]:
        value = value + ref[...].astype(F32)
    refs[-1][...] = value.astype(refs[-1].dtype)


def grads_body(parts, query_held, query_got, hidden, grads, query_grad, kept, sent):
    tokens, width = hidden.shape
    query = query_held[:, :HD] + query_got[:, :HD].astype(F32)
    query_grad[...] = query.astype(BF16)
    total = jnp.zeros((tokens, KV), F32)
    for chip in range(parts.shape[0]):
        total = total + parts[chip, :tokens, :].astype(F32)
    grads[...] = total.astype(BF16)
    core = lax.axis_index("core")
    cut = width // CORES
    first = 0
    for grad in (query_grad[...], grads[...]):
        value = contract(grad, hidden[...], 0, 0)
        rows = pl.ds(first, value.shape[0])
        left, right = value[:, :cut], value[:, cut:]
        kept[rows, :] = jnp.where(core == 0, left, right).astype(BF16)
        sent[rows, :] = jnp.where(core == 0, right, left).astype(BF16)
        first += value.shape[0]


def input_body(
    w_query_hbm,
    w_key_hbm,
    w_value_hbm,
    w_junction_hbm,
    parts,
    kept_sum,
    query_got,
    donor_hot,
    grads,
    query_grad,
    kept,
    sent,
    weights,
    w_junction,
    sems,
):
    copies = [
        pltpu.make_async_copy(source, weights.at[pl.ds(i * HD, HD)], sems.at[i])
        for i, source in enumerate((w_query_hbm, w_key_hbm, w_value_hbm))
    ]
    copies.append(pltpu.make_async_copy(w_junction_hbm, w_junction, sems.at[3]))
    for copy in copies:
        copy.start()
    both = jnp.concatenate([query_grad[...], grads[...]], axis=1)
    chips, height, _ = parts.shape
    tokens = grads.shape[0]
    part = height - tokens
    slot_rows = parts[:, tokens:, :PJ].reshape(chips * part, PJ)
    feature_grad = kept_sum[...] + query_got[:, LANES:].astype(F32)
    feature_grad = (feature_grad + contract(donor_hot[...], slot_rows, 0, 0)).astype(BF16)
    for copy in copies:
        copy.wait()
    value = contract(weights[...], both, 0, 1) + contract(w_junction[...], feature_grad, 1, 1)
    blocks = value.reshape((2 * kept.shape[0],) + kept.shape[1:])
    kept[...], sent[...] = halve(blocks, lax.axis_index("side"))


def tiles_of(rows, columns, count):
    high, wide = rows * 2 // count, columns // 2
    return [(i, pl.ds(i // 2 * high, high), pl.ds(i % 2 * wide, wide)) for i in range(count)]


def pair_body(held, got, out, total, sems):
    chips, part, _ = total.shape
    copies = []
    for chip in range(chips):
        rows = pl.ds(chip * part, part)
        value = held[rows, :].astype(F32) + got[rows, :].astype(F32)
        total[chip] = value.astype(BF16)
        copy = pltpu.make_async_copy(total.at[chip], out.at[chip], sems.at[chip])
        copy.start()
        copies.append(copy)
    for copy in copies:
        copy.wait()


def sum_body(parts, total):
    value = parts[0].astype(F32)
    for i in range(1, parts.shape[0]):
        value = value + parts[i].astype(F32)
    total[...] = value.astype(total.dtype)


def cut_body(parts, tiles, whole):
    value = parts[0].astype(F32)
    for i in range(1, parts.shape[0]):
        value = value + parts[i].astype(F32)
    whole[...] = value
    for i, rows, columns in tiles_of(*whole.shape, tiles.shape[0]):
        tiles[i] = whole[rows, columns].astype(BF16)


def spread_body(parts, copies):
    value = parts[0].astype(F32)
    for i in range(1, parts.shape[0]):
        value = value + parts[i].astype(F32)
    value = value.astype(BF16)
    for i in range(copies.shape[0]):
        copies[i] = value


def join_body(tiles, joined, whole):
    for i, rows, columns in tiles_of(*whole.shape, tiles.shape[0]):
        whole[rows, columns] = tiles[i].astype(F32)
    joined[...] = whole[...].astype(BF16)


def place(source, outs, sems, core):
    cut = source.shape[1]
    columns = pl.ds(pl.multiple_of(core * cut, cut), cut)
    copies = [
        pltpu.make_async_copy(source.at[pl.ds(i * HD, HD)], out.at[:, columns], sems.at[i])
        for i, out in enumerate(outs)
    ]
    for copy in copies:
        copy.start()
    for copy in copies:
        copy.wait()


def own_half_body(mine, *refs):
    place(mine, refs[:3], refs[3], lax.axis_index("core"))


def other_half_body(theirs, *refs):
    place(theirs, refs[3:6], refs[6], 1 - lax.axis_index("core"))


def swap(value, axis="core"):
    return lax.ppermute(value, axis, [(0, 1), (1, 0)])


def in_hbm(*values):
    return [pltpu.with_memory_space_constraint(value, pltpu.HBM) for value in values]


def exchange(value, axis):
    return lax.all_to_all(value, axis, 0, 0, tiled=True)


def on_device(
    hidden_in,
    ctx_grad,
    w_query,
    w_key,
    w_value,
    w_junction,
    donor_pos,
    acceptor_pos,
    junction_counts,
    pred_grad,
):
    hidden = hidden_in[0]
    tokens, width = hidden.shape
    chips = lax.axis_size("x")
    intervals = lax.axis_size("interval")
    heads = lax.axis_size("pair") * SIDES
    half = chips * tokens
    buckets, per = donor_pos.shape[2:]
    slots = buckets * per
    height = tokens + slots // chips

    message, donor_hot = local_call(
        project_body,
        [((chips, height, KV), BF16, True), ((slots, tokens), BF16)],
        operands=8,
        fetched=8,
        scratch=[
            pltpu.VMEM((tokens, KV), BF16),
            pltpu.VMEM((slots, KV), BF16),
            pltpu.VMEM((tokens, width), BF16),
            pltpu.VMEM((KV, width), BF16),
            pltpu.VMEM((width, PJ), BF16),
            pltpu.VMEM((buckets, per), jnp.int32),
            pltpu.VMEM((buckets, per), jnp.int32),
            pltpu.VMEM((1, buckets), jnp.int32),
            pltpu.VMEM((buckets, per), F32),
            pltpu.SemaphoreType.DMA((8,)),
            pltpu.SemaphoreType.DMA((2 * chips,)),
        ],
    )(
        *in_hbm(
            hidden,
            w_key,
            w_value,
            w_junction,
            donor_pos[0, 0],
            acceptor_pos[0, 0],
            junction_counts[0],
            pred_grad[0, 0],
        )
    )
    mine = exchange(message, "x")
    (own,) = local_call(query_body, [((tokens, 2 * LANES + PJ), BF16)], operands=4)(
        hidden, w_query, w_junction, ctx_grad[0].T
    )
    other = swap(own)
    expd, dprobs, stats = local_call(
        score_body,
        [((CORES, tokens, half), F32), ((CORES, tokens, half), F32), ((CORES, 8, tokens), F32)],
        operands=3,
    )(own, other, mine)
    got = swap(stats)
    back, kept_sum, sent_sum = local_call(
        slot_body,
        [((chips, height - tokens, PJ), BF16), ((tokens, PJ), F32), ((tokens, PJ), F32)],
        operands=3,
    )(own, other, mine)
    terms, query_sent, query_held = local_call(
        grad_body,
        [
            ((chips, height, KV), BF16, True),
            ((tokens, LANES + PJ), BF16, True),
            ((tokens, LANES), F32),
        ],
        operands=9,
        scratch=[
            pltpu.VMEM((chips, height, KV), BF16),
            pltpu.VMEM((tokens, LANES + PJ), BF16),
        ]
        + [pltpu.VMEM((CORES * tokens, half), BF16)] * 2
        + [pltpu.SemaphoreType.DMA((2,))],
    )(own, other, mine, expd, dprobs, stats, got, back, sent_sum)
    query_got = swap(query_sent)
    parts = exchange(terms, "x")
    parts, query_got = lax.optimization_barrier((parts, query_got))
    rows = 3 * HD
    cut = width // CORES
    block = (width // heads, tokens)
    grads, query_grad, weight_held, weight_sent = local_call(
        grads_body,
        [((tokens, KV), BF16), ((tokens, HD), BF16), ((rows, cut), BF16), ((rows, cut), BF16)],
        operands=4,
    )(parts, query_held, query_got, hidden)
    held, sent = local_call(
        input_body,
        [((heads // 2,) + block, F32), ((heads // 2,) + block, BF16)],
        operands=10,
        fetched=4,
        scratch=[
            pltpu.VMEM((rows, width), BF16),
            pltpu.VMEM((width, PJ), BF16),
            pltpu.SemaphoreType.DMA((4,)),
        ],
    )(
        *in_hbm(w_query, w_key, w_value, w_junction),
        parts,
        kept_sum,
        query_got,
        donor_hot,
        grads,
        query_grad,
    )

    weight_got, sent = lax.optimization_barrier((swap(weight_sent), sent))
    part = rows // chips
    (term,) = local_call(
        pair_body,
        [((chips, part, cut), BF16, True)],
        operands=2,
        scratch=[pltpu.VMEM((chips, part, cut), BF16), pltpu.SemaphoreType.DMA((chips,))],
    )(weight_held, weight_got)
    tile = (part * 2 // intervals, cut // 2)
    (tiles,) = local_call(
        cut_body, [((intervals,) + tile, BF16)], operands=1, scratch=[pltpu.VMEM((part, cut), F32)]
    )(exchange(term, "x"))
    tiles, got = lax.optimization_barrier((tiles, swap(sent, "side")))
    (blocks,) = local_call(total_body, [((heads // SIDES,) + block, BF16)], operands=2)(held, got)
    (copies,) = local_call(spread_body, [((intervals,) + tile, BF16)], operands=1)(
        exchange(tiles, "interval")
    )
    (term,) = local_call(
        join_body, [((part, cut), BF16)], operands=1, scratch=[pltpu.VMEM((part, cut), F32)]
    )(exchange(copies, "interval"))
    blocks = exchange(blocks, "pair")
    term = lax.all_gather(term, "x", axis=0, tiled=True)
    term, blocks = lax.optimization_barrier((term, blocks))
    (grad_input,) = local_call(sum_body, [(block, BF16)], operands=1)(blocks)
    wide = [((HD, width), BF16)] * 3
    sems = [pltpu.SemaphoreType.DMA((3,))]
    theirs = swap(term)
    grads = local_call(own_half_body, wide, operands=1, scratch=sems, space=pl.ANY)(term)
    grads = local_call(
        other_half_body,
        wide,
        operands=4,
        scratch=sems,
        space=pl.ANY,
        aliases={i + 1: i for i in range(3)},
    )(theirs, *grads)
    return (grad_input.T[None],) + tuple(grads)


def solution(mesh):
    axes = (mesh.shape["interval"], mesh.shape["seq"] // CORES, CORES)
    axes += (mesh.shape["head"] // SIDES, SIDES)
    split = Mesh(mesh.devices.reshape(axes), ("interval", "x", "core", "pair", "side"))
    seq, head = ("x", "core"), ("pair", "side")
    placed = (
        P("interval", seq, None),
        P("interval", seq, head),
        P(head, None),
        P(head, None),
        P(head, None),
        P(),
        P("interval", seq, None, head),
        P("interval", seq, None, head),
        P("interval", seq, None),
        P("interval", seq, None, head),
    )
    return jax.shard_map(
        on_device,
        mesh=split,
        in_specs=placed,
        out_specs=(P("interval", seq, head), P(head, None), P(head, None), P(head, None)),
        check_vma=False,
    )
```

```python
import jax
import jax.numpy as jnp
from jax import lax
from jax.experimental import pallas as pl
from jax.experimental.pallas import tpu as pltpu
from jax.sharding import Mesh
from jax.sharding import PartitionSpec as P

HD = 192
PJ = 128
CORES = 2
SIDES = 2
LANES = 256
BAND = 128
KV = 2 * HD
SHIFT = KV - LANES
F32 = jnp.float32
BF16 = jnp.bfloat16
VMEM_BYTES = 20 * 1024 * 1024


def contract(a, b, dim_a, dim_b, precision=None):
    return lax.dot_general(
        a, b, (((dim_a,), (dim_b,)), ((), ())), precision=precision, preferred_element_type=F32
    )


def iota(shape, axis):
    return lax.broadcasted_iota(jnp.int32, shape, axis)


def local_call(body, outs, operands, scratch=(), fetched=0, space=pltpu.VMEM, aliases={}):
    specs = [pl.BlockSpec(memory_space=pltpu.HBM)] * fetched
    specs += [pl.BlockSpec(memory_space=space)] * (operands - fetched)
    shapes = [
        (pltpu.HBM if len(out) > 2 else jax.ShapeDtypeStruct)(out[0], out[1]) for out in outs
    ]
    return pl.pallas_call(
        body,
        out_shape=tuple(shapes),
        in_specs=specs,
        out_specs=tuple(
            pl.BlockSpec(memory_space=pltpu.HBM if len(out) > 2 else space) for out in outs
        ),
        scratch_shapes=list(scratch),
        input_output_aliases=dict(aliases),
        compiler_params=pltpu.CompilerParams(vmem_limit_bytes=VMEM_BYTES),
    )


def split_terms(term, count=2):
    pieces = []
    for _ in range(count):
        piece = term.astype(BF16)
        pieces.append(piece)
        term = term - piece.astype(F32)
    return pieces


def project_body(
    hidden_hbm,
    w_key_hbm,
    w_value_hbm,
    w_junction_hbm,
    donor_hbm,
    acceptor_hbm,
    counts_hbm,
    pred_hbm,
    message,
    donor_hot,
    rows,
    slot_rows,
    hidden,
    weights,
    w_junction,
    donor_pos,
    acceptor_pos,
    counts,
    pred_grad,
    sems,
    row_sems,
):
    targets = (
        donor_pos,
        acceptor_pos,
        counts,
        pred_grad,
        hidden,
        weights.at[pl.ds(0, HD)],
        weights.at[pl.ds(HD, HD)],
        w_junction,
    )
    sources = (
        donor_hbm,
        acceptor_hbm,
        counts_hbm,
        pred_hbm,
        hidden_hbm,
        w_key_hbm,
        w_value_hbm,
        w_junction_hbm,
    )
    copies = [
        pltpu.make_async_copy(source, target, sems.at[i])
        for i, (source, target) in enumerate(zip(sources, targets))
    ]
    for copy in copies:
        copy.start()
    for copy in copies[:4]:
        copy.wait()
    chips = message.shape[0]
    tokens = hidden.shape[0]
    buckets, per = donor_pos.shape
    slots = buckets * per
    square = iota((buckets, buckets), 0) == iota((buckets, buckets), 1)
    limit = jnp.sum(
        jnp.where(square, counts[...].astype(F32), 0.0), axis=1, keepdims=True
    )
    head = lax.axis_index("pair") * SIDES + lax.axis_index("side")
    slot_ids = head * per + iota((buckets, per), 1)
    live_grad = jnp.where(slot_ids.astype(F32) < limit, pred_grad[...], 0.0)
    pick_bucket = (iota((slots, buckets), 0) // per == iota((slots, buckets), 1)).astype(F32)
    own_slot = iota((slots, per), 0) % per == iota((slots, per), 1)

    def to_column(value):
        wide = contract(pick_bucket, value.astype(F32), 1, 0, lax.Precision.HIGHEST)
        return jnp.sum(jnp.where(own_slot, wide, 0.0), axis=1, keepdims=True)

    donor = to_column(donor_pos[...])
    hot = jnp.where(iota((slots, tokens), 1).astype(F32) == donor, 1.0, 0.0).astype(BF16)
    donor_hot[...] = hot
    lane = iota((slots, PJ), 1)
    scalars = [to_column(acceptor_pos[...])]
    scalars += [piece.astype(F32) for piece in split_terms(to_column(live_grad), 3)]
    extra = jnp.zeros((slots, PJ), F32)
    for i, column in enumerate(scalars):
        extra = jnp.where(lane == i, column, extra)
    for copy in copies[4:]:
        copy.wait()
    x = hidden[...]
    rows[...] = contract(x, weights[...], 1, 1).astype(BF16)
    part = slots // chips
    leaving = [
        pltpu.make_async_copy(rows, message.at[chip, pl.ds(0, tokens)], row_sems.at[chip])
        for chip in range(chips)
    ]
    for copy in leaving:
        copy.start()
    feats = contract(x, w_junction[...], 1, 0).astype(BF16)
    slot_rows[...] = jnp.concatenate(
        [
            contract(hot, feats, 1, 0).astype(BF16),
            extra.astype(BF16),
            jnp.zeros((slots, KV - 2 * PJ), BF16),
        ],
        axis=1,
    )
    last = [
        pltpu.make_async_copy(
            slot_rows.at[pl.ds(chip * part, part)],
            message.at[chip, pl.ds(tokens, part)],
            row_sems.at[chips + chip],
        )
        for chip in range(chips)
    ]
    for copy in last:
        copy.start()
    for copy in leaving + last:
        copy.wait()


def query_body(hidden, w_query, w_junction, ctx_t, rows):
    tokens = hidden.shape[0]
    pad = jnp.zeros((tokens, LANES - HD), BF16)
    value = contract(hidden[...], w_query[...], 1, 1).astype(BF16)
    rows[:, :LANES] = jnp.concatenate([value, pad], axis=1)
    ctx = jnp.transpose(ctx_t[...].astype(F32)).astype(BF16)
    rows[:, LANES : 2 * LANES] = jnp.concatenate([pad, ctx], axis=1)
    rows[:, 2 * LANES :] = contract(hidden[...], w_junction[...], 1, 0).astype(BF16)


def diagonal(size):
    return iota((size, size), 0) == iota((size, size), 1)


def score_body(own, other, mine, expd, dprobs, stats):
    tokens = own.shape[0]
    half = mine.shape[0] * tokens
    keys = mine[:, :tokens, :].reshape(half, KV)
    square = diagonal(BAND)
    blank = jnp.zeros((8 - 3, BAND), F32)
    for i, rows in enumerate((own, other)):
        for start in range(0, tokens, BAND):
            band = pl.ds(start, BAND)
            score = contract(rows[band, :LANES], keys[:, :LANES], 1, 1) * HD ** (-0.5)
            row_max = jnp.max(score, axis=-1, keepdims=True)
            value = jnp.exp(score - row_max)
            dprob = contract(rows[band, LANES : 2 * LANES], keys[:, SHIFT:], 1, 1)
            expd[i, band, :] = value
            dprobs[i, band, :] = dprob
            columns = (
                row_max,
                jnp.sum(value, axis=-1, keepdims=True),
                jnp.sum(value * dprob, axis=-1, keepdims=True),
            )
            lines = [
                jnp.sum(jnp.where(square, column, 0.0), axis=0, keepdims=True)
                for column in columns
            ]
            stats[i, :, band] = jnp.concatenate(lines + [blank], axis=0)


def slot_body(own, other, mine, back, kept_sum, sent_sum):
    tokens = own.shape[0]
    chips, height, _ = mine.shape
    part = height - tokens
    slots = chips * part
    slot_rows = mine[:, tokens:, :].astype(F32).reshape(slots, KV)
    donor_feat = slot_rows[:, :PJ]
    extra = slot_rows[:, PJ : 2 * PJ]
    acceptor = extra[:, 0:1]
    slot_scale = extra[:, 1:2] + extra[:, 2:3] + extra[:, 3:4]
    shard = iota((slots, 1), 0) % part // (part // CORES)
    here = shard == lax.axis_index("core")
    place = iota((slots, tokens), 1).astype(F32) == acceptor
    hots = [
        jnp.where(place, jnp.where(chosen, 1.0, 0.0), 0.0).astype(BF16)
        for chosen in (here, jnp.logical_not(here))
    ]
    accept_feat = contract(hots[0], own[:, 2 * LANES :], 1, 0) + contract(
        hots[1], other[:, 2 * LANES :], 1, 0
    )
    pair_scale = PJ ** (-0.5)
    pair_score = jnp.sum(donor_feat * accept_feat, axis=-1, keepdims=True) * pair_scale
    slot_grad = slot_scale * jax.nn.sigmoid(pair_score) * pair_scale
    pieces = split_terms(slot_grad * donor_feat)
    for hot, total in zip(hots, (kept_sum, sent_sum)):
        total[...] = contract(hot, pieces[0], 0, 0) + contract(hot, pieces[1], 0, 0)
    back[...] = (slot_grad * accept_feat).astype(BF16).reshape(chips, part, PJ)


def grad_body(
    own,
    other,
    mine,
    expd,
    dprobs,
    stats,
    got,
    back,
    sent_sum,
    terms_out,
    sent_out,
    kept,
    terms,
    sent,
    probs_b,
    dscores_b,
    sems,
):
    tokens = own.shape[0]
    chips, height, _ = mine.shape
    part = height - tokens
    half = chips * tokens
    scale = HD ** (-0.5)
    square = diagonal(BAND)
    for i in range(CORES):
        for start in range(0, tokens, BAND):
            band = pl.ds(start, BAND)
            here, there = stats[i, :, band], got[1 - i, :, band]
            top = jnp.maximum(here[0:1], there[0:1])
            near, far = jnp.exp(here[0:1] - top), jnp.exp(there[0:1] - top)
            inverse = 1.0 / (here[1:2] * near + there[1:2] * far)
            delta = (here[2:3] * near + there[2:3] * far) * inverse
            factor, delta = (
                jnp.sum(jnp.where(square, line, 0.0), axis=1, keepdims=True)
                for line in (near * inverse, delta)
            )
            probs = expd[i, band, :] * factor
            rows = pl.ds(i * tokens + start, BAND)
            probs_b[rows, :] = probs.astype(BF16)
            dscores_b[rows, :] = (probs * (dprobs[i, band, :] - delta)).astype(BF16)
    rows = jnp.concatenate([own[:, : 2 * LANES], other[:, : 2 * LANES]], axis=0)
    key_term = contract(dscores_b[...], rows[:, :LANES], 0, 0) * scale
    value_term = contract(probs_b[...], rows[:, LANES:], 0, 0)
    middle = key_term[:, SHIFT:] + value_term[:, :SHIFT]
    for first, value in (
        (0, key_term[:, :SHIFT]),
        (SHIFT, middle),
        (LANES, value_term[:, SHIFT:]),
    ):
        terms[:, :tokens, first : first + SHIFT] = value.astype(BF16).reshape(
            chips, tokens, SHIFT
        )
    terms[:, tokens:, :PJ] = back[...]
    terms[:, tokens:, PJ:] = jnp.zeros((chips, part, KV - PJ), BF16)
    first = pltpu.make_async_copy(terms, terms_out, sems.at[0])
    first.start()
    keys = mine[:, :tokens, :LANES].reshape(half, LANES)
    query_term = contract(dscores_b[...], keys, 1, 0) * scale
    kept[...] = query_term[:tokens, :]
    sent[:, :LANES] = query_term[tokens:, :].astype(BF16)
    sent[:, LANES:] = sent_sum[...].astype(BF16)
    second = pltpu.make_async_copy(sent, sent_out, sems.at[1])
    second.start()
    first.wait()
    second.wait()


def halve(value, side):
    blocks = value.reshape((value.shape[0] // 2, 2) + value.shape[1:])
    odd = side == 1
    kept = jnp.where(odd, blocks[:, 1], blocks[:, 0])
    sent = jnp.where(odd, blocks[:, 0], blocks[:, 1])
    return kept, sent.astype(BF16)


def total_body(*refs):
    value = refs[0][...].astype(F32)
    for ref in refs[1:-1]:
        value = value + ref[...].astype(F32)
    refs[-1][...] = value.astype(refs[-1].dtype)


def grads_body(parts, query_held, query_got, hidden, grads, query_grad, kept, sent):
    tokens, width = hidden.shape
    query = query_held[:, :HD] + query_got[:, :HD].astype(F32)
    query_grad[...] = query.astype(BF16)
    total = jnp.zeros((tokens, KV), F32)
    for chip in range(parts.shape[0]):
        total = total + parts[chip, :tokens, :].astype(F32)
    grads[...] = total.astype(BF16)
    core = lax.axis_index("core")
    cut = width // CORES
    first = 0
    for grad in (query_grad[...], grads[...]):
        value = contract(grad, hidden[...], 0, 0)
        rows = pl.ds(first, value.shape[0])
        left, right = value[:, :cut], value[:, cut:]
        kept[rows, :] = jnp.where(core == 0, left, right).astype(BF16)
        sent[rows, :] = jnp.where(core == 0, right, left).astype(BF16)
        first += value.shape[0]


def input_body(
    w_query_hbm,
    w_key_hbm,
    w_value_hbm,
    w_junction_hbm,
    parts,
    kept_sum,
    query_got,
    donor_hot,
    grads,
    query_grad,
    kept,
    sent,
    weights,
    w_junction,
    sems,
):
    copies = [
        pltpu.make_async_copy(source, weights.at[pl.ds(i * HD, HD)], sems.at[i])
        for i, source in enumerate((w_query_hbm, w_key_hbm, w_value_hbm))
    ]
    copies.append(pltpu.make_async_copy(w_junction_hbm, w_junction, sems.at[3]))
    for copy in copies:
        copy.start()
    both = jnp.concatenate([query_grad[...], grads[...]], axis=1)
    chips, height, _ = parts.shape
    tokens = grads.shape[0]
    part = height - tokens
    slot_rows = parts[:, tokens:, :PJ].reshape(chips * part, PJ)
    feature_grad = kept_sum[...] + query_got[:, LANES:].astype(F32)
    feature_grad = (feature_grad + contract(donor_hot[...], slot_rows, 0, 0)).astype(BF16)
    for copy in copies:
        copy.wait()
    value = contract(weights[...], both, 0, 1) + contract(w_junction[...], feature_grad, 1, 1)
    blocks = value.reshape((2 * kept.shape[0],) + kept.shape[1:])
    kept[...], sent[...] = halve(blocks, lax.axis_index("side"))


def tiles_of(rows, columns, count):
    high, wide = rows * 2 // count, columns // 2
    return [(i, pl.ds(i // 2 * high, high), pl.ds(i % 2 * wide, wide)) for i in range(count)]


def pair_body(held, got, out, total, sems):
    chips, part, _ = total.shape
    copies = []
    for chip in range(chips):
        rows = pl.ds(chip * part, part)
        value = held[rows, :].astype(F32) + got[rows, :].astype(F32)
        total[chip] = value.astype(BF16)
        copy = pltpu.make_async_copy(total.at[chip], out.at[chip], sems.at[chip])
        copy.start()
        copies.append(copy)
    for copy in copies:
        copy.wait()


def sum_body(parts, total):
    value = parts[0].astype(F32)
    for i in range(1, parts.shape[0]):
        value = value + parts[i].astype(F32)
    total[...] = value.astype(total.dtype)


def cut_body(parts, tiles, whole):
    value = parts[0].astype(F32)
    for i in range(1, parts.shape[0]):
        value = value + parts[i].astype(F32)
    whole[...] = value
    for i, rows, columns in tiles_of(*whole.shape, tiles.shape[0]):
        tiles[i] = whole[rows, columns].astype(BF16)


def spread_body(parts, copies):
    value = parts[0].astype(F32)
    for i in range(1, parts.shape[0]):
        value = value + parts[i].astype(F32)
    value = value.astype(BF16)
    for i in range(copies.shape[0]):
        copies[i] = value


def join_body(tiles, joined, whole):
    for i, rows, columns in tiles_of(*whole.shape, tiles.shape[0]):
        whole[rows, columns] = tiles[i].astype(F32)
    joined[...] = whole[...].astype(BF16)


def place(source, outs, sems, core):
    cut = source.shape[1]
    columns = pl.ds(pl.multiple_of(core * cut, cut), cut)
    copies = [
        pltpu.make_async_copy(source.at[pl.ds(i * HD, HD)], out.at[:, columns], sems.at[i])
        for i, out in enumerate(outs)
    ]
    for copy in copies:
        copy.start()
    for copy in copies:
        copy.wait()


def own_half_body(mine, *refs):
    place(mine, refs[:3], refs[3], lax.axis_index("core"))


def other_half_body(theirs, *refs):
    place(theirs, refs[3:6], refs[6], 1 - lax.axis_index("core"))


def swap(value, axis="core"):
    return lax.ppermute(value, axis, [(0, 1), (1, 0)])


def in_hbm(*values):
    return [pltpu.with_memory_space_constraint(value, pltpu.HBM) for value in values]


def exchange(value, axis):
    return lax.all_to_all(value, axis, 0, 0, tiled=True)


def on_device(
    hidden_in,
    ctx_grad,
    w_query,
    w_key,
    w_value,
    w_junction,
    donor_pos,
    acceptor_pos,
    junction_counts,
    pred_grad,
):
    hidden = hidden_in[0]
    tokens, width = hidden.shape
    chips = lax.axis_size("x")
    intervals = lax.axis_size("interval")
    heads = lax.axis_size("pair") * SIDES
    half = chips * tokens
    buckets, per = donor_pos.shape[2:]
    slots = buckets * per
    height = tokens + slots // chips

    message, donor_hot = local_call(
        project_body,
        [((chips, height, KV), BF16, True), ((slots, tokens), BF16)],
        operands=8,
        fetched=8,
        scratch=[
            pltpu.VMEM((tokens, KV), BF16),
            pltpu.VMEM((slots, KV), BF16),
            pltpu.VMEM((tokens, width), BF16),
            pltpu.VMEM((KV, width), BF16),
            pltpu.VMEM((width, PJ), BF16),
            pltpu.VMEM((buckets, per), jnp.int32),
            pltpu.VMEM((buckets, per), jnp.int32),
            pltpu.VMEM((1, buckets), jnp.int32),
            pltpu.VMEM((buckets, per), F32),
            pltpu.SemaphoreType.DMA((8,)),
            pltpu.SemaphoreType.DMA((2 * chips,)),
        ],
    )(
        *in_hbm(
            hidden,
            w_key,
            w_value,
            w_junction,
            donor_pos[0, 0],
            acceptor_pos[0, 0],
            junction_counts[0],
            pred_grad[0, 0],
        )
    )
    mine = exchange(message, "x")
    (own,) = local_call(query_body, [((tokens, 2 * LANES + PJ), BF16)], operands=4)(
        hidden, w_query, w_junction, ctx_grad[0].T
    )
    other = swap(own)
    expd, dprobs, stats = local_call(
        score_body,
        [((CORES, tokens, half), F32), ((CORES, tokens, half), F32), ((CORES, 8, tokens), F32)],
        operands=3,
    )(own, other, mine)
    got = swap(stats)
    back, kept_sum, sent_sum = local_call(
        slot_body,
        [((chips, height - tokens, PJ), BF16), ((tokens, PJ), F32), ((tokens, PJ), F32)],
        operands=3,
    )(own, other, mine)
    terms, query_sent, query_held = local_call(
        grad_body,
        [
            ((chips, height, KV), BF16, True),
            ((tokens, LANES + PJ), BF16, True),
            ((tokens, LANES), F32),
        ],
        operands=9,
        scratch=[
            pltpu.VMEM((chips, height, KV), BF16),
            pltpu.VMEM((tokens, LANES + PJ), BF16),
        ]
        + [pltpu.VMEM((CORES * tokens, half), BF16)] * 2
        + [pltpu.SemaphoreType.DMA((2,))],
    )(own, other, mine, expd, dprobs, stats, got, back, sent_sum)
    query_got = swap(query_sent)
    parts = exchange(terms, "x")
    parts, query_got = lax.optimization_barrier((parts, query_got))
    rows = 3 * HD
    cut = width // CORES
    block = (width // heads, tokens)
    grads, query_grad, weight_held, weight_sent = local_call(
        grads_body,
        [((tokens, KV), BF16), ((tokens, HD), BF16), ((rows, cut), BF16), ((rows, cut), BF16)],
        operands=4,
    )(parts, query_held, query_got, hidden)
    held, sent = local_call(
        input_body,
        [((heads // 2,) + block, F32), ((heads // 2,) + block, BF16)],
        operands=10,
        fetched=4,
        scratch=[
            pltpu.VMEM((rows, width), BF16),
            pltpu.VMEM((width, PJ), BF16),
            pltpu.SemaphoreType.DMA((4,)),
        ],
    )(
        *in_hbm(w_query, w_key, w_value, w_junction),
        parts,
        kept_sum,
        query_got,
        donor_hot,
        grads,
        query_grad,
    )

    weight_got = swap(weight_sent)
    part = rows // chips
    (term,) = local_call(
        pair_body,
        [((chips, part, cut), BF16, True)],
        operands=2,
        scratch=[pltpu.VMEM((chips, part, cut), BF16), pltpu.SemaphoreType.DMA((chips,))],
    )(weight_held, weight_got)
    tile = (part * 2 // intervals, cut // 2)
    (tiles,) = local_call(
        cut_body, [((intervals,) + tile, BF16)], operands=1, scratch=[pltpu.VMEM((part, cut), F32)]
    )(exchange(term, "x"))
    got = swap(sent, "side")
    (copies,) = local_call(spread_body, [((intervals,) + tile, BF16)], operands=1)(
        exchange(tiles, "interval")
    )
    copies, got = lax.optimization_barrier((copies, got))
    (blocks,) = local_call(total_body, [((heads // SIDES,) + block, BF16)], operands=2)(held, got)
    (term,) = local_call(
        join_body, [((part, cut), BF16)], operands=1, scratch=[pltpu.VMEM((part, cut), F32)]
    )(exchange(copies, "interval"))
    blocks = exchange(blocks, "pair")
    term = lax.all_gather(term, "x", axis=0, tiled=True)
    term, blocks = lax.optimization_barrier((term, blocks))
    (grad_input,) = local_call(sum_body, [(block, BF16)], operands=1)(blocks)
    wide = [((HD, width), BF16)] * 3
    sems = [pltpu.SemaphoreType.DMA((3,))]
    theirs = swap(term)
    grads = local_call(own_half_body, wide, operands=1, scratch=sems, space=pl.ANY)(term)
    grads = local_call(
        other_half_body,
        wide,
        operands=4,
        scratch=sems,
        space=pl.ANY,
        aliases={i + 1: i for i in range(3)},
    )(theirs, *grads)
    return (grad_input.T[None],) + tuple(grads)


def solution(mesh):
    axes = (mesh.shape["interval"], mesh.shape["seq"] // CORES, CORES)
    axes += (mesh.shape["head"] // SIDES, SIDES)
    split = Mesh(mesh.devices.reshape(axes), ("interval", "x", "core", "pair", "side"))
    seq, head = ("x", "core"), ("pair", "side")
    placed = (
        P("interval", seq, None),
        P("interval", seq, head),
        P(head, None),
        P(head, None),
        P(head, None),
        P(),
        P("interval", seq, None, head),
        P("interval", seq, None, head),
        P("interval", seq, None),
        P("interval", seq, None, head),
    )
    return jax.shard_map(
        on_device,
        mesh=split,
        in_specs=placed,
        out_specs=(P("interval", seq, head), P(head, None), P(head, None), P(head, None)),
        check_vma=False,
    )
```

```python
import jax
import jax.numpy as jnp
from jax import lax
from jax.experimental import pallas as pl
from jax.experimental.pallas import tpu as pltpu
from jax.sharding import Mesh
from jax.sharding import PartitionSpec as P

HD = 192
PJ = 128
CORES = 2
SIDES = 2
LANES = 256
BAND = 128
KV = 2 * HD
SHIFT = KV - LANES
F32 = jnp.float32
BF16 = jnp.bfloat16
VMEM_BYTES = 20 * 1024 * 1024


def contract(a, b, dim_a, dim_b, precision=None):
    return lax.dot_general(
        a, b, (((dim_a,), (dim_b,)), ((), ())), precision=precision, preferred_element_type=F32
    )


def iota(shape, axis):
    return lax.broadcasted_iota(jnp.int32, shape, axis)


def local_call(body, outs, operands, scratch=(), fetched=0, space=pltpu.VMEM, aliases={}):
    specs = [pl.BlockSpec(memory_space=pltpu.HBM)] * fetched
    specs += [pl.BlockSpec(memory_space=space)] * (operands - fetched)
    shapes = [
        (pltpu.HBM if len(out) > 2 else jax.ShapeDtypeStruct)(out[0], out[1]) for out in outs
    ]
    return pl.pallas_call(
        body,
        out_shape=tuple(shapes),
        in_specs=specs,
        out_specs=tuple(
            pl.BlockSpec(memory_space=pltpu.HBM if len(out) > 2 else space) for out in outs
        ),
        scratch_shapes=list(scratch),
        input_output_aliases=dict(aliases),
        compiler_params=pltpu.CompilerParams(vmem_limit_bytes=VMEM_BYTES),
    )


def split_terms(term, count=2):
    pieces = []
    for _ in range(count):
        piece = term.astype(BF16)
        pieces.append(piece)
        term = term - piece.astype(F32)
    return pieces


def project_body(
    hidden_hbm,
    w_key_hbm,
    w_value_hbm,
    w_junction_hbm,
    donor_hbm,
    acceptor_hbm,
    counts_hbm,
    pred_hbm,
    message,
    donor_hot,
    rows,
    slot_rows,
    hidden,
    weights,
    w_junction,
    donor_pos,
    acceptor_pos,
    counts,
    pred_grad,
    sems,
    row_sems,
):
    targets = (
        donor_pos,
        acceptor_pos,
        counts,
        pred_grad,
        hidden,
        weights.at[pl.ds(0, HD)],
        weights.at[pl.ds(HD, HD)],
        w_junction,
    )
    sources = (
        donor_hbm,
        acceptor_hbm,
        counts_hbm,
        pred_hbm,
        hidden_hbm,
        w_key_hbm,
        w_value_hbm,
        w_junction_hbm,
    )
    copies = [
        pltpu.make_async_copy(source, target, sems.at[i])
        for i, (source, target) in enumerate(zip(sources, targets))
    ]
    for copy in copies:
        copy.start()
    for copy in copies[:4]:
        copy.wait()
    chips = message.shape[0]
    tokens = hidden.shape[0]
    buckets, per = donor_pos.shape
    slots = buckets * per
    square = iota((buckets, buckets), 0) == iota((buckets, buckets), 1)
    limit = jnp.sum(
        jnp.where(square, counts[...].astype(F32), 0.0), axis=1, keepdims=True
    )
    head = lax.axis_index("pair") * SIDES + lax.axis_index("side")
    slot_ids = head * per + iota((buckets, per), 1)
    live_grad = jnp.where(slot_ids.astype(F32) < limit, pred_grad[...], 0.0)
    pick_bucket = (iota((slots, buckets), 0) // per == iota((slots, buckets), 1)).astype(F32)
    own_slot = iota((slots, per), 0) % per == iota((slots, per), 1)

    def to_column(value):
        wide = contract(pick_bucket, value.astype(F32), 1, 0, lax.Precision.HIGHEST)
        return jnp.sum(jnp.where(own_slot, wide, 0.0), axis=1, keepdims=True)

    donor = to_column(donor_pos[...])
    hot = jnp.where(iota((slots, tokens), 1).astype(F32) == donor, 1.0, 0.0).astype(BF16)
    donor_hot[...] = hot
    lane = iota((slots, PJ), 1)
    scalars = [to_column(acceptor_pos[...])]
    scalars += [piece.astype(F32) for piece in split_terms(to_column(live_grad), 3)]
    extra = jnp.zeros((slots, PJ), F32)
    for i, column in enumerate(scalars):
        extra = jnp.where(lane == i, column, extra)
    for copy in copies[4:7]:
        copy.wait()
    x = hidden[...]
    rows[...] = contract(x, weights[...], 1, 1).astype(BF16)
    part = slots // chips
    leaving = [
        pltpu.make_async_copy(rows, message.at[chip, pl.ds(0, tokens)], row_sems.at[chip])
        for chip in range(chips)
    ]
    for copy in leaving:
        copy.start()
    copies[7].wait()
    feats = contract(x, w_junction[...], 1, 0).astype(BF16)
    slot_rows[...] = jnp.concatenate(
        [
            contract(hot, feats, 1, 0).astype(BF16),
            extra.astype(BF16),
            jnp.zeros((slots, KV - 2 * PJ), BF16),
        ],
        axis=1,
    )
    last = [
        pltpu.make_async_copy(
            slot_rows.at[pl.ds(chip * part, part)],
            message.at[chip, pl.ds(tokens, part)],
            row_sems.at[chips + chip],
        )
        for chip in range(chips)
    ]
    for copy in last:
        copy.start()
    for copy in leaving + last:
        copy.wait()


def query_body(hidden, w_query, w_junction, ctx_t, rows):
    tokens = hidden.shape[0]
    pad = jnp.zeros((tokens, LANES - HD), BF16)
    value = contract(hidden[...], w_query[...], 1, 1).astype(BF16)
    rows[:, :LANES] = jnp.concatenate([value, pad], axis=1)
    ctx = jnp.transpose(ctx_t[...].astype(F32)).astype(BF16)
    rows[:, LANES : 2 * LANES] = jnp.concatenate([pad, ctx], axis=1)
    rows[:, 2 * LANES :] = contract(hidden[...], w_junction[...], 1, 0).astype(BF16)


def diagonal(size):
    return iota((size, size), 0) == iota((size, size), 1)


def score_body(own, other, mine, expd, dprobs, stats):
    tokens = own.shape[0]
    half = mine.shape[0] * tokens
    keys = mine[:, :tokens, :].reshape(half, KV)
    square = diagonal(BAND)
    blank = jnp.zeros((8 - 3, BAND), F32)
    for i, rows in enumerate((own, other)):
        for start in range(0, tokens, BAND):
            band = pl.ds(start, BAND)
            score = contract(rows[band, :LANES], keys[:, :LANES], 1, 1) * HD ** (-0.5)
            row_max = jnp.max(score, axis=-1, keepdims=True)
            value = jnp.exp(score - row_max)
            dprob = contract(rows[band, LANES : 2 * LANES], keys[:, SHIFT:], 1, 1)
            expd[i, band, :] = value
            dprobs[i, band, :] = dprob
            columns = (
                row_max,
                jnp.sum(value, axis=-1, keepdims=True),
                jnp.sum(value * dprob, axis=-1, keepdims=True),
            )
            lines = [
                jnp.sum(jnp.where(square, column, 0.0), axis=0, keepdims=True)
                for column in columns
            ]
            stats[i, :, band] = jnp.concatenate(lines + [blank], axis=0)


def slot_body(own, other, mine, back, kept_sum, sent_sum):
    tokens = own.shape[0]
    chips, height, _ = mine.shape
    part = height - tokens
    slots = chips * part
    slot_rows = mine[:, tokens:, :].astype(F32).reshape(slots, KV)
    donor_feat = slot_rows[:, :PJ]
    extra = slot_rows[:, PJ : 2 * PJ]
    acceptor = extra[:, 0:1]
    slot_scale = extra[:, 1:2] + extra[:, 2:3] + extra[:, 3:4]
    shard = iota((slots, 1), 0) % part // (part // CORES)
    here = shard == lax.axis_index("core")
    place = iota((slots, tokens), 1).astype(F32) == acceptor
    hots = [
        jnp.where(place, jnp.where(chosen, 1.0, 0.0), 0.0).astype(BF16)
        for chosen in (here, jnp.logical_not(here))
    ]
    accept_feat = contract(hots[0], own[:, 2 * LANES :], 1, 0) + contract(
        hots[1], other[:, 2 * LANES :], 1, 0
    )
    pair_scale = PJ ** (-0.5)
    pair_score = jnp.sum(donor_feat * accept_feat, axis=-1, keepdims=True) * pair_scale
    slot_grad = slot_scale * jax.nn.sigmoid(pair_score) * pair_scale
    pieces = split_terms(slot_grad * donor_feat)
    for hot, total in zip(hots, (kept_sum, sent_sum)):
        total[...] = contract(hot, pieces[0], 0, 0) + contract(hot, pieces[1], 0, 0)
    back[...] = (slot_grad * accept_feat).astype(BF16).reshape(chips, part, PJ)


def grad_body(
    own,
    other,
    mine,
    expd,
    dprobs,
    stats,
    got,
    back,
    sent_sum,
    terms_out,
    sent_out,
    kept,
    terms,
    sent,
    probs_b,
    dscores_b,
    sems,
):
    tokens = own.shape[0]
    chips, height, _ = mine.shape
    part = height - tokens
    half = chips * tokens
    scale = HD ** (-0.5)
    square = diagonal(BAND)
    for i in range(CORES):
        for start in range(0, tokens, BAND):
            band = pl.ds(start, BAND)
            here, there = stats[i, :, band], got[1 - i, :, band]
            top = jnp.maximum(here[0:1], there[0:1])
            near, far = jnp.exp(here[0:1] - top), jnp.exp(there[0:1] - top)
            inverse = 1.0 / (here[1:2] * near + there[1:2] * far)
            delta = (here[2:3] * near + there[2:3] * far) * inverse
            factor, delta = (
                jnp.sum(jnp.where(square, line, 0.0), axis=1, keepdims=True)
                for line in (near * inverse, delta)
            )
            probs = expd[i, band, :] * factor
            rows = pl.ds(i * tokens + start, BAND)
            probs_b[rows, :] = probs.astype(BF16)
            dscores_b[rows, :] = (probs * (dprobs[i, band, :] - delta)).astype(BF16)
    rows = jnp.concatenate([own[:, : 2 * LANES], other[:, : 2 * LANES]], axis=0)
    key_term = contract(dscores_b[...], rows[:, :LANES], 0, 0) * scale
    value_term = contract(probs_b[...], rows[:, LANES:], 0, 0)
    middle = key_term[:, SHIFT:] + value_term[:, :SHIFT]
    for first, value in (
        (0, key_term[:, :SHIFT]),
        (SHIFT, middle),
        (LANES, value_term[:, SHIFT:]),
    ):
        terms[:, :tokens, first : first + SHIFT] = value.astype(BF16).reshape(
            chips, tokens, SHIFT
        )
    terms[:, tokens:, :PJ] = back[...]
    terms[:, tokens:, PJ:] = jnp.zeros((chips, part, KV - PJ), BF16)
    first = pltpu.make_async_copy(terms, terms_out, sems.at[0])
    first.start()
    keys = mine[:, :tokens, :LANES].reshape(half, LANES)
    query_term = contract(dscores_b[...], keys, 1, 0) * scale
    kept[...] = query_term[:tokens, :]
    sent[:, :LANES] = query_term[tokens:, :].astype(BF16)
    sent[:, LANES:] = sent_sum[...].astype(BF16)
    second = pltpu.make_async_copy(sent, sent_out, sems.at[1])
    second.start()
    first.wait()
    second.wait()


def halve(value, side):
    blocks = value.reshape((value.shape[0] // 2, 2) + value.shape[1:])
    odd = side == 1
    kept = jnp.where(odd, blocks[:, 1], blocks[:, 0])
    sent = jnp.where(odd, blocks[:, 0], blocks[:, 1])
    return kept, sent.astype(BF16)


def total_body(*refs):
    value = refs[0][...].astype(F32)
    for ref in refs[1:-1]:
        value = value + ref[...].astype(F32)
    refs[-1][...] = value.astype(refs[-1].dtype)


def grads_body(parts, query_held, query_got, hidden, grads, query_grad, kept, sent):
    tokens, width = hidden.shape
    query = query_held[:, :HD] + query_got[:, :HD].astype(F32)
    query_grad[...] = query.astype(BF16)
    total = jnp.zeros((tokens, KV), F32)
    for chip in range(parts.shape[0]):
        total = total + parts[chip, :tokens, :].astype(F32)
    grads[...] = total.astype(BF16)
    core = lax.axis_index("core")
    cut = width // CORES
    first = 0
    for grad in (query_grad[...], grads[...]):
        value = contract(grad, hidden[...], 0, 0)
        rows = pl.ds(first, value.shape[0])
        left, right = value[:, :cut], value[:, cut:]
        kept[rows, :] = jnp.where(core == 0, left, right).astype(BF16)
        sent[rows, :] = jnp.where(core == 0, right, left).astype(BF16)
        first += value.shape[0]


def input_body(
    w_query_hbm,
    w_key_hbm,
    w_value_hbm,
    w_junction_hbm,
    parts,
    kept_sum,
    query_got,
    donor_hot,
    grads,
    query_grad,
    kept,
    sent,
    weights,
    w_junction,
    sems,
):
    copies = [
        pltpu.make_async_copy(source, weights.at[pl.ds(i * HD, HD)], sems.at[i])
        for i, source in enumerate((w_query_hbm, w_key_hbm, w_value_hbm))
    ]
    copies.append(pltpu.make_async_copy(w_junction_hbm, w_junction, sems.at[3]))
    for copy in copies:
        copy.start()
    both = jnp.concatenate([query_grad[...], grads[...]], axis=1)
    chips, height, _ = parts.shape
    tokens = grads.shape[0]
    part = height - tokens
    slot_rows = parts[:, tokens:, :PJ].reshape(chips * part, PJ)
    feature_grad = kept_sum[...] + query_got[:, LANES:].astype(F32)
    feature_grad = (feature_grad + contract(donor_hot[...], slot_rows, 0, 0)).astype(BF16)
    for copy in copies:
        copy.wait()
    value = contract(weights[...], both, 0, 1) + contract(w_junction[...], feature_grad, 1, 1)
    blocks = value.reshape((2 * kept.shape[0],) + kept.shape[1:])
    kept[...], sent[...] = halve(blocks, lax.axis_index("side"))


def tiles_of(rows, columns, count):
    high, wide = rows * 2 // count, columns // 2
    return [(i, pl.ds(i // 2 * high, high), pl.ds(i % 2 * wide, wide)) for i in range(count)]


def pair_body(held, got, out, total, sems):
    chips, part, _ = total.shape
    copies = []
    for chip in range(chips):
        rows = pl.ds(chip * part, part)
        value = held[rows, :].astype(F32) + got[rows, :].astype(F32)
        total[chip] = value.astype(BF16)
        copy = pltpu.make_async_copy(total.at[chip], out.at[chip], sems.at[chip])
        copy.start()
        copies.append(copy)
    for copy in copies:
        copy.wait()


def sum_body(parts, total):
    value = parts[0].astype(F32)
    for i in range(1, parts.shape[0]):
        value = value + parts[i].astype(F32)
    total[...] = value.astype(total.dtype)


def cut_body(parts, tiles, whole):
    value = parts[0].astype(F32)
    for i in range(1, parts.shape[0]):
        value = value + parts[i].astype(F32)
    whole[...] = value
    for i, rows, columns in tiles_of(*whole.shape, tiles.shape[0]):
        tiles[i] = whole[rows, columns].astype(BF16)


def spread_body(parts, copies):
    value = parts[0].astype(F32)
    for i in range(1, parts.shape[0]):
        value = value + parts[i].astype(F32)
    value = value.astype(BF16)
    for i in range(copies.shape[0]):
        copies[i] = value


def join_body(tiles, joined, whole):
    for i, rows, columns in tiles_of(*whole.shape, tiles.shape[0]):
        whole[rows, columns] = tiles[i].astype(F32)
    joined[...] = whole[...].astype(BF16)


def place(source, outs, sems, core):
    cut = source.shape[1]
    columns = pl.ds(pl.multiple_of(core * cut, cut), cut)
    copies = [
        pltpu.make_async_copy(source.at[pl.ds(i * HD, HD)], out.at[:, columns], sems.at[i])
        for i, out in enumerate(outs)
    ]
    for copy in copies:
        copy.start()
    for copy in copies:
        copy.wait()


def own_half_body(mine, *refs):
    place(mine, refs[:3], refs[3], lax.axis_index("core"))


def other_half_body(theirs, *refs):
    place(theirs, refs[3:6], refs[6], 1 - lax.axis_index("core"))


def swap(value, axis="core"):
    return lax.ppermute(value, axis, [(0, 1), (1, 0)])


def in_hbm(*values):
    return [pltpu.with_memory_space_constraint(value, pltpu.HBM) for value in values]


def exchange(value, axis):
    return lax.all_to_all(value, axis, 0, 0, tiled=True)


def on_device(
    hidden_in,
    ctx_grad,
    w_query,
    w_key,
    w_value,
    w_junction,
    donor_pos,
    acceptor_pos,
    junction_counts,
    pred_grad,
):
    hidden = hidden_in[0]
    tokens, width = hidden.shape
    chips = lax.axis_size("x")
    intervals = lax.axis_size("interval")
    heads = lax.axis_size("pair") * SIDES
    half = chips * tokens
    buckets, per = donor_pos.shape[2:]
    slots = buckets * per
    height = tokens + slots // chips

    message, donor_hot = local_call(
        project_body,
        [((chips, height, KV), BF16, True), ((slots, tokens), BF16)],
        operands=8,
        fetched=8,
        scratch=[
            pltpu.VMEM((tokens, KV), BF16),
            pltpu.VMEM((slots, KV), BF16),
            pltpu.VMEM((tokens, width), BF16),
            pltpu.VMEM((KV, width), BF16),
            pltpu.VMEM((width, PJ), BF16),
            pltpu.VMEM((buckets, per), jnp.int32),
            pltpu.VMEM((buckets, per), jnp.int32),
            pltpu.VMEM((1, buckets), jnp.int32),
            pltpu.VMEM((buckets, per), F32),
            pltpu.SemaphoreType.DMA((8,)),
            pltpu.SemaphoreType.DMA((2 * chips,)),
        ],
    )(
        *in_hbm(
            hidden,
            w_key,
            w_value,
            w_junction,
            donor_pos[0, 0],
            acceptor_pos[0, 0],
            junction_counts[0],
            pred_grad[0, 0],
        )
    )
    mine = exchange(message, "x")
    (own,) = local_call(query_body, [((tokens, 2 * LANES + PJ), BF16)], operands=4)(
        hidden, w_query, w_junction, ctx_grad[0].T
    )
    other = swap(own)
    expd, dprobs, stats = local_call(
        score_body,
        [((CORES, tokens, half), F32), ((CORES, tokens, half), F32), ((CORES, 8, tokens), F32)],
        operands=3,
    )(own, other, mine)
    got = swap(stats)
    back, kept_sum, sent_sum = local_call(
        slot_body,
        [((chips, height - tokens, PJ), BF16), ((tokens, PJ), F32), ((tokens, PJ), F32)],
        operands=3,
    )(own, other, mine)
    terms, query_sent, query_held = local_call(
        grad_body,
        [
            ((chips, height, KV), BF16, True),
            ((tokens, LANES + PJ), BF16, True),
            ((tokens, LANES), F32),
        ],
        operands=9,
        scratch=[
            pltpu.VMEM((chips, height, KV), BF16),
            pltpu.VMEM((tokens, LANES + PJ), BF16),
        ]
        + [pltpu.VMEM((CORES * tokens, half), BF16)] * 2
        + [pltpu.SemaphoreType.DMA((2,))],
    )(own, other, mine, expd, dprobs, stats, got, back, sent_sum)
    query_got = swap(query_sent)
    parts = exchange(terms, "x")
    parts, query_got = lax.optimization_barrier((parts, query_got))
    rows = 3 * HD
    cut = width // CORES
    block = (width // heads, tokens)
    grads, query_grad, weight_held, weight_sent = local_call(
        grads_body,
        [((tokens, KV), BF16), ((tokens, HD), BF16), ((rows, cut), BF16), ((rows, cut), BF16)],
        operands=4,
    )(parts, query_held, query_got, hidden)
    held, sent = local_call(
        input_body,
        [((heads // 2,) + block, F32), ((heads // 2,) + block, BF16)],
        operands=10,
        fetched=4,
        scratch=[
            pltpu.VMEM((rows, width), BF16),
            pltpu.VMEM((width, PJ), BF16),
            pltpu.SemaphoreType.DMA((4,)),
        ],
    )(
        *in_hbm(w_query, w_key, w_value, w_junction),
        parts,
        kept_sum,
        query_got,
        donor_hot,
        grads,
        query_grad,
    )

    weight_got = swap(weight_sent)
    part = rows // chips
    (term,) = local_call(
        pair_body,
        [((chips, part, cut), BF16, True)],
        operands=2,
        scratch=[pltpu.VMEM((chips, part, cut), BF16), pltpu.SemaphoreType.DMA((chips,))],
    )(weight_held, weight_got)
    tile = (part * 2 // intervals, cut // 2)
    (tiles,) = local_call(
        cut_body, [((intervals,) + tile, BF16)], operands=1, scratch=[pltpu.VMEM((part, cut), F32)]
    )(exchange(term, "x"))
    got = swap(sent, "side")
    (copies,) = local_call(spread_body, [((intervals,) + tile, BF16)], operands=1)(
        exchange(tiles, "interval")
    )
    copies, got = lax.optimization_barrier((copies, got))
    (blocks,) = local_call(total_body, [((heads // SIDES,) + block, BF16)], operands=2)(held, got)
    (term,) = local_call(
        join_body, [((part, cut), BF16)], operands=1, scratch=[pltpu.VMEM((part, cut), F32)]
    )(exchange(copies, "interval"))
    blocks = exchange(blocks, "pair")
    term = lax.all_gather(term, "x", axis=0, tiled=True)
    term, blocks = lax.optimization_barrier((term, blocks))
    (grad_input,) = local_call(sum_body, [(block, BF16)], operands=1)(blocks)
    wide = [((HD, width), BF16)] * 3
    sems = [pltpu.SemaphoreType.DMA((3,))]
    theirs = swap(term)
    grads = local_call(own_half_body, wide, operands=1, scratch=sems, space=pl.ANY)(term)
    grads = local_call(
        other_half_body,
        wide,
        operands=4,
        scratch=sems,
        space=pl.ANY,
        aliases={i + 1: i for i in range(3)},
    )(theirs, *grads)
    return (grad_input.T[None],) + tuple(grads)


def solution(mesh):
    axes = (mesh.shape["interval"], mesh.shape["seq"] // CORES, CORES)
    axes += (mesh.shape["head"] // SIDES, SIDES)
    split = Mesh(mesh.devices.reshape(axes), ("interval", "x", "core", "pair", "side"))
    seq, head = ("x", "core"), ("pair", "side")
    placed = (
        P("interval", seq, None),
        P("interval", seq, head),
        P(head, None),
        P(head, None),
        P(head, None),
        P(),
        P("interval", seq, None, head),
        P("interval", seq, None, head),
        P("interval", seq, None),
        P("interval", seq, None, head),
    )
    return jax.shard_map(
        on_device,
        mesh=split,
        in_specs=placed,
        out_specs=(P("interval", seq, head), P(head, None), P(head, None), P(head, None)),
        check_vma=False,
    )
```
